32 devices in a mesh: grp: 2 (over y), gx: 4 (over z), gy: 4 (over x, core).
Axes of the slice: x: 2, y: 2, z: 4, core: 2. Of those that a mesh axis runs over, the one named last changes fastest.
Arguments:
- input_activation: bfloat16 [32, 32, 1024], P(('grp', 'gx'), 'gy'), parts along dimension 0, may hold values from -6 to 6
- pre_one: bfloat16 [32, 32, 1024], P(('grp', 'gx'), 'gy'), parts along dimension 0, may hold values from -6 to 6
- pre_two: bfloat16 [32, 32, 1024], P(('grp', 'gx'), 'gy'), parts along dimension 0, may hold values from -6 to 6
- w_one: bfloat16 [27, 64, 64], replicated, may hold values from -0.15625 to 0.15625
- w_two: bfloat16 [27, 64, 64], replicated, may hold values from -0.15625 to 0.15625
- w_trans: bfloat16 [512, 512], replicated, may hold values from -0.5 to 0.5
- keep_mask: int32 [8, 8], replicated, may hold values 0 or 1
- out_grad: bfloat16 [16, 16, 8, 512], P('grp', 'gy', None, 'gx'), parts along dimension 0, may hold values from -6 to 6
Outputs:
- grad_in: bfloat16 [32, 32, 1024], P(('grp', 'gx'), 'gy'), parts along dimension 0
- grad_w_one: float32 [54, 64, 64], P('grp'), parts along dimension 0
- grad_w_two: float32 [54, 64, 64], P('grp'), parts along dimension 0
- grad_w_trans: float32 [1024, 512], P('grp'), parts along dimension 0
The draws below stay inside these ranges and needn't reach their ends.
There are 2 independent parts, one for each index of `grp`. The reference program is written for one: setup_inputs(seed, part) draws one part's arguments, and reference() takes and returns one part's arrays. A program takes and returns all parts, laid end to end along the dimension named above; an argument that names none is the same for every part. Nothing has to cross between parts.
All inputs are finite; a program needn't handle non-finite values.
Results may differ from the reference program's by a relative error of at most 0.0058.
Values may be sent and summed in bfloat16 or wider, within the bound.
No kernel may reach another device: no remote copies, remote signals or barrier semaphores. Data moves between devices by JAX's collectives and lax.ppermute only.
A program may use at most 64 MiB of HBM per device.

```python
import math
import jax
import jax.numpy as jnp

CH = 64
DILATION_STEP = 2
NZ = 16
NX = 16
NY = 32
TCH = 512


def place_ends(entries, stream_key, least, high):
    longest = entries.shape.index(max(entries.shape))
    spots = []
    for shift in (0, 1):
        where = [jax.random.randint(jax.random.fold_in(stream_key, axis), (), 0, length) for axis, length in enumerate(entries.shape)]
        where[longest] = (where[longest] + shift) % entries.shape[longest]
        spots.append(tuple(where))
    return entries.at[spots[0]].set(least).at[spots[1]].set(high)


def levels(stream_key, extent, pieces, least, top_value):
    loudness = 1.0
    for position, blocks in pieces:
        draws = jax.random.uniform(jax.random.fold_in(jax.random.fold_in(stream_key, 6), position), (blocks,), jnp.float32, least / len(pieces), top_value / len(pieces))
        loudness = loudness * jnp.repeat(jnp.exp(draws), extent[position] // blocks).reshape((-1,) + (1,) * (len(extent) - 1 - position))
    return loudness


def gaussian(stream_key, dims, scale, bound, shards=(), held_as=jnp.bfloat16):
    values = scale * jax.random.normal(stream_key, dims, jnp.float32)
    if shards:
        values = values * levels(stream_key, dims, shards, -0.22, 0.18)
    return jnp.clip(values, -bound, bound).astype(held_as)


def setup_inputs(seed: int = 0, part: int = 0) -> dict:
    seeds = jax.random.split(jax.random.key(seed), 9)
    part_splits = jax.random.split(jax.random.fold_in(seeds[8], part), 9)
    input_activation = gaussian(part_splits[0], (NX, NY, NZ * CH), 1.0, 6.0, ((0, 4), (1, 4)))
    pre_one = gaussian(part_splits[1], (NX, NY, NZ * CH), 1.0, 6.0, ((0, 4), (1, 4)))
    pre_two = gaussian(part_splits[2], (NX, NY, NZ * CH), 1.0, 6.0, ((0, 4), (1, 4)))
    w_one = gaussian(seeds[3], (27, CH, CH), (27 * CH) ** -0.5, 0.15625)
    w_two = gaussian(seeds[4], (27, CH, CH), (27 * CH) ** -0.5, 0.15625)
    w_trans = gaussian(seeds[5], (TCH, TCH), (TCH // 4) ** -0.5, 0.5)
    keep_mask = place_ends((jax.random.randint(seeds[6], (8, 8), 0, 4) < 1).astype(jnp.int32), jax.random.fold_in(seeds[6], 1), 0, 1)
    out_grad = gaussian(part_splits[7], (NX // 2, NY // 2, NZ // 2, TCH), 1.0, 6.0, ((1, 4), (3, 4)))
    return {"input_activation": input_activation, "pre_one": pre_one, "pre_two": pre_two, "w_one": w_one, "w_two": w_two, "w_trans": w_trans, "keep_mask": keep_mask, "out_grad": out_grad}


def split_layout(joined_layout):
    return joined_layout.reshape(joined_layout.shape[0], joined_layout.shape[1], -1, CH)

def to_blocks(cube_volume):
    shape_all = cube_volume.shape
    parted = cube_volume.reshape(shape_all[0] // 2, 2, shape_all[1] // 2, 2, shape_all[2] // 2, 2, shape_all[3])
    parted = parted.transpose(0, 2, 4, 1, 3, 5, 6)
    return parted.reshape(shape_all[0] // 2, shape_all[1] // 2, shape_all[2] // 2, 8 * shape_all[3])

def from_blocks(blocked, channel_count):
    shape_all = blocked.shape
    parted = blocked.reshape(shape_all[0], shape_all[1], shape_all[2], 2, 2, 2, channel_count)
    parted = parted.transpose(0, 3, 1, 4, 2, 5, 6)
    return parted.reshape(2 * shape_all[0], 2 * shape_all[1], 2 * shape_all[2], channel_count)

def weight_grad(cube_volume, upstream_gradient):
    padded_input = jnp.pad(cube_volume.astype(jnp.float32), ((DILATION_STEP, DILATION_STEP), (DILATION_STEP, DILATION_STEP), (DILATION_STEP, DILATION_STEP), (0, 0)))
    grid_extent = upstream_gradient.shape
    flat_grad = upstream_gradient.astype(jnp.float32).reshape(-1, CH)
    partials = []
    for x_index in range(3):
        for y_index in range(3):
            for tap_index in range(3):
                sliding_window = padded_input[DILATION_STEP * x_index:DILATION_STEP * x_index + grid_extent[0], DILATION_STEP * y_index:DILATION_STEP * y_index + grid_extent[1], DILATION_STEP * tap_index:DILATION_STEP * tap_index + grid_extent[2]]
                partials.append(jnp.dot(sliding_window.reshape(-1, CH).T, flat_grad))
    return jnp.stack(partials)

def data_grad(upstream_gradient, weights):
    padded_input = jnp.pad(upstream_gradient.astype(jnp.float32), ((DILATION_STEP, DILATION_STEP), (DILATION_STEP, DILATION_STEP), (DILATION_STEP, DILATION_STEP), (0, 0)))
    weights_wide = weights.astype(jnp.float32)
    grid_extent = upstream_gradient.shape
    running = jnp.zeros((grid_extent[0] * grid_extent[1] * grid_extent[2], CH), jnp.float32)
    for x_index in range(3):
        for y_index in range(3):
            for tap_index in range(3):
                sliding_window = padded_input[DILATION_STEP * (2 - x_index):DILATION_STEP * (2 - x_index) + grid_extent[0], DILATION_STEP * (2 - y_index):DILATION_STEP * (2 - y_index) + grid_extent[1], DILATION_STEP * (2 - tap_index):DILATION_STEP * (2 - tap_index) + grid_extent[2]]
                running = running + jnp.dot(sliding_window.reshape(-1, CH), weights_wide[(x_index * 3 + y_index) * 3 + tap_index].T)
    return running.reshape(grid_extent)

def reference(input_activation, pre_one, pre_two, w_one, w_two, w_trans, keep_mask, out_grad):
    factor = 1.0 / math.sqrt(NX * NY * NZ)
    blocks = jnp.repeat(jnp.repeat(keep_mask.astype(jnp.float32), CH, axis=0), CH, axis=1)
    w_kept = w_trans.astype(jnp.float32) * blocks
    grad_rows = out_grad.astype(jnp.float32).reshape(-1, TCH)
    back_blocks = jnp.dot(grad_rows, w_kept.T).astype(jnp.bfloat16)
    act_two = split_layout(jnp.maximum(pre_two, 0))
    two_rows = to_blocks(act_two).reshape(-1, TCH).astype(jnp.float32)
    grad_w_trans = jnp.dot(two_rows.T, grad_rows) * blocks * factor
    back_two = from_blocks(back_blocks.reshape(NX // 2, NY // 2, NZ // 2, TCH), CH)
    back_two = jnp.where(split_layout(pre_two) > 0, back_two, jnp.zeros_like(back_two))
    first_activation = split_layout(jnp.maximum(pre_one, 0))
    grad_w_two = weight_grad(first_activation, back_two) * factor
    first_backward = data_grad(back_two, w_two)
    first_backward = jnp.where(split_layout(pre_one) > 0, first_backward, jnp.zeros_like(first_backward)).astype(jnp.bfloat16)
    grad_w_one = weight_grad(split_layout(input_activation), first_backward) * factor
    grad_in = data_grad(first_backward, w_one).astype(jnp.bfloat16).reshape(NX, NY, NZ * CH)
    return (grad_in, grad_w_one, grad_w_two, grad_w_trans)
```

```python
import functools
import math

import jax
import jax.numpy as jnp
from jax import lax
from jax.experimental import pallas as pl
from jax.experimental.pallas import tpu as pltpu
from jax.sharding import PartitionSpec as P

DILATION_STEP = 2
VMEM = pltpu.MemorySpace.VMEM
SMEM = pltpu.MemorySpace.SMEM
F32 = jnp.float32
BF16 = jnp.bfloat16


def padded(cells, sides, width):
    for axis, dim in sides:
        count = lax.axis_size(axis)
        ends = count - 1
        head = lax.slice_in_dim(cells, 0, width, axis=dim)
        tail = lax.slice_in_dim(cells, cells.shape[dim] - width, cells.shape[dim], axis=dim)
        cells = jnp.concatenate(
            [
                lax.ppermute(tail, axis, [(i, (i + 1) % count) for i in range(ends)]),
                cells,
                lax.ppermute(head, axis, [((i + 1) % count, i) for i in range(ends)]),
            ],
            axis=dim,
        )
    return cells


def split_layout(joined_layout, channel_count):
    return joined_layout.reshape(joined_layout.shape[0], joined_layout.shape[1], -1, channel_count)


def to_blocks(cube_volume):
    shape_all = cube_volume.shape
    parted = cube_volume.reshape(
        shape_all[0] // 2, 2, shape_all[1] // 2, 2, shape_all[2] // 2, 2, shape_all[3]
    )
    parted = parted.transpose(0, 2, 4, 1, 3, 5, 6)
    return parted.reshape(shape_all[0] // 2, shape_all[1] // 2, shape_all[2] // 2, 8 * shape_all[3])


def from_blocks(blocked, channel_count):
    shape_all = blocked.shape
    parted = blocked.reshape(shape_all[0], shape_all[1], shape_all[2], 2, 2, 2, channel_count)
    parted = parted.transpose(0, 3, 1, 4, 2, 5, 6)
    return parted.reshape(2 * shape_all[0], 2 * shape_all[1], 2 * shape_all[2], channel_count)


def padding_depth(cube_volume, margin):
    return jnp.pad(cube_volume, ((0, 0), (0, 0), (margin, margin), (0, 0)))


def weight_terms(bordered_input, upstream_gradient):
    channel_count = upstream_gradient.shape[3]
    grid_extent = upstream_gradient.shape
    padded_input = padding_depth(bordered_input, DILATION_STEP)
    flat_grad = upstream_gradient.reshape(-1, channel_count)
    partials = []
    for x_index in range(3):
        for y_index in range(3):
            sliding_window = padded_input[
                DILATION_STEP * x_index : DILATION_STEP * x_index + grid_extent[0],
                DILATION_STEP * y_index : DILATION_STEP * y_index + grid_extent[1],
            ]
            columns = jnp.concatenate(
                [
                    sliding_window[
                        :, :, DILATION_STEP * tap_index : DILATION_STEP * tap_index + grid_extent[2]
                    ].reshape(-1, channel_count)
                    for tap_index in range(3)
                ],
                axis=1,
            )
            partials.append(
                lax.dot_general(
                    columns, flat_grad, (((0,), (0,)), ((), ())), preferred_element_type=jnp.float32
                )
            )
    return jnp.stack(partials).reshape(27, channel_count, channel_count)


def data_terms(bordered_input, weights):
    channel_count = weights.shape[1]
    x_stretch = bordered_input.shape[0] - 2 * DILATION_STEP
    y_stretch = bordered_input.shape[1] - 2 * DILATION_STEP
    depth_cells = bordered_input.shape[2]
    padded_input = padding_depth(bordered_input, DILATION_STEP)
    stacked = jnp.transpose(weights, (0, 2, 1)).reshape(9, 3 * channel_count, channel_count)
    running = jnp.zeros((x_stretch * y_stretch * depth_cells, channel_count), jnp.float32)
    for x_index in range(3):
        for y_index in range(3):
            sliding_window = padded_input[
                DILATION_STEP * (2 - x_index) : DILATION_STEP * (2 - x_index) + x_stretch,
                DILATION_STEP * (2 - y_index) : DILATION_STEP * (2 - y_index) + y_stretch,
            ]
            columns = jnp.concatenate(
                [
                    sliding_window[
                        :,
                        :,
                        DILATION_STEP * (2 - tap_index) : DILATION_STEP * (2 - tap_index)
                        + depth_cells,
                    ].reshape(-1, channel_count)
                    for tap_index in range(3)
                ],
                axis=1,
            )
            running = running + jnp.dot(
                columns, stacked[x_index * 3 + y_index], preferred_element_type=jnp.float32
            )
    return running.reshape(x_stretch, y_stretch, depth_cells, channel_count)


def body(input_activation, pre_one, pre_two, w_one, w_two, w_trans, keep_mask, out_grad):
    channel_count = w_one.shape[1]
    x_stretch, y_stretch, joined_layout = input_activation.shape
    depth_cells = joined_layout // channel_count
    width_t = w_trans.shape[0]
    factor = 1.0 / math.sqrt(
        x_stretch * lax.axis_size("gx") * y_stretch * lax.axis_size("gy") * depth_cells
    )
    blocks = jnp.repeat(
        jnp.repeat(keep_mask.astype(jnp.bfloat16), channel_count, axis=0), channel_count, axis=1
    )
    w_kept = w_trans * blocks
    regrouped = lax.all_to_all(out_grad, "gx", split_axis=0, concat_axis=3, tiled=True)
    grad_rows = regrouped.reshape(-1, width_t)
    back_blocks = lax.dot_general(
        grad_rows, w_kept, (((1,), (1,)), ((), ())), preferred_element_type=jnp.float32
    ).astype(jnp.bfloat16)
    act_two = split_layout(jnp.maximum(pre_two, 0), channel_count)
    two_rows = to_blocks(act_two).reshape(-1, width_t)
    trans_term = (
        lax.dot_general(
            two_rows, grad_rows, (((0,), (0,)), ((), ())), preferred_element_type=jnp.float32
        )
        * blocks.astype(jnp.float32)
        * factor
    )
    grad_w_trans = lax.psum(trans_term, ("gx", "gy"))
    back_two = from_blocks(
        back_blocks.reshape(x_stretch // 2, y_stretch // 2, depth_cells // 2, width_t),
        channel_count,
    )
    back_two = jnp.where(
        split_layout(pre_two, channel_count) > 0, back_two, jnp.zeros_like(back_two)
    )
    first_activation = jnp.maximum(pre_one, 0)
    bordered_input = padded(
        jnp.concatenate([input_activation, first_activation], axis=2),
        (("gx", 0), ("gy", 1)),
        DILATION_STEP,
    )
    in_rim = split_layout(bordered_input[:, :, :joined_layout], channel_count)
    one_rim = split_layout(bordered_input[:, :, joined_layout:], channel_count)
    two_term = weight_terms(one_rim, back_two) * factor
    flattened_backward = back_two.reshape(x_stretch, y_stretch, joined_layout)
    narrowed_slice = split_layout(
        padded(flattened_backward, (("gx", 0), ("gy", 1)), DILATION_STEP), channel_count
    )
    first_backward = data_terms(narrowed_slice, w_two)
    first_backward = jnp.where(
        split_layout(pre_one, channel_count) > 0, first_backward, jnp.zeros_like(first_backward)
    ).astype(jnp.bfloat16)
    one_grad_rim = split_layout(
        padded(
            first_backward.reshape(x_stretch, y_stretch, joined_layout),
            (("gx", 0), ("gy", 1)),
            DILATION_STEP,
        ),
        channel_count,
    )
    grad_w_two = lax.psum(two_term, ("gx", "gy"))
    one_term = weight_terms(in_rim, first_backward) * factor
    grad_w_one = lax.psum(one_term, ("gx", "gy"))
    grad_in = (
        data_terms(one_grad_rim, w_one)
        .astype(jnp.bfloat16)
        .reshape(x_stretch, y_stretch, joined_layout)
    )
    return (grad_in, grad_w_one, grad_w_two, grad_w_trans)


def call(kernel, out_shape, scratch, flops, *args):
    spec = [
        pl.BlockSpec(memory_space=SMEM if a.dtype == jnp.int32 and a.ndim == 1 else VMEM)
        for a in args
    ]
    outs = jax.tree.map(lambda _: pl.BlockSpec(memory_space=VMEM), out_shape)
    return pl.pallas_call(
        kernel,
        out_shape=out_shape,
        in_specs=spec,
        out_specs=outs,
        scratch_shapes=scratch,
        cost_estimate=pl.CostEstimate(
            flops=flops, transcendentals=0, bytes_accessed=sum(a.size * a.dtype.itemsize for a in args)
        ),
        compiler_params=pltpu.CompilerParams(vmem_limit_bytes=48 * 1024 * 1024),
    )(*args)


def transition_kernel(
    factor, at_ref, a0, a1, a2, a3, w_ref, keep_ref, back_ref, one_ref, low_ref, high_ref, trans_ref, og_ref, two_ref
):
    me = at_ref[0]
    parts = (a0, a1, a2, a3)
    n = len(parts)
    rows = a0.shape[0] // 3
    for s, part in enumerate(parts):
        src = lax.rem(me + n - s, n)
        og_ref[src] = part[0:rows]
        spot = pl.ds(src * 4, 4)
        two_ref[spot] = part[rows : 2 * rows].reshape(4, rows // 4, 128)
        one_ref[spot] = part[2 * rows : 3 * rows].reshape(4, rows // 4, 128)
    og = jnp.concatenate([og_ref[j] for j in range(n)], axis=1)
    width = w_ref.shape[0]
    blocks = keep_ref.shape[0]
    side = width // blocks
    left = (
        lax.broadcasted_iota(jnp.int32, (width, blocks), 0) // side
        == lax.broadcasted_iota(jnp.int32, (width, blocks), 1)
    ).astype(BF16)
    right = (
        lax.broadcasted_iota(jnp.int32, (blocks, width), 1) // side
        == lax.broadcasted_iota(jnp.int32, (blocks, width), 0)
    ).astype(BF16)
    keep = keep_ref[...].astype(F32).astype(BF16)
    wide = jnp.dot(keep, right, preferred_element_type=F32).astype(BF16)
    mask = jnp.dot(left, wide, preferred_element_type=F32)
    kept = (w_ref[...].astype(F32) * mask).astype(BF16)
    back = lax.dot_general(og, kept, (((1,), (1,)), ((), ())), preferred_element_type=F32)
    two = two_ref[...].astype(F32).reshape(8, 2, 4, 2, 8, 128)
    cells = []
    for p in range(2):
        halves = []
        for q in range(2):
            pre = two[:, p, :, q]
            at = (p * 2 + q) * 128
            grad = back[:, at : at + 128].reshape(8, 4, 8, 128)
            halves.append(jnp.where(pre > 0, grad, 0.0))
            cells.append(jnp.maximum(pre, 0.0).reshape(256, 128).astype(BF16))
        back_ref[:, p] = jnp.stack(halves, axis=2).reshape(8, 64, 128).astype(BF16)
    flat = jnp.concatenate(cells, axis=1)
    trans = lax.dot_general(flat, og, (((0,), (0,)), ((), ())), preferred_element_type=F32)
    trans_ref[...] = trans * mask * factor
    low_ref[:, :, 0:32] = back_ref[:, :, 0:32]
    high_ref[:, :, 0:32] = back_ref[:, :, 32:64]
    low_ref[:, :, 32:48] = one_ref[:, 0:16].reshape(8, 2, 16, 128)
    high_ref[:, :, 32:48] = one_ref[:, 48:64].reshape(8, 2, 16, 128)


def triple(v):
    x, rows, _ = v.shape
    flat = v.reshape(x * rows, 128)
    t = lax.broadcasted_iota(jnp.int32, flat.shape, 0) % 8
    later = jnp.where(t == 7, 0.0, pltpu.roll(flat, x * rows - 1, 0))
    earlier = jnp.where(t == 0, 0.0, pltpu.roll(flat, 1, 0))
    wide = jnp.concatenate([later, flat, earlier], axis=1)
    return wide.astype(BF16).reshape(x, rows, 384)


def fold(sums, factor, out_ref, at):
    lane = lax.broadcasted_iota(jnp.int32, (64, 128), 1)
    taps = []
    for g in sums:
        for l in range(3):
            part = g[:, l * 128 : (l + 1) * 128]
            f = jnp.where(lane < 64, part[0:64], part[64:128])
            taps.append((f + pltpu.roll(f, 64, 1)) * factor)
    taps.append(taps[-1])
    for m in range(14):
        row = at + (m % 7) * 64
        out_ref[m // 7, row : row + 64] = jnp.where(lane < 64, taps[2 * m], taps[2 * m + 1])


def conv_kernel(
    factor, at_ref, back_ref, one_ref, left_ref, right_ref, w2_ref, w1_ref, i0, i1, i2, i3, trans_ref,
    grad_ref, sums_ref, wide_ref, outer_ref, in_ref, acc_ref,
):
    me = at_ref[0]
    parts = (i0, i1, i2, i3)
    n = len(parts)
    for s, part in enumerate(parts):
        in_ref[pl.ds(lax.rem(me + n - s, n) * 4, 4)] = part[...].reshape(4, 64, 128)
    edge = jnp.zeros((2, 128, 384), BF16)
    wide_ref[0:2] = edge
    wide_ref[18:20] = edge
    outer_ref[0:2] = edge[:, :96]
    outer_ref[18:20] = edge[:, :96]
    wide_ref[2:18, 0:32] = triple(left_ref[:, 0:32].astype(F32))
    wide_ref[2:18, 32:96] = triple(back_ref[...].astype(F32))
    wide_ref[2:18, 96:128] = triple(right_ref[:, 0:32].astype(F32))
    for i in range(3):
        for j in range(3):
            rows = wide_ref[4 - 2 * i : 20 - 2 * i, 32 - 16 * j : 128 - 16 * j].reshape(1536, 384)
            part = jnp.dot(rows, w2_ref[i * 3 + j], preferred_element_type=F32)
            if i == 0 and j == 0:
                acc_ref[...] = part
            else:
                acc_ref[...] += part
    pre = jnp.concatenate([left_ref[:, 32:48], one_ref[...], right_ref[:, 32:48]], axis=1).astype(F32)
    first = jnp.where(pre > 0, acc_ref[...].reshape(16, 96, 128), 0.0)
    outer_ref[2:18] = triple(first)
    act = jnp.maximum(one_ref[...].astype(F32), 0.0).reshape(1024, 128).T.astype(BF16)
    sums = []
    for i in range(3):
        for j in range(3):
            rows = wide_ref[4 - 2 * i : 20 - 2 * i, 48 - 16 * j : 112 - 16 * j].reshape(1024, 384)
            sums.append(jnp.dot(act, rows, preferred_element_type=F32))
    fold(sums, factor, sums_ref, 448)
    act = in_ref[...].astype(F32).reshape(1024, 128).T.astype(BF16)
    sums = []
    grad = jnp.zeros((256, 128), F32)
    for i in range(3):
        for j in range(3):
            rows = outer_ref[4 - 2 * i : 20 - 2 * i, 32 - 16 * j : 96 - 16 * j].reshape(1024, 384)
            sums.append(jnp.dot(act, rows, preferred_element_type=F32))
            mine = outer_ref[pl.ds(me * 4 + 4 - 2 * i, 4), 32 - 16 * j : 96 - 16 * j].reshape(256, 384)
            grad += jnp.dot(mine, w1_ref[i * 3 + j], preferred_element_type=F32)
    fold(sums, factor, sums_ref, 0)
    grad_ref[...] = grad.reshape(4, 64, 128).astype(BF16)
    for h in range(2):
        for m in range(4):
            sums_ref[h, 896 + 256 * m : 1152 + 256 * m] = trans_ref[
                256 * h : 256 * h + 256, 128 * m : 128 * m + 128
            ]


def spread_kernel(at_ref, mine_ref, other_ref, one_ref, two_ref, trans_ref):
    def emit(low_ref, high_ref):
        for h, ref in enumerate((low_ref, high_ref)):
            for out, at in ((one_ref, 0), (two_ref, 448)):
                for m in range(7):
                    block = ref[at + 64 * m : at + 64 * m + 64]
                    tap = 2 * (7 * h + m)
                    out[tap] = block[:, 0:64]
                    if tap < 26:
                        out[tap + 1] = block[:, 64:128]
            for m in range(4):
                trans_ref[256 * h : 256 * h + 256, 128 * m : 128 * m + 128] = ref[
                    896 + 256 * m : 1152 + 256 * m
                ]

    @pl.when(at_ref[0] == 0)
    def _():
        emit(mine_ref, other_ref)

    @pl.when(at_ref[0] != 0)
    def _():
        emit(other_ref, mine_ref)


def twin(weights):
    turned = jnp.transpose(weights, (0, 2, 1))
    none = jnp.zeros_like(turned)
    both = jnp.concatenate(
        [jnp.concatenate([turned, none], axis=2), jnp.concatenate([none, turned], axis=2)], axis=1
    )
    return both.reshape(9, 384, 128)


def rotate(value, axis, step):
    n = lax.axis_size(axis)
    return lax.ppermute(value, axis, [(i, (i + step) % n) for i in range(n)])


def swap(value, axis, bit):
    n = lax.axis_size(axis)
    return lax.ppermute(value, axis, [(i, i ^ bit) for i in range(n)])


def slab_body(input_activation, pre_one, pre_two, w_one, w_two, w_trans, keep_mask, out_grad):
    factor = 1.0 / math.sqrt(
        input_activation.shape[0] * 4 * input_activation.shape[1] * 4 * (input_activation.shape[2] // 64)
    )
    gx = lax.axis_index("gx").astype(jnp.int32)
    gy = lax.axis_index("gy").astype(jnp.int32)
    core = lax.rem(gy, 2)
    first = jnp.concatenate(
        [out_grad.reshape(256, 128), pre_two.reshape(256, 128), pre_one.reshape(256, 128)], axis=0
    )
    firsts = [first] + [rotate(first, "gx", s) for s in (1, 2, 3)]
    second = input_activation.reshape(256, 128)
    seconds = [second] + [rotate(second, "gx", s) for s in (1, 2, 3)]
    shape = jax.ShapeDtypeStruct
    back, one, low, high, trans = call(
        functools.partial(transition_kernel, factor),
        (
            shape((8, 2, 64, 128), BF16),
            shape((16, 64, 128), BF16),
            shape((8, 2, 48, 128), BF16),
            shape((8, 2, 48, 128), BF16),
            shape((512, 512), F32),
        ),
        [pltpu.VMEM((4, 256, 128), BF16), pltpu.VMEM((16, 64, 128), BF16)],
        4 * 256 * 512 * 512,
        gx.reshape(1),
        *firsts,
        w_trans,
        keep_mask,
    )
    n = lax.axis_size("gy")
    from_left = lax.ppermute(high, "gy", [(i, i + 1) for i in range(n - 1)])
    from_right = lax.ppermute(low, "gy", [(i + 1, i) for i in range(n - 1)])
    grad_in, sums = call(
        functools.partial(conv_kernel, factor),
        (shape((4, 64, 128), BF16), shape((2, 1920, 128), F32)),
        [
            pltpu.VMEM((20, 128, 384), BF16),
            pltpu.VMEM((20, 96, 384), BF16),
            pltpu.VMEM((16, 64, 128), BF16),
            pltpu.VMEM((1536, 128), F32),
        ],
        2 * 128 * 3456 * (1536 + 1024 + 1024 + 256),
        gx.reshape(1),
        back.reshape(16, 64, 128),
        one,
        from_left.reshape(16, 48, 128),
        from_right.reshape(16, 48, 128),
        twin(w_two),
        twin(w_one),
        *seconds,
        trans,
    )
    mine = lax.dynamic_index_in_dim(sums, core, 0, keepdims=False)
    other = lax.dynamic_index_in_dim(sums, 1 - core, 0, keepdims=False)
    mine = (mine + swap(other, "gy", 1)).astype(BF16)
    mine = mine.astype(F32) + swap(mine, "gy", 2).astype(F32)
    other = swap(mine, "gy", 1)
    grad_w_one, grad_w_two, grad_w_trans = call(
        spread_kernel,
        (shape((27, 64, 64), F32), shape((27, 64, 64), F32), shape((512, 512), F32)),
        [],
        0,
        core.reshape(1),
        mine,
        other,
    )
    return (grad_in.reshape(input_activation.shape), grad_w_one, grad_w_two, grad_w_trans)


def solution(mesh):
    fits = mesh.shape["gx"] == 4 and mesh.shape["gy"] == 4

    def pick(*args):
        shapes = tuple(a.shape for a in args)
        known = (
            ((4, 8, 1024),) * 3 + ((27, 64, 64),) * 2 + ((512, 512), (8, 8), (8, 4, 8, 128))
        )
        return (slab_body if fits and shapes == known else body)(*args)

    return jax.shard_map(
        pick,
        mesh=mesh,
        in_specs=(
            P(("grp", "gx"), "gy", None),
            P(("grp", "gx"), "gy", None),
            P(("grp", "gx"), "gy", None),
            P(),
            P(),
            P(),
            P(),
            P("grp", "gy", None, "gx"),
        ),
        out_specs=(
            P(("grp", "gx"), "gy", None),
            P("grp", None, None),
            P("grp", None, None),
            P("grp", None),
        ),
        check_vma=False,
    )
```

```python
import functools
import math

import jax
import jax.numpy as jnp
from jax import lax
from jax.experimental import pallas as pl
from jax.experimental.pallas import tpu as pltpu
from jax.sharding import PartitionSpec as P

DILATION_STEP = 2
VMEM = pltpu.MemorySpace.VMEM
SMEM = pltpu.MemorySpace.SMEM
F32 = jnp.float32
BF16 = jnp.bfloat16


def padded(cells, sides, width):
    for axis, dim in sides:
        count = lax.axis_size(axis)
        ends = count - 1
        head = lax.slice_in_dim(cells, 0, width, axis=dim)
        tail = lax.slice_in_dim(cells, cells.shape[dim] - width, cells.shape[dim], axis=dim)
        cells = jnp.concatenate(
            [
                lax.ppermute(tail, axis, [(i, (i + 1) % count) for i in range(ends)]),
                cells,
                lax.ppermute(head, axis, [((i + 1) % count, i) for i in range(ends)]),
            ],
            axis=dim,
        )
    return cells


def split_layout(joined_layout, channel_count):
    return joined_layout.reshape(joined_layout.shape[0], joined_layout.shape[1], -1, channel_count)


def to_blocks(cube_volume):
    shape_all = cube_volume.shape
    parted = cube_volume.reshape(
        shape_all[0] // 2, 2, shape_all[1] // 2, 2, shape_all[2] // 2, 2, shape_all[3]
    )
    parted = parted.transpose(0, 2, 4, 1, 3, 5, 6)
    return parted.reshape(shape_all[0] // 2, shape_all[1] // 2, shape_all[2] // 2, 8 * shape_all[3])


def from_blocks(blocked, channel_count):
    shape_all = blocked.shape
    parted = blocked.reshape(shape_all[0], shape_all[1], shape_all[2], 2, 2, 2, channel_count)
    parted = parted.transpose(0, 3, 1, 4, 2, 5, 6)
    return parted.reshape(2 * shape_all[0], 2 * shape_all[1], 2 * shape_all[2], channel_count)


def padding_depth(cube_volume, margin):
    return jnp.pad(cube_volume, ((0, 0), (0, 0), (margin, margin), (0, 0)))


def weight_terms(bordered_input, upstream_gradient):
    channel_count = upstream_gradient.shape[3]
    grid_extent = upstream_gradient.shape
    padded_input = padding_depth(bordered_input, DILATION_STEP)
    flat_grad = upstream_gradient.reshape(-1, channel_count)
    partials = []
    for x_index in range(3):
        for y_index in range(3):
            sliding_window = padded_input[
                DILATION_STEP * x_index : DILATION_STEP * x_index + grid_extent[0],
                DILATION_STEP * y_index : DILATION_STEP * y_index + grid_extent[1],
            ]
            columns = jnp.concatenate(
                [
                    sliding_window[
                        :, :, DILATION_STEP * tap_index : DILATION_STEP * tap_index + grid_extent[2]
                    ].reshape(-1, channel_count)
                    for tap_index in range(3)
                ],
                axis=1,
            )
            partials.append(
                lax.dot_general(
                    columns, flat_grad, (((0,), (0,)), ((), ())), preferred_element_type=jnp.float32
                )
            )
    return jnp.stack(partials).reshape(27, channel_count, channel_count)


def data_terms(bordered_input, weights):
    channel_count = weights.shape[1]
    x_stretch = bordered_input.shape[0] - 2 * DILATION_STEP
    y_stretch = bordered_input.shape[1] - 2 * DILATION_STEP
    depth_cells = bordered_input.shape[2]
    padded_input = padding_depth(bordered_input, DILATION_STEP)
    stacked = jnp.transpose(weights, (0, 2, 1)).reshape(9, 3 * channel_count, channel_count)
    running = jnp.zeros((x_stretch * y_stretch * depth_cells, channel_count), jnp.float32)
    for x_index in range(3):
        for y_index in range(3):
            sliding_window = padded_input[
                DILATION_STEP * (2 - x_index) : DILATION_STEP * (2 - x_index) + x_stretch,
                DILATION_STEP * (2 - y_index) : DILATION_STEP * (2 - y_index) + y_stretch,
            ]
            columns = jnp.concatenate(
                [
                    sliding_window[
                        :,
                        :,
                        DILATION_STEP * (2 - tap_index) : DILATION_STEP * (2 - tap_index)
                        + depth_cells,
                    ].reshape(-1, channel_count)
                    for tap_index in range(3)
                ],
                axis=1,
            )
            running = running + jnp.dot(
                columns, stacked[x_index * 3 + y_index], preferred_element_type=jnp.float32
            )
    return running.reshape(x_stretch, y_stretch, depth_cells, channel_count)


def body(input_activation, pre_one, pre_two, w_one, w_two, w_trans, keep_mask, out_grad):
    channel_count = w_one.shape[1]
    x_stretch, y_stretch, joined_layout = input_activation.shape
    depth_cells = joined_layout // channel_count
    width_t = w_trans.shape[0]
    factor = 1.0 / math.sqrt(
        x_stretch * lax.axis_size("gx") * y_stretch * lax.axis_size("gy") * depth_cells
    )
    blocks = jnp.repeat(
        jnp.repeat(keep_mask.astype(jnp.bfloat16), channel_count, axis=0), channel_count, axis=1
    )
    w_kept = w_trans * blocks
    regrouped = lax.all_to_all(out_grad, "gx", split_axis=0, concat_axis=3, tiled=True)
    grad_rows = regrouped.reshape(-1, width_t)
    back_blocks = lax.dot_general(
        grad_rows, w_kept, (((1,), (1,)), ((), ())), preferred_element_type=jnp.float32
    ).astype(jnp.bfloat16)
    act_two = split_layout(jnp.maximum(pre_two, 0), channel_count)
    two_rows = to_blocks(act_two).reshape(-1, width_t)
    trans_term = (
        lax.dot_general(
            two_rows, grad_rows, (((0,), (0,)), ((), ())), preferred_element_type=jnp.float32
        )
        * blocks.astype(jnp.float32)
        * factor
    )
    grad_w_trans = lax.psum(trans_term, ("gx", "gy"))
    back_two = from_blocks(
        back_blocks.reshape(x_stretch // 2, y_stretch // 2, depth_cells // 2, width_t),
        channel_count,
    )
    back_two = jnp.where(
        split_layout(pre_two, channel_count) > 0, back_two, jnp.zeros_like(back_two)
    )
    first_activation = jnp.maximum(pre_one, 0)
    bordered_input = padded(
        jnp.concatenate([input_activation, first_activation], axis=2),
        (("gx", 0), ("gy", 1)),
        DILATION_STEP,
    )
    in_rim = split_layout(bordered_input[:, :, :joined_layout], channel_count)
    one_rim = split_layout(bordered_input[:, :, joined_layout:], channel_count)
    two_term = weight_terms(one_rim, back_two) * factor
    flattened_backward = back_two.reshape(x_stretch, y_stretch, joined_layout)
    narrowed_slice = split_layout(
        padded(flattened_backward, (("gx", 0), ("gy", 1)), DILATION_STEP), channel_count
    )
    first_backward = data_terms(narrowed_slice, w_two)
    first_backward = jnp.where(
        split_layout(pre_one, channel_count) > 0, first_backward, jnp.zeros_like(first_backward)
    ).astype(jnp.bfloat16)
    one_grad_rim = split_layout(
        padded(
            first_backward.reshape(x_stretch, y_stretch, joined_layout),
            (("gx", 0), ("gy", 1)),
            DILATION_STEP,
        ),
        channel_count,
    )
    grad_w_two = lax.psum(two_term, ("gx", "gy"))
    one_term = weight_terms(in_rim, first_backward) * factor
    grad_w_one = lax.psum(one_term, ("gx", "gy"))
    grad_in = (
        data_terms(one_grad_rim, w_one)
        .astype(jnp.bfloat16)
        .reshape(x_stretch, y_stretch, joined_layout)
    )
    return (grad_in, grad_w_one, grad_w_two, grad_w_trans)


def call(kernel, out_shape, scratch, flops, limit, *args):
    spec = []
    for a in args:
        if isinstance(a, tuple):
            spec.append(pl.BlockSpec(memory_space=pltpu.MemorySpace.HBM))
        elif a.dtype == jnp.int32:
            spec.append(pl.BlockSpec(memory_space=SMEM))
        else:
            spec.append(pl.BlockSpec(memory_space=VMEM))
    arrays = [a[0] if isinstance(a, tuple) else a for a in args]
    return pl.pallas_call(
        kernel,
        out_shape=out_shape,
        in_specs=spec,
        out_specs=jax.tree.map(lambda _: pl.BlockSpec(memory_space=VMEM), out_shape),
        scratch_shapes=scratch,
        cost_estimate=pl.CostEstimate(
            flops=flops,
            transcendentals=0,
            bytes_accessed=sum(a.size * a.dtype.itemsize for a in arrays),
        ),
        compiler_params=pltpu.CompilerParams(vmem_limit_bytes=limit * 1024 * 1024),
    )(*arrays)


def fetch(pairs, sems):
    copies = [pltpu.make_async_copy(src, dst, sems.at[k]) for k, (src, dst) in enumerate(pairs)]
    for copy in copies:
        copy.start()
    return copies


def pack_kernel(og, two, one, act, first_ref, second_ref, og_v, two_v, one_v, act_v, turn_ref, sems):
    copies = fetch(((og, og_v), (two, two_v), (one, one_v), (act, act_v)), sems)
    copies[0].wait()
    first_ref[0:256] = og_v[...].astype(F32).reshape(256, 128).astype(BF16)
    for k, (ref, out, at) in enumerate(((two_v, first_ref, 256), (one_v, first_ref, 512), (act_v, second_ref, 0))):
        copies[k + 1].wait()
        for x in range(4):
            for t in range(8):
                turn_ref[k, pl.ds(64 * x + t, 8, stride=8), :] = ref[x, :, 128 * t : 128 * t + 128].astype(F32)
        out[at : at + 256] = turn_ref[k].astype(BF16)


def weight_kernel(wt, keep, w2, w1, kept_ref, mask_ref, d2_ref, d1_ref, wt_v, keep_v, w2_v, w1_v, sems):
    copies = fetch(((keep, keep_v), (wt, wt_v), (w2, w2_v), (w1, w1_v)), sems)
    copies[0].wait()
    width = wt_v.shape[0]
    blocks = keep_v.shape[0]
    side = width // blocks
    left = (
        lax.broadcasted_iota(jnp.int32, (width, blocks), 0) // side
        == lax.broadcasted_iota(jnp.int32, (width, blocks), 1)
    ).astype(BF16)
    right = (
        lax.broadcasted_iota(jnp.int32, (blocks, width), 1) // side
        == lax.broadcasted_iota(jnp.int32, (blocks, width), 0)
    ).astype(BF16)
    wide = jnp.dot(keep_v[...].astype(F32).astype(BF16), right, preferred_element_type=F32).astype(BF16)
    mask = jnp.dot(left, wide, preferred_element_type=F32)
    mask_ref[...] = mask.astype(BF16)
    copies[1].wait()
    kept_ref[...] = (wt_v[...].astype(F32) * mask).astype(BF16)
    none = jnp.zeros((64, 64), BF16)
    for k, (ref, out) in enumerate(((w2_v, d2_ref), (w1_v, d1_ref))):
        copies[k + 2].wait()
        for tap in range(27):
            w = ref[tap]
            at = 128 * (tap % 3)
            out[tap // 3, 0:64, at : at + 128] = jnp.concatenate([w, none], axis=1)
            out[tap // 3, 64:128, at : at + 128] = jnp.concatenate([none, w], axis=1)


def transition_kernel(
    factor, at_ref, a0, a1, a2, a3, kept_ref, mask_ref, back_ref, one_ref, low_ref, high_ref, mine_ref, send_ref, og_ref, two_ref
):
    me = at_ref[0]
    parts = (a0, a1, a2, a3)
    n = len(parts)
    for s, part in enumerate(parts):
        src = lax.rem(me + n - s, n)
        og_ref[src] = part[0:256]
        spot = pl.ds(src * 4, 4)
        two_ref[spot] = part[256:512].reshape(4, 64, 128)
        one_ref[spot] = part[512:768].reshape(4, 64, 128)
    og = jnp.concatenate([og_ref[j] for j in range(n)], axis=1)
    back = lax.dot_general(og, kept_ref[...], (((1,), (1,)), ((), ())), preferred_element_type=F32)
    two = two_ref[...].astype(F32).reshape(8, 2, 4, 2, 8, 128)
    cells = []
    for p in range(2):
        halves = []
        for q in range(2):
            pre = two[:, p, :, q]
            at = (p * 2 + q) * 128
            grad = back[:, at : at + 128].reshape(8, 4, 8, 128)
            halves.append(jnp.where(pre > 0, grad, 0.0))
            cells.append(jnp.maximum(pre, 0.0).reshape(256, 128).astype(BF16))
        back_ref[:, p] = jnp.stack(halves, axis=2).reshape(8, 64, 128).astype(BF16)
    low_ref[:, :, 0:32] = back_ref[:, :, 0:32]
    high_ref[:, :, 0:32] = back_ref[:, :, 32:64]
    low_ref[:, :, 32:48] = one_ref[:, 0:16].reshape(8, 2, 16, 128)
    high_ref[:, :, 32:48] = one_ref[:, 48:64].reshape(8, 2, 16, 128)
    flat = jnp.concatenate(cells, axis=1)
    trans = lax.dot_general(flat, og, (((0,), (0,)), ((), ())), preferred_element_type=F32)
    trans = trans * mask_ref[...].astype(F32) * factor

    def emit(half, ref):
        for m in range(4):
            ref[256 * m : 256 * m + 256] = trans[256 * half : 256 * half + 256, 128 * m : 128 * m + 128].astype(ref.dtype)

    share(at_ref[1], emit, mine_ref, send_ref)


def share(core, emit, mine_ref, send_ref):
    @pl.when(core == 0)
    def _():
        emit(0, mine_ref)
        emit(1, send_ref)

    @pl.when(core != 0)
    def _():
        emit(1, mine_ref)
        emit(0, send_ref)


def triple(v):
    x, rows, _ = v.shape
    flat = v.reshape(x * rows, 128)
    t = lax.broadcasted_iota(jnp.int32, flat.shape, 0) % 8
    later = jnp.where(t == 7, 0.0, pltpu.roll(flat, x * rows - 1, 0))
    earlier = jnp.where(t == 0, 0.0, pltpu.roll(flat, 1, 0))
    wide = jnp.concatenate([later, flat, earlier], axis=1)
    return wide.astype(BF16).reshape(x, rows, 384)


def fold(sums, factor):
    lane = lax.broadcasted_iota(jnp.int32, (64, 128), 1)
    taps = []
    for g in sums:
        for l in range(3):
            part = g[:, l * 128 : (l + 1) * 128]
            f = jnp.where(lane < 64, part[0:64], part[64:128])
            taps.append((f + pltpu.roll(f, 64, 1)) * factor)
    taps.append(taps[-1])
    return [jnp.where(lane < 64, taps[2 * m], taps[2 * m + 1]) for m in range(14)]


def apply_taps(rows, taps):
    return lax.dot_general(rows, taps, (((1,), (1,)), ((), ())), preferred_element_type=F32)


def conv_kernel(
    factor, at_ref, back_ref, one_ref, left_ref, right_ref, w2_ref, w1_ref, i0, i1, i2, i3,
    grad_ref, mine_ref, send_ref, wide_ref, outer_ref, in_ref, acc_ref, turn_ref,
):
    me = at_ref[0]
    parts = (i0, i1, i2, i3)
    n = len(parts)
    for s, part in enumerate(parts):
        in_ref[pl.ds(lax.rem(me + n - s, n) * 4, 4)] = part[...].reshape(4, 64, 128)
    edge = jnp.zeros((2, 128, 384), BF16)
    wide_ref[0:2] = edge
    wide_ref[18:20] = edge
    outer_ref[0:2] = edge[:, :96]
    outer_ref[18:20] = edge[:, :96]
    wide_ref[2:18, 0:32] = triple(left_ref[:, 0:32].astype(F32))
    wide_ref[2:18, 32:96] = triple(back_ref[...].astype(F32))
    wide_ref[2:18, 96:128] = triple(right_ref[:, 0:32].astype(F32))
    for i in range(3):
        for j in range(3):
            rows = wide_ref[4 - 2 * i : 20 - 2 * i, 32 - 16 * j : 128 - 16 * j].reshape(1536, 384)
            part = apply_taps(rows, w2_ref[i * 3 + j])
            if i == 0 and j == 0:
                acc_ref[...] = part
            else:
                acc_ref[...] += part
    pre = jnp.concatenate([left_ref[:, 32:48], one_ref[...], right_ref[:, 32:48]], axis=1).astype(F32)
    outer_ref[2:18] = triple(jnp.where(pre > 0, acc_ref[...].reshape(16, 96, 128), 0.0))
    act = jnp.maximum(one_ref[...].astype(F32), 0.0).reshape(1024, 128).T.astype(BF16)
    sums = []
    for i in range(3):
        for j in range(3):
            rows = wide_ref[4 - 2 * i : 20 - 2 * i, 48 - 16 * j : 112 - 16 * j].reshape(1024, 384)
            sums.append(jnp.dot(act, rows, preferred_element_type=F32))
    second = fold(sums, factor)
    act = in_ref[...].astype(F32).reshape(1024, 128).T.astype(BF16)
    sums = []
    grad = jnp.zeros((256, 128), F32)
    for i in range(3):
        for j in range(3):
            rows = outer_ref[4 - 2 * i : 20 - 2 * i, 32 - 16 * j : 96 - 16 * j].reshape(1024, 384)
            sums.append(jnp.dot(act, rows, preferred_element_type=F32))
            mine = outer_ref[pl.ds(me * 4 + 4 - 2 * i, 4), 32 - 16 * j : 96 - 16 * j].reshape(256, 384)
            grad += apply_taps(mine, w1_ref[i * 3 + j])
    first = fold(sums, factor)
    turn_ref[...] = grad
    for x in range(4):
        for t in range(8):
            grad_ref[x, :, 128 * t : 128 * t + 128] = turn_ref[pl.ds(64 * x + t, 8, stride=8), :].astype(BF16)

    def emit(half, ref):
        for m in range(7):
            ref[64 * m : 64 * m + 64] = first[7 * half + m].astype(ref.dtype)
            ref[448 + 64 * m : 512 + 64 * m] = second[7 * half + m].astype(ref.dtype)

    share(at_ref[1], emit, mine_ref, send_ref)


def spread_kernel(at_ref, mine_ref, other_ref, tmine_ref, tother_ref, one_ref, two_ref, trans_ref):
    def emit(half, ref, tref):
        for out, at in ((one_ref, 0), (two_ref, 448)):
            for m in range(7):
                block = ref[at + 64 * m : at + 64 * m + 64].astype(F32)
                tap = 2 * (7 * half + m)
                out[tap] = block[:, 0:64]
                if tap < 26:
                    out[tap + 1] = block[:, 64:128]
        for m in range(4):
            trans_ref[256 * half : 256 * half + 256, 128 * m : 128 * m + 128] = tref[256 * m : 256 * m + 256].astype(F32)

    @pl.when(at_ref[1] == 0)
    def _():
        emit(0, mine_ref, tmine_ref)
        emit(1, other_ref, tother_ref)

    @pl.when(at_ref[1] != 0)
    def _():
        emit(1, mine_ref, tmine_ref)
        emit(0, other_ref, tother_ref)


def rotate(value, axis, step):
    n = lax.axis_size(axis)
    return lax.ppermute(value, axis, [(i, (i + step) % n) for i in range(n)])


def swap(value, axis, bit):
    n = lax.axis_size(axis)
    return lax.ppermute(value, axis, [(i, i ^ bit) for i in range(n)])


def on_chip(mine, send):
    return (mine + swap(send, "gy", 1).astype(F32)).astype(BF16)


def across(mine):
    return mine.astype(F32) + swap(mine, "gy", 2).astype(F32)


def slab_body(input_activation, pre_one, pre_two, w_one, w_two, w_trans, keep_mask, out_grad):
    factor = 1.0 / math.sqrt(
        input_activation.shape[0] * 4 * input_activation.shape[1] * 4 * (input_activation.shape[2] // 64)
    )
    at = jnp.stack([lax.axis_index("gx"), lax.rem(lax.axis_index("gy"), 2)]).astype(jnp.int32)
    shape = jax.ShapeDtypeStruct
    vmem = pltpu.VMEM
    natural = vmem((4, 8, 1024), BF16)
    first, second = call(
        pack_kernel,
        (shape((768, 128), BF16), shape((256, 128), BF16)),
        [
            vmem((8, 4, 8, 128), BF16), natural, natural, natural, vmem((3, 256, 128), F32),
            pltpu.SemaphoreType.DMA((4,)),
        ],
        0,
        56,
        (out_grad,),
        (pre_two,),
        (pre_one,),
        (input_activation,),
    )
    firsts = [first] + [rotate(first, "gx", s) for s in (1, 2, 3)]
    seconds = [second] + [rotate(second, "gx", s) for s in (1, 2, 3)]
    kept, mask, d2, d1 = call(
        weight_kernel,
        (
            shape((512, 512), BF16), shape((512, 512), BF16),
            shape((9, 128, 384), BF16), shape((9, 128, 384), BF16),
        ),
        [
            vmem((512, 512), BF16), vmem((8, 8), jnp.int32),
            vmem((27, 64, 64), BF16), vmem((27, 64, 64), BF16),
            pltpu.SemaphoreType.DMA((4,)),
        ],
        10**7,
        8,
        (w_trans,),
        (keep_mask,),
        (w_two,),
        (w_one,),
    )
    back, one, low, high, tmine, tsend = call(
        functools.partial(transition_kernel, factor),
        (
            shape((8, 2, 64, 128), BF16),
            shape((16, 64, 128), BF16),
            shape((8, 2, 48, 128), BF16),
            shape((8, 2, 48, 128), BF16),
            shape((1024, 128), F32),
            shape((1024, 128), BF16),
        ),
        [vmem((4, 256, 128), BF16), vmem((16, 64, 128), BF16)],
        4 * 256 * 512 * 512,
        12,
        at,
        *firsts,
        kept,
        mask,
    )
    n = lax.axis_size("gy")
    from_left = lax.ppermute(high, "gy", [(i, i + 1) for i in range(n - 1)])
    from_right = lax.ppermute(low, "gy", [(i + 1, i) for i in range(n - 1)])
    tmine = on_chip(tmine, tsend)
    tmine, from_left, from_right = lax.optimization_barrier((tmine, from_left, from_right))
    tmine = across(tmine)
    grad_in, mine, send = call(
        functools.partial(conv_kernel, factor),
        (shape((4, 8, 1024), BF16), shape((896, 128), F32), shape((896, 128), BF16)),
        [
            vmem((20, 128, 384), BF16),
            vmem((20, 96, 384), BF16),
            vmem((16, 64, 128), BF16),
            vmem((1536, 128), F32),
            vmem((256, 128), F32),
        ],
        2 * 128 * 3456 * (1536 + 1024 + 1024 + 256),
        20,
        at,
        back.reshape(16, 64, 128),
        one,
        from_left.reshape(16, 48, 128),
        from_right.reshape(16, 48, 128),
        d2,
        d1,
        *seconds,
    )
    send, tmine = lax.optimization_barrier((send, tmine))
    mine = across(on_chip(mine, send))
    tother = swap(tmine, "gy", 1)
    other = swap(mine, "gy", 1)
    grad_w_one, grad_w_two, grad_w_trans = call(
        spread_kernel,
        (shape((27, 64, 64), F32), shape((27, 64, 64), F32), shape((512, 512), F32)),
        [],
        0,
        12,
        at,
        mine,
        other,
        tmine,
        tother,
    )
    return (grad_in, grad_w_one, grad_w_two, grad_w_trans)


def solution(mesh):
    fits = mesh.shape["gx"] == 4 and mesh.shape["gy"] == 4

    def pick(*args):
        shapes = tuple(a.shape for a in args)
        known = (
            ((4, 8, 1024),) * 3 + ((27, 64, 64),) * 2 + ((512, 512), (8, 8), (8, 4, 8, 128))
        )
        return (slab_body if fits and shapes == known else body)(*args)

    return jax.shard_map(
        pick,
        mesh=mesh,
        in_specs=(
            P(("grp", "gx"), "gy", None),
            P(("grp", "gx"), "gy", None),
            P(("grp", "gx"), "gy", None),
            P(),
            P(),
            P(),
            P(),
            P("grp", "gy", None, "gx"),
        ),
        out_specs=(
            P(("grp", "gx"), "gy", None),
            P("grp", None, None),
            P("grp", None, None),
            P("grp", None),
        ),
        check_vma=False,
    )
```

```python
import functools
import math

import jax
import jax.numpy as jnp
from jax import lax
from jax.experimental import pallas as pl
from jax.experimental.pallas import tpu as pltpu
from jax.sharding import PartitionSpec as P

DILATION_STEP = 2
VMEM = pltpu.MemorySpace.VMEM
SMEM = pltpu.MemorySpace.SMEM
F32 = jnp.float32
BF16 = jnp.bfloat16


def padded(cells, sides, width):
    for axis, dim in sides:
        count = lax.axis_size(axis)
        ends = count - 1
        head = lax.slice_in_dim(cells, 0, width, axis=dim)
        tail = lax.slice_in_dim(cells, cells.shape[dim] - width, cells.shape[dim], axis=dim)
        cells = jnp.concatenate(
            [
                lax.ppermute(tail, axis, [(i, (i + 1) % count) for i in range(ends)]),
                cells,
                lax.ppermute(head, axis, [((i + 1) % count, i) for i in range(ends)]),
            ],
            axis=dim,
        )
    return cells


def split_layout(joined_layout, channel_count):
    return joined_layout.reshape(joined_layout.shape[0], joined_layout.shape[1], -1, channel_count)


def to_blocks(cube_volume):
    shape_all = cube_volume.shape
    parted = cube_volume.reshape(
        shape_all[0] // 2, 2, shape_all[1] // 2, 2, shape_all[2] // 2, 2, shape_all[3]
    )
    parted = parted.transpose(0, 2, 4, 1, 3, 5, 6)
    return parted.reshape(shape_all[0] // 2, shape_all[1] // 2, shape_all[2] // 2, 8 * shape_all[3])


def from_blocks(blocked, channel_count):
    shape_all = blocked.shape
    parted = blocked.reshape(shape_all[0], shape_all[1], shape_all[2], 2, 2, 2, channel_count)
    parted = parted.transpose(0, 3, 1, 4, 2, 5, 6)
    return parted.reshape(2 * shape_all[0], 2 * shape_all[1], 2 * shape_all[2], channel_count)


def padding_depth(cube_volume, margin):
    return jnp.pad(cube_volume, ((0, 0), (0, 0), (margin, margin), (0, 0)))


def weight_terms(bordered_input, upstream_gradient):
    channel_count = upstream_gradient.shape[3]
    grid_extent = upstream_gradient.shape
    padded_input = padding_depth(bordered_input, DILATION_STEP)
    flat_grad = upstream_gradient.reshape(-1, channel_count)
    partials = []
    for x_index in range(3):
        for y_index in range(3):
            sliding_window = padded_input[
                DILATION_STEP * x_index : DILATION_STEP * x_index + grid_extent[0],
                DILATION_STEP * y_index : DILATION_STEP * y_index + grid_extent[1],
            ]
            columns = jnp.concatenate(
                [
                    sliding_window[
                        :, :, DILATION_STEP * tap_index : DILATION_STEP * tap_index + grid_extent[2]
                    ].reshape(-1, channel_count)
                    for tap_index in range(3)
                ],
                axis=1,
            )
            partials.append(
                lax.dot_general(
                    columns, flat_grad, (((0,), (0,)), ((), ())), preferred_element_type=jnp.float32
                )
            )
    return jnp.stack(partials).reshape(27, channel_count, channel_count)


def data_terms(bordered_input, weights):
    channel_count = weights.shape[1]
    x_stretch = bordered_input.shape[0] - 2 * DILATION_STEP
    y_stretch = bordered_input.shape[1] - 2 * DILATION_STEP
    depth_cells = bordered_input.shape[2]
    padded_input = padding_depth(bordered_input, DILATION_STEP)
    stacked = jnp.transpose(weights, (0, 2, 1)).reshape(9, 3 * channel_count, channel_count)
    running = jnp.zeros((x_stretch * y_stretch * depth_cells, channel_count), jnp.float32)
    for x_index in range(3):
        for y_index in range(3):
            sliding_window = padded_input[
                DILATION_STEP * (2 - x_index) : DILATION_STEP * (2 - x_index) + x_stretch,
                DILATION_STEP * (2 - y_index) : DILATION_STEP * (2 - y_index) + y_stretch,
            ]
            columns = jnp.concatenate(
                [
                    sliding_window[
                        :,
                        :,
                        DILATION_STEP * (2 - tap_index) : DILATION_STEP * (2 - tap_index)
                        + depth_cells,
                    ].reshape(-1, channel_count)
                    for tap_index in range(3)
                ],
                axis=1,
            )
            running = running + jnp.dot(
                columns, stacked[x_index * 3 + y_index], preferred_element_type=jnp.float32
            )
    return running.reshape(x_stretch, y_stretch, depth_cells, channel_count)


def body(input_activation, pre_one, pre_two, w_one, w_two, w_trans, keep_mask, out_grad):
    channel_count = w_one.shape[1]
    x_stretch, y_stretch, joined_layout = input_activation.shape
    depth_cells = joined_layout // channel_count
    width_t = w_trans.shape[0]
    factor = 1.0 / math.sqrt(
        x_stretch * lax.axis_size("gx") * y_stretch * lax.axis_size("gy") * depth_cells
    )
    blocks = jnp.repeat(
        jnp.repeat(keep_mask.astype(jnp.bfloat16), channel_count, axis=0), channel_count, axis=1
    )
    w_kept = w_trans * blocks
    regrouped = lax.all_to_all(out_grad, "gx", split_axis=0, concat_axis=3, tiled=True)
    grad_rows = regrouped.reshape(-1, width_t)
    back_blocks = lax.dot_general(
        grad_rows, w_kept, (((1,), (1,)), ((), ())), preferred_element_type=jnp.float32
    ).astype(jnp.bfloat16)
    act_two = split_layout(jnp.maximum(pre_two, 0), channel_count)
    two_rows = to_blocks(act_two).reshape(-1, width_t)
    trans_term = (
        lax.dot_general(
            two_rows, grad_rows, (((0,), (0,)), ((), ())), preferred_element_type=jnp.float32
        )
        * blocks.astype(jnp.float32)
        * factor
    )
    grad_w_trans = lax.psum(trans_term, ("gx", "gy"))
    back_two = from_blocks(
        back_blocks.reshape(x_stretch // 2, y_stretch // 2, depth_cells // 2, width_t),
        channel_count,
    )
    back_two = jnp.where(
        split_layout(pre_two, channel_count) > 0, back_two, jnp.zeros_like(back_two)
    )
    first_activation = jnp.maximum(pre_one, 0)
    bordered_input = padded(
        jnp.concatenate([input_activation, first_activation], axis=2),
        (("gx", 0), ("gy", 1)),
        DILATION_STEP,
    )
    in_rim = split_layout(bordered_input[:, :, :joined_layout], channel_count)
    one_rim = split_layout(bordered_input[:, :, joined_layout:], channel_count)
    two_term = weight_terms(one_rim, back_two) * factor
    flattened_backward = back_two.reshape(x_stretch, y_stretch, joined_layout)
    narrowed_slice = split_layout(
        padded(flattened_backward, (("gx", 0), ("gy", 1)), DILATION_STEP), channel_count
    )
    first_backward = data_terms(narrowed_slice, w_two)
    first_backward = jnp.where(
        split_layout(pre_one, channel_count) > 0, first_backward, jnp.zeros_like(first_backward)
    ).astype(jnp.bfloat16)
    one_grad_rim = split_layout(
        padded(
            first_backward.reshape(x_stretch, y_stretch, joined_layout),
            (("gx", 0), ("gy", 1)),
            DILATION_STEP,
        ),
        channel_count,
    )
    grad_w_two = lax.psum(two_term, ("gx", "gy"))
    one_term = weight_terms(in_rim, first_backward) * factor
    grad_w_one = lax.psum(one_term, ("gx", "gy"))
    grad_in = (
        data_terms(one_grad_rim, w_one)
        .astype(jnp.bfloat16)
        .reshape(x_stretch, y_stretch, joined_layout)
    )
    return (grad_in, grad_w_one, grad_w_two, grad_w_trans)


def call(kernel, out_shape, scratch, flops, limit, *args):
    spec = []
    for a in args:
        if isinstance(a, tuple):
            spec.append(pl.BlockSpec(memory_space=pltpu.MemorySpace.HBM))
        elif a.dtype == jnp.int32:
            spec.append(pl.BlockSpec(memory_space=SMEM))
        else:
            spec.append(pl.BlockSpec(memory_space=VMEM))
    arrays = [a[0] if isinstance(a, tuple) else a for a in args]
    return pl.pallas_call(
        kernel,
        out_shape=out_shape,
        in_specs=spec,
        out_specs=jax.tree.map(lambda _: pl.BlockSpec(memory_space=VMEM), out_shape),
        scratch_shapes=scratch,
        cost_estimate=pl.CostEstimate(
            flops=flops,
            transcendentals=0,
            bytes_accessed=sum(a.size * a.dtype.itemsize for a in arrays),
        ),
        compiler_params=pltpu.CompilerParams(vmem_limit_bytes=limit * 1024 * 1024),
    )(*arrays)


def fetch(pairs, sems):
    copies = [pltpu.make_async_copy(src, dst, sems.at[k]) for k, (src, dst) in enumerate(pairs)]
    for copy in copies:
        copy.start()
    return copies


def pack_kernel(og, two, one, act, first_ref, second_ref, og_v, two_v, one_v, act_v, turn_ref, sems):
    copies = fetch(((og, og_v), (two, two_v), (one, one_v), (act, act_v)), sems)
    copies[0].wait()
    first_ref[0:256] = og_v[...].astype(F32).reshape(256, 128).astype(BF16)
    for k, (ref, out, at) in enumerate(((two_v, first_ref, 256), (one_v, first_ref, 512), (act_v, second_ref, 0))):
        copies[k + 1].wait()
        for x in range(4):
            for t in range(8):
                turn_ref[k, pl.ds(64 * x + t, 8, stride=8), :] = ref[x, :, 128 * t : 128 * t + 128].astype(F32)
        out[at : at + 256] = turn_ref[k].astype(BF16)


def weight_kernel(wt, keep, w2, w1, kept_ref, mask_ref, d2_ref, d1_ref, wt_v, keep_v, w2_v, w1_v, sems):
    copies = fetch(((keep, keep_v), (wt, wt_v), (w2, w2_v), (w1, w1_v)), sems)
    copies[0].wait()
    width = wt_v.shape[0]
    blocks = keep_v.shape[0]
    side = width // blocks
    left = (
        lax.broadcasted_iota(jnp.int32, (width, blocks), 0) // side
        == lax.broadcasted_iota(jnp.int32, (width, blocks), 1)
    ).astype(BF16)
    right = (
        lax.broadcasted_iota(jnp.int32, (blocks, width), 1) // side
        == lax.broadcasted_iota(jnp.int32, (blocks, width), 0)
    ).astype(BF16)
    wide = jnp.dot(keep_v[...].astype(F32).astype(BF16), right, preferred_element_type=F32).astype(BF16)
    mask = jnp.dot(left, wide, preferred_element_type=F32)
    mask_ref[...] = mask.astype(BF16)
    copies[1].wait()
    kept_ref[...] = (wt_v[...].astype(F32) * mask).astype(BF16)
    none = jnp.zeros((64, 64), BF16)
    for k, (ref, out) in enumerate(((w2_v, d2_ref), (w1_v, d1_ref))):
        copies[k + 2].wait()
        for tap in range(27):
            w = ref[tap]
            at = 128 * (tap % 3)
            out[tap // 3, 0:64, at : at + 128] = jnp.concatenate([w, none], axis=1)
            out[tap // 3, 64:128, at : at + 128] = jnp.concatenate([none, w], axis=1)


def transition_kernel(
    factor, at_ref, a0, a1, a2, a3, kept_ref, mask_ref, back_ref, one_ref, low_ref, high_ref, mine_ref, send_ref, og_ref, two_ref
):
    me = at_ref[0]
    parts = (a0, a1, a2, a3)
    n = len(parts)
    for s, part in enumerate(parts):
        src = lax.rem(me + n - s, n)
        og_ref[src] = part[0:256]
        spot = pl.ds(src * 4, 4)
        two_ref[spot] = part[256:512].reshape(4, 64, 128)
        one_ref[spot] = part[512:768].reshape(4, 64, 128)
    og = jnp.concatenate([og_ref[j] for j in range(n)], axis=1)
    back = lax.dot_general(og, kept_ref[...], (((1,), (1,)), ((), ())), preferred_element_type=F32)
    two = two_ref[...].astype(F32).reshape(8, 2, 4, 2, 8, 128)
    cells = []
    for p in range(2):
        halves = []
        for q in range(2):
            pre = two[:, p, :, q]
            at = (p * 2 + q) * 128
            grad = back[:, at : at + 128].reshape(8, 4, 8, 128)
            halves.append(jnp.where(pre > 0, grad, 0.0))
            cells.append(jnp.maximum(pre, 0.0).reshape(256, 128).astype(BF16))
        back_ref[:, p] = jnp.stack(halves, axis=2).reshape(8, 64, 128).astype(BF16)
    low_ref[:, :, 0:32] = back_ref[:, :, 0:32]
    high_ref[:, :, 0:32] = back_ref[:, :, 32:64]
    low_ref[:, :, 32:48] = one_ref[:, 0:16].reshape(8, 2, 16, 128)
    high_ref[:, :, 32:48] = one_ref[:, 48:64].reshape(8, 2, 16, 128)
    flat = jnp.concatenate(cells, axis=1)
    trans = lax.dot_general(flat, og, (((0,), (0,)), ((), ())), preferred_element_type=F32)
    trans = trans * mask_ref[...].astype(F32) * factor

    def emit(half, ref):
        for m in range(4):
            ref[256 * m : 256 * m + 256] = trans[256 * half : 256 * half + 256, 128 * m : 128 * m + 128].astype(ref.dtype)

    share(at_ref[1], emit, mine_ref, send_ref)


def share(core, emit, mine_ref, send_ref):
    @pl.when(core == 0)
    def _():
        emit(0, mine_ref)
        emit(1, send_ref)

    @pl.when(core != 0)
    def _():
        emit(1, mine_ref)
        emit(0, send_ref)


def triple(v):
    x, rows, _ = v.shape
    flat = v.reshape(x * rows, 128)
    t = lax.broadcasted_iota(jnp.int32, flat.shape, 0) % 8
    later = jnp.where(t == 7, 0.0, pltpu.roll(flat, x * rows - 1, 0))
    earlier = jnp.where(t == 0, 0.0, pltpu.roll(flat, 1, 0))
    wide = jnp.concatenate([later, flat, earlier], axis=1)
    return wide.astype(BF16).reshape(x, rows, 384)


def fold(sums, factor):
    lane = lax.broadcasted_iota(jnp.int32, (64, 128), 1)
    taps = []
    for g in sums:
        for l in range(3):
            part = g[:, l * 128 : (l + 1) * 128]
            f = jnp.where(lane < 64, part[0:64], part[64:128])
            taps.append((f + pltpu.roll(f, 64, 1)) * factor)
    taps.append(taps[-1])
    return [jnp.where(lane < 64, taps[2 * m], taps[2 * m + 1]) for m in range(14)]


def apply_taps(rows, taps):
    return lax.dot_general(rows, taps, (((1,), (1,)), ((), ())), preferred_element_type=F32)


def conv_kernel(
    factor, at_ref, back_ref, one_ref, left_ref, right_ref, w2_ref, w1_ref, i0, i1, i2, i3,
    grad_ref, mine_ref, send_ref, wide_ref, outer_ref, in_ref, acc_ref, turn_ref,
):
    me = at_ref[0]
    parts = (i0, i1, i2, i3)
    n = len(parts)
    for s, part in enumerate(parts):
        in_ref[pl.ds(lax.rem(me + n - s, n) * 4, 4)] = part[...].reshape(4, 64, 128)
    edge = jnp.zeros((2, 128, 384), BF16)
    wide_ref[0:2] = edge
    wide_ref[18:20] = edge
    outer_ref[0:2] = edge[:, :96]
    outer_ref[18:20] = edge[:, :96]
    wide_ref[2:18, 0:32] = triple(left_ref[:, 0:32].astype(F32))
    wide_ref[2:18, 32:96] = triple(back_ref[...].astype(F32))
    wide_ref[2:18, 96:128] = triple(right_ref[:, 0:32].astype(F32))
    for i in range(3):
        for j in range(3):
            rows = wide_ref[4 - 2 * i : 20 - 2 * i, 32 - 16 * j : 128 - 16 * j].reshape(1536, 384)
            part = apply_taps(rows, w2_ref[i * 3 + j])
            if i == 0 and j == 0:
                acc_ref[...] = part
            else:
                acc_ref[...] += part
    pre = jnp.concatenate([left_ref[:, 32:48], one_ref[...], right_ref[:, 32:48]], axis=1).astype(F32)
    outer_ref[2:18] = triple(jnp.where(pre > 0, acc_ref[...].reshape(16, 96, 128), 0.0))
    act = jnp.maximum(one_ref[...].astype(F32), 0.0).reshape(1024, 128).T.astype(BF16)
    sums = []
    for i in range(3):
        for j in range(3):
            rows = wide_ref[4 - 2 * i : 20 - 2 * i, 48 - 16 * j : 112 - 16 * j].reshape(1024, 384)
            sums.append(jnp.dot(act, rows, preferred_element_type=F32))
    second = fold(sums, factor)
    act = in_ref[...].astype(F32).reshape(1024, 128).T.astype(BF16)
    sums = []
    grad = jnp.zeros((256, 128), F32)
    for i in range(3):
        for j in range(3):
            rows = outer_ref[4 - 2 * i : 20 - 2 * i, 32 - 16 * j : 96 - 16 * j].reshape(1024, 384)
            sums.append(jnp.dot(act, rows, preferred_element_type=F32))
            mine = outer_ref[pl.ds(me * 4 + 4 - 2 * i, 4), 32 - 16 * j : 96 - 16 * j].reshape(256, 384)
            grad += apply_taps(mine, w1_ref[i * 3 + j])
    first = fold(sums, factor)
    turn_ref[...] = grad
    for x in range(4):
        for t in range(8):
            grad_ref[x, :, 128 * t : 128 * t + 128] = turn_ref[pl.ds(64 * x + t, 8, stride=8), :].astype(BF16)

    def emit(half, ref):
        for m in range(7):
            ref[64 * m : 64 * m + 64] = first[7 * half + m].astype(ref.dtype)
            ref[448 + 64 * m : 512 + 64 * m] = second[7 * half + m].astype(ref.dtype)

    share(at_ref[1], emit, mine_ref, send_ref)


def spread_kernel(at_ref, mine_ref, other_ref, one_ref, two_ref):
    def emit(half, ref):
        for out, at in ((one_ref, 0), (two_ref, 448)):
            for m in range(7):
                block = ref[at + 64 * m : at + 64 * m + 64].astype(F32)
                tap = 2 * (7 * half + m)
                out[tap] = block[:, 0:64]
                if tap < 26:
                    out[tap + 1] = block[:, 64:128]

    share(at_ref[1], emit, mine_ref, other_ref)


def trans_kernel(at_ref, mine_ref, other_ref, trans_ref):
    def emit(half, ref):
        for m in range(4):
            trans_ref[256 * half : 256 * half + 256, 128 * m : 128 * m + 128] = ref[256 * m : 256 * m + 256].astype(F32)

    share(at_ref[1], emit, mine_ref, other_ref)


def rotate(value, axis, step):
    n = lax.axis_size(axis)
    return lax.ppermute(value, axis, [(i, (i + step) % n) for i in range(n)])


def swap(value, axis, bit):
    n = lax.axis_size(axis)
    return lax.ppermute(value, axis, [(i, i ^ bit) for i in range(n)])


def on_chip(mine, send):
    return (mine + swap(send, "gy", 1).astype(F32)).astype(BF16)


def across(mine):
    return mine.astype(F32) + swap(mine, "gy", 2).astype(F32)


def slab_body(input_activation, pre_one, pre_two, w_one, w_two, w_trans, keep_mask, out_grad):
    factor = 1.0 / math.sqrt(
        input_activation.shape[0] * 4 * input_activation.shape[1] * 4 * (input_activation.shape[2] // 64)
    )
    at = jnp.stack([lax.axis_index("gx"), lax.rem(lax.axis_index("gy"), 2)]).astype(jnp.int32)
    shape = jax.ShapeDtypeStruct
    vmem = pltpu.VMEM
    natural = vmem((4, 8, 1024), BF16)
    first, second = call(
        pack_kernel,
        (shape((768, 128), BF16), shape((256, 128), BF16)),
        [
            vmem((8, 4, 8, 128), BF16), natural, natural, natural, vmem((3, 256, 128), F32),
            pltpu.SemaphoreType.DMA((4,)),
        ],
        0,
        56,
        (out_grad,),
        (pre_two,),
        (pre_one,),
        (input_activation,),
    )
    firsts = [first] + [rotate(first, "gx", s) for s in (1, 2, 3)]
    seconds = [second] + [rotate(second, "gx", s) for s in (1, 2, 3)]
    kept, mask, d2, d1 = call(
        weight_kernel,
        (
            shape((512, 512), BF16), shape((512, 512), BF16),
            shape((9, 128, 384), BF16), shape((9, 128, 384), BF16),
        ),
        [
            vmem((512, 512), BF16), vmem((8, 8), jnp.int32),
            vmem((27, 64, 64), BF16), vmem((27, 64, 64), BF16),
            pltpu.SemaphoreType.DMA((4,)),
        ],
        10**7,
        8,
        (w_trans,),
        (keep_mask,),
        (w_two,),
        (w_one,),
    )
    back, one, low, high, tmine, tsend = call(
        functools.partial(transition_kernel, factor),
        (
            shape((8, 2, 64, 128), BF16),
            shape((16, 64, 128), BF16),
            shape((8, 2, 48, 128), BF16),
            shape((8, 2, 48, 128), BF16),
            shape((1024, 128), F32),
            shape((1024, 128), BF16),
        ),
        [vmem((4, 256, 128), BF16), vmem((16, 64, 128), BF16)],
        4 * 256 * 512 * 512,
        12,
        at,
        *firsts,
        kept,
        mask,
    )
    tsend, *seconds = lax.optimization_barrier((tsend, *seconds))
    n = lax.axis_size("gy")
    from_left = lax.ppermute(high, "gy", [(i, i + 1) for i in range(n - 1)])
    from_right = lax.ppermute(low, "gy", [(i + 1, i) for i in range(n - 1)])
    tmine = on_chip(tmine, tsend)
    tmine, from_left, from_right = lax.optimization_barrier((tmine, from_left, from_right))
    tmine = across(tmine)
    grad_in, mine, send = call(
        functools.partial(conv_kernel, factor),
        (shape((4, 8, 1024), BF16), shape((896, 128), F32), shape((896, 128), BF16)),
        [
            vmem((20, 128, 384), BF16),
            vmem((20, 96, 384), BF16),
            vmem((16, 64, 128), BF16),
            vmem((1536, 128), F32),
            vmem((256, 128), F32),
        ],
        2 * 128 * 3456 * (1536 + 1024 + 1024 + 256),
        20,
        at,
        back.reshape(16, 64, 128),
        one,
        from_left.reshape(16, 48, 128),
        from_right.reshape(16, 48, 128),
        d2,
        d1,
        *seconds,
    )
    send, tmine = lax.optimization_barrier((send, tmine))
    mine = across(on_chip(mine, send))
    tother = swap(tmine, "gy", 1)
    other = swap(mine, "gy", 1)
    grad_w_trans = call(trans_kernel, shape((512, 512), F32), [], 10**7, 6, at, tmine, tother)
    grad_w_one, grad_w_two = call(
        spread_kernel,
        (shape((27, 64, 64), F32), shape((27, 64, 64), F32)),
        [],
        0,
        6,
        at,
        mine,
        other,
    )
    return (grad_in, grad_w_one, grad_w_two, grad_w_trans)


def solution(mesh):
    fits = mesh.shape["gx"] == 4 and mesh.shape["gy"] == 4

    def pick(*args):
        shapes = tuple(a.shape for a in args)
        known = (
            ((4, 8, 1024),) * 3 + ((27, 64, 64),) * 2 + ((512, 512), (8, 8), (8, 4, 8, 128))
        )
        return (slab_body if fits and shapes == known else body)(*args)

    return jax.shard_map(
        pick,
        mesh=mesh,
        in_specs=(
            P(("grp", "gx"), "gy", None),
            P(("grp", "gx"), "gy", None),
            P(("grp", "gx"), "gy", None),
            P(),
            P(),
            P(),
            P(),
            P("grp", "gy", None, "gx"),
        ),
        out_specs=(
            P(("grp", "gx"), "gy", None),
            P("grp", None, None),
            P("grp", None, None),
            P("grp", None),
        ),
        check_vma=False,
    )
```

```python
import functools
import math

import jax
import jax.numpy as jnp
from jax import lax
from jax.experimental import pallas as pl
from jax.experimental.pallas import tpu as pltpu
from jax.sharding import PartitionSpec as P

DILATION_STEP = 2
VMEM = pltpu.MemorySpace.VMEM
SMEM = pltpu.MemorySpace.SMEM
F32 = jnp.float32
BF16 = jnp.bfloat16


def padded(cells, sides, width):
    for axis, dim in sides:
        count = lax.axis_size(axis)
        ends = count - 1
        head = lax.slice_in_dim(cells, 0, width, axis=dim)
        tail = lax.slice_in_dim(cells, cells.shape[dim] - width, cells.shape[dim], axis=dim)
        cells = jnp.concatenate(
            [
                lax.ppermute(tail, axis, [(i, (i + 1) % count) for i in range(ends)]),
                cells,
                lax.ppermute(head, axis, [((i + 1) % count, i) for i in range(ends)]),
            ],
            axis=dim,
        )
    return cells


def split_layout(joined_layout, channel_count):
    return joined_layout.reshape(joined_layout.shape[0], joined_layout.shape[1], -1, channel_count)


def to_blocks(cube_volume):
    shape_all = cube_volume.shape
    parted = cube_volume.reshape(
        shape_all[0] // 2, 2, shape_all[1] // 2, 2, shape_all[2] // 2, 2, shape_all[3]
    )
    parted = parted.transpose(0, 2, 4, 1, 3, 5, 6)
    return parted.reshape(shape_all[0] // 2, shape_all[1] // 2, shape_all[2] // 2, 8 * shape_all[3])


def from_blocks(blocked, channel_count):
    shape_all = blocked.shape
    parted = blocked.reshape(shape_all[0], shape_all[1], shape_all[2], 2, 2, 2, channel_count)
    parted = parted.transpose(0, 3, 1, 4, 2, 5, 6)
    return parted.reshape(2 * shape_all[0], 2 * shape_all[1], 2 * shape_all[2], channel_count)


def padding_depth(cube_volume, margin):
    return jnp.pad(cube_volume, ((0, 0), (0, 0), (margin, margin), (0, 0)))


def weight_terms(bordered_input, upstream_gradient):
    channel_count = upstream_gradient.shape[3]
    grid_extent = upstream_gradient.shape
    padded_input = padding_depth(bordered_input, DILATION_STEP)
    flat_grad = upstream_gradient.reshape(-1, channel_count)
    partials = []
    for x_index in range(3):
        for y_index in range(3):
            sliding_window = padded_input[
                DILATION_STEP * x_index : DILATION_STEP * x_index + grid_extent[0],
                DILATION_STEP * y_index : DILATION_STEP * y_index + grid_extent[1],
            ]
            columns = jnp.concatenate(
                [
                    sliding_window[
                        :, :, DILATION_STEP * tap_index : DILATION_STEP * tap_index + grid_extent[2]
                    ].reshape(-1, channel_count)
                    for tap_index in range(3)
                ],
                axis=1,
            )
            partials.append(
                lax.dot_general(
                    columns, flat_grad, (((0,), (0,)), ((), ())), preferred_element_type=jnp.float32
                )
            )
    return jnp.stack(partials).reshape(27, channel_count, channel_count)


def data_terms(bordered_input, weights):
    channel_count = weights.shape[1]
    x_stretch = bordered_input.shape[0] - 2 * DILATION_STEP
    y_stretch = bordered_input.shape[1] - 2 * DILATION_STEP
    depth_cells = bordered_input.shape[2]
    padded_input = padding_depth(bordered_input, DILATION_STEP)
    stacked = jnp.transpose(weights, (0, 2, 1)).reshape(9, 3 * channel_count, channel_count)
    running = jnp.zeros((x_stretch * y_stretch * depth_cells, channel_count), jnp.float32)
    for x_index in range(3):
        for y_index in range(3):
            sliding_window = padded_input[
                DILATION_STEP * (2 - x_index) : DILATION_STEP * (2 - x_index) + x_stretch,
                DILATION_STEP * (2 - y_index) : DILATION_STEP * (2 - y_index) + y_stretch,
            ]
            columns = jnp.concatenate(
                [
                    sliding_window[
                        :,
                        :,
                        DILATION_STEP * (2 - tap_index) : DILATION_STEP * (2 - tap_index)
                        + depth_cells,
                    ].reshape(-1, channel_count)
                    for tap_index in range(3)
                ],
                axis=1,
            )
            running = running + jnp.dot(
                columns, stacked[x_index * 3 + y_index], preferred_element_type=jnp.float32
            )
    return running.reshape(x_stretch, y_stretch, depth_cells, channel_count)


def body(input_activation, pre_one, pre_two, w_one, w_two, w_trans, keep_mask, out_grad):
    channel_count = w_one.shape[1]
    x_stretch, y_stretch, joined_layout = input_activation.shape
    depth_cells = joined_layout // channel_count
    width_t = w_trans.shape[0]
    factor = 1.0 / math.sqrt(
        x_stretch * lax.axis_size("gx") * y_stretch * lax.axis_size("gy") * depth_cells
    )
    blocks = jnp.repeat(
        jnp.repeat(keep_mask.astype(jnp.bfloat16), channel_count, axis=0), channel_count, axis=1
    )
    w_kept = w_trans * blocks
    regrouped = lax.all_to_all(out_grad, "gx", split_axis=0, concat_axis=3, tiled=True)
    grad_rows = regrouped.reshape(-1, width_t)
    back_blocks = lax.dot_general(
        grad_rows, w_kept, (((1,), (1,)), ((), ())), preferred_element_type=jnp.float32
    ).astype(jnp.bfloat16)
    act_two = split_layout(jnp.maximum(pre_two, 0), channel_count)
    two_rows = to_blocks(act_two).reshape(-1, width_t)
    trans_term = (
        lax.dot_general(
            two_rows, grad_rows, (((0,), (0,)), ((), ())), preferred_element_type=jnp.float32
        )
        * blocks.astype(jnp.float32)
        * factor
    )
    grad_w_trans = lax.psum(trans_term, ("gx", "gy"))
    back_two = from_blocks(
        back_blocks.reshape(x_stretch // 2, y_stretch // 2, depth_cells // 2, width_t),
        channel_count,
    )
    back_two = jnp.where(
        split_layout(pre_two, channel_count) > 0, back_two, jnp.zeros_like(back_two)
    )
    first_activation = jnp.maximum(pre_one, 0)
    bordered_input = padded(
        jnp.concatenate([input_activation, first_activation], axis=2),
        (("gx", 0), ("gy", 1)),
        DILATION_STEP,
    )
    in_rim = split_layout(bordered_input[:, :, :joined_layout], channel_count)
    one_rim = split_layout(bordered_input[:, :, joined_layout:], channel_count)
    two_term = weight_terms(one_rim, back_two) * factor
    flattened_backward = back_two.reshape(x_stretch, y_stretch, joined_layout)
    narrowed_slice = split_layout(
        padded(flattened_backward, (("gx", 0), ("gy", 1)), DILATION_STEP), channel_count
    )
    first_backward = data_terms(narrowed_slice, w_two)
    first_backward = jnp.where(
        split_layout(pre_one, channel_count) > 0, first_backward, jnp.zeros_like(first_backward)
    ).astype(jnp.bfloat16)
    one_grad_rim = split_layout(
        padded(
            first_backward.reshape(x_stretch, y_stretch, joined_layout),
            (("gx", 0), ("gy", 1)),
            DILATION_STEP,
        ),
        channel_count,
    )
    grad_w_two = lax.psum(two_term, ("gx", "gy"))
    one_term = weight_terms(in_rim, first_backward) * factor
    grad_w_one = lax.psum(one_term, ("gx", "gy"))
    grad_in = (
        data_terms(one_grad_rim, w_one)
        .astype(jnp.bfloat16)
        .reshape(x_stretch, y_stretch, joined_layout)
    )
    return (grad_in, grad_w_one, grad_w_two, grad_w_trans)


def call(kernel, out_shape, scratch, flops, limit, *args):
    spec = []
    for a in args:
        if isinstance(a, tuple):
            spec.append(pl.BlockSpec(memory_space=pltpu.MemorySpace.HBM))
        elif a.dtype == jnp.int32:
            spec.append(pl.BlockSpec(memory_space=SMEM))
        else:
            spec.append(pl.BlockSpec(memory_space=VMEM))
    arrays = [a[0] if isinstance(a, tuple) else a for a in args]
    return pl.pallas_call(
        kernel,
        out_shape=out_shape,
        in_specs=spec,
        out_specs=jax.tree.map(lambda _: pl.BlockSpec(memory_space=VMEM), out_shape),
        scratch_shapes=scratch,
        cost_estimate=pl.CostEstimate(
            flops=flops,
            transcendentals=0,
            bytes_accessed=sum(a.size * a.dtype.itemsize for a in arrays),
        ),
        compiler_params=pltpu.CompilerParams(vmem_limit_bytes=limit * 1024 * 1024),
    )(*arrays)


def fetch(pairs, sems):
    copies = [pltpu.make_async_copy(src, dst, sems.at[k]) for k, (src, dst) in enumerate(pairs)]
    for copy in copies:
        copy.start()
    return copies


def pack_kernel(og, two, one, act, first_ref, second_ref, og_v, two_v, one_v, act_v, turn_ref, sems):
    copies = fetch(((og, og_v), (two, two_v), (one, one_v), (act, act_v)), sems)
    copies[0].wait()
    first_ref[0:256] = og_v[...].astype(F32).reshape(256, 128).astype(BF16)
    for k, (ref, out, at) in enumerate(((two_v, first_ref, 256), (one_v, second_ref, 0), (act_v, second_ref, 256))):
        copies[k + 1].wait()
        for x in range(4):
            for t in range(8):
                turn_ref[k, pl.ds(64 * x + t, 8, stride=8), :] = ref[x, :, 128 * t : 128 * t + 128].astype(F32)
        out[at : at + 256] = turn_ref[k].astype(BF16)


def weight_kernel(wt, keep, w2, w1, kept_ref, mask_ref, d2_ref, d1_ref, wt_v, keep_v, w2_v, w1_v, sems):
    copies = fetch(((keep, keep_v), (wt, wt_v), (w2, w2_v), (w1, w1_v)), sems)
    copies[0].wait()
    width = wt_v.shape[0]
    blocks = keep_v.shape[0]
    side = width // blocks
    left = (
        lax.broadcasted_iota(jnp.int32, (width, blocks), 0) // side
        == lax.broadcasted_iota(jnp.int32, (width, blocks), 1)
    ).astype(BF16)
    right = (
        lax.broadcasted_iota(jnp.int32, (blocks, width), 1) // side
        == lax.broadcasted_iota(jnp.int32, (blocks, width), 0)
    ).astype(BF16)
    wide = jnp.dot(keep_v[...].astype(F32).astype(BF16), right, preferred_element_type=F32).astype(BF16)
    mask = jnp.dot(left, wide, preferred_element_type=F32)
    mask_ref[...] = mask.astype(BF16)
    copies[1].wait()
    kept_ref[...] = (wt_v[...].astype(F32) * mask).astype(BF16)
    none = jnp.zeros((64, 64), BF16)
    for k, (ref, out) in enumerate(((w2_v, d2_ref), (w1_v, d1_ref))):
        copies[k + 2].wait()
        for tap in range(27):
            w = ref[tap]
            at = 128 * (tap % 3)
            out[tap // 3, 0:64, at : at + 128] = jnp.concatenate([w, none], axis=1)
            out[tap // 3, 64:128, at : at + 128] = jnp.concatenate([none, w], axis=1)


def transition_kernel(
    factor, at_ref, a0, a1, a2, a3, kept_ref, mask_ref, back_ref, low_ref, high_ref, mine_ref, send_ref, og_ref, two_ref
):
    me = at_ref[0]
    parts = (a0, a1, a2, a3)
    n = len(parts)
    for s, part in enumerate(parts):
        src = lax.rem(me + n - s, n)
        og_ref[src] = part[0:256]
        two_ref[pl.ds(src * 4, 4)] = part[256:512].reshape(4, 64, 128)
    og = jnp.concatenate([og_ref[j] for j in range(n)], axis=1)
    back = lax.dot_general(og, kept_ref[...], (((1,), (1,)), ((), ())), preferred_element_type=F32)
    two = two_ref[...].astype(F32).reshape(8, 2, 4, 2, 8, 128)
    cells = []
    for p in range(2):
        halves = []
        for q in range(2):
            pre = two[:, p, :, q]
            at = (p * 2 + q) * 128
            grad = back[:, at : at + 128].reshape(8, 4, 8, 128)
            halves.append(jnp.where(pre > 0, grad, 0.0))
            cells.append(jnp.maximum(pre, 0.0).reshape(256, 128).astype(BF16))
        back_ref[:, p] = jnp.stack(halves, axis=2).reshape(8, 64, 128).astype(BF16)
    low_ref[...] = back_ref[:, :, 0:16].reshape(16, 16, 128)
    high_ref[...] = back_ref[:, :, 48:64].reshape(16, 16, 128)
    flat = jnp.concatenate(cells, axis=1)
    trans = lax.dot_general(flat, og, (((0,), (0,)), ((), ())), preferred_element_type=F32)
    trans = trans * mask_ref[...].astype(F32) * factor

    def emit(half, ref):
        for m in range(4):
            ref[256 * m : 256 * m + 256] = trans[256 * half : 256 * half + 256, 128 * m : 128 * m + 128].astype(ref.dtype)

    share(at_ref[1], emit, mine_ref, send_ref)


def share(core, emit, mine_ref, send_ref):
    @pl.when(core == 0)
    def _():
        emit(0, mine_ref)
        emit(1, send_ref)

    @pl.when(core != 0)
    def _():
        emit(1, mine_ref)
        emit(0, send_ref)


def triple(v):
    x, rows, _ = v.shape
    flat = v.reshape(x * rows, 128)
    t = lax.broadcasted_iota(jnp.int32, flat.shape, 0) % 8
    later = jnp.where(t == 7, 0.0, pltpu.roll(flat, x * rows - 1, 0))
    earlier = jnp.where(t == 0, 0.0, pltpu.roll(flat, 1, 0))
    wide = jnp.concatenate([later, flat, earlier], axis=1)
    return wide.astype(BF16).reshape(x, rows, 384)


def fold(sums, factor):
    lane = lax.broadcasted_iota(jnp.int32, (64, 128), 1)
    taps = []
    for g in sums:
        for l in range(3):
            part = g[:, l * 128 : (l + 1) * 128]
            f = jnp.where(lane < 64, part[0:64], part[64:128])
            taps.append((f + pltpu.roll(f, 64, 1)) * factor)
    taps.append(taps[-1])
    return [jnp.where(lane < 64, taps[2 * m], taps[2 * m + 1]) for m in range(14)]


def apply_taps(rows, taps):
    return lax.dot_general(rows, taps, (((1,), (1,)), ((), ())), preferred_element_type=F32)


def widen(wide_ref, left_ref, own_ref, right_ref):
    edge = jnp.zeros((2, 96, 384), BF16)
    wide_ref[0:2] = edge
    wide_ref[18:20] = edge
    wide_ref[2:18, 0:16] = triple(left_ref[...].astype(F32))
    wide_ref[2:18, 16:80] = triple(own_ref[...].astype(F32))
    wide_ref[2:18, 80:96] = triple(right_ref[...].astype(F32))


def weight_sums(act, wide_ref):
    turned = act.T.astype(BF16)
    sums = []
    for i in range(3):
        for j in range(3):
            rows = wide_ref[4 - 2 * i : 20 - 2 * i, 32 - 16 * j : 96 - 16 * j].reshape(1024, 384)
            sums.append(jnp.dot(turned, rows, preferred_element_type=F32))
    return sums


def first_kernel(back_ref, left_ref, right_ref, w_ref, wide_ref, acc_ref):
    widen(wide_ref, left_ref, back_ref, right_ref)
    for i in range(3):
        for j in range(3):
            rows = wide_ref[4 - 2 * i : 20 - 2 * i, 32 - 16 * j : 96 - 16 * j].reshape(1024, 384)
            part = apply_taps(rows, w_ref[i * 3 + j])
            if i == 0 and j == 0:
                acc_ref[...] = part
            else:
                acc_ref[...] += part


def mask_kernel(at_ref, acc_ref, p0, p1, p2, p3, first_ref, low_ref, high_ref, one_ref, act_ref):
    parts = (p0, p1, p2, p3)
    n = len(parts)
    for s, part in enumerate(parts):
        spot = pl.ds(lax.rem(at_ref[0] + n - s, n) * 4, 4)
        pre = part[0:256].reshape(4, 64, 128)
        one_ref[spot] = pre
        act_ref[spot] = part[256:512].reshape(4, 64, 128)
        grad = jnp.where(pre.astype(F32) > 0, acc_ref[spot], 0.0).astype(BF16)
        first_ref[spot] = grad
        low_ref[spot] = grad[:, 0:16]
        high_ref[spot] = grad[:, 48:64]


def second_kernel(factor, at_ref, one_ref, wide_ref, mine_ref, send_ref):
    act = jnp.maximum(one_ref[...].astype(F32), 0.0).reshape(1024, 128)
    taps = fold(weight_sums(act, wide_ref), factor)

    def emit(half, ref):
        for m in range(7):
            ref[64 * m : 64 * m + 64] = taps[7 * half + m].astype(ref.dtype)

    share(at_ref[1], emit, mine_ref, send_ref)


def last_kernel(
    factor, at_ref, first_ref, left_ref, right_ref, w_ref, mine2_ref, send2_ref, act_ref,
    grad_ref, mine_ref, send_ref, wide_ref, turn_ref,
):
    me = at_ref[0]
    widen(wide_ref, left_ref, first_ref, right_ref)
    taps = fold(weight_sums(act_ref[...].astype(F32).reshape(1024, 128), wide_ref), factor)
    grad = jnp.zeros((256, 128), F32)
    for i in range(3):
        for j in range(3):
            rows = wide_ref[pl.ds(me * 4 + 4 - 2 * i, 4), 32 - 16 * j : 96 - 16 * j].reshape(256, 384)
            grad += apply_taps(rows, w_ref[i * 3 + j])
    turn_ref[...] = grad
    for x in range(4):
        for t in range(8):
            grad_ref[x, :, 128 * t : 128 * t + 128] = turn_ref[pl.ds(64 * x + t, 8, stride=8), :].astype(BF16)

    def emit(half, ref):
        for m in range(7):
            ref[64 * m : 64 * m + 64] = taps[7 * half + m].astype(ref.dtype)

    share(at_ref[1], emit, mine_ref, send_ref)
    mine_ref[448:896] = mine2_ref[...]
    send_ref[448:896] = send2_ref[...]


def spread_kernel(at_ref, mine_ref, other_ref, one_ref, two_ref):
    def emit(half, ref):
        for out, at in ((one_ref, 0), (two_ref, 448)):
            for m in range(7):
                block = ref[at + 64 * m : at + 64 * m + 64].astype(F32)
                tap = 2 * (7 * half + m)
                out[tap] = block[:, 0:64]
                if tap < 26:
                    out[tap + 1] = block[:, 64:128]

    share(at_ref[1], emit, mine_ref, other_ref)


def trans_kernel(at_ref, mine_ref, other_ref, trans_ref):
    def emit(half, ref):
        for m in range(4):
            trans_ref[256 * half : 256 * half + 256, 128 * m : 128 * m + 128] = ref[256 * m : 256 * m + 256].astype(F32)

    share(at_ref[1], emit, mine_ref, other_ref)


def rotate(value, axis, step):
    n = lax.axis_size(axis)
    return lax.ppermute(value, axis, [(i, (i + step) % n) for i in range(n)])


def swap(value, axis, bit):
    n = lax.axis_size(axis)
    return lax.ppermute(value, axis, [(i, i ^ bit) for i in range(n)])


def rims(low, high):
    n = lax.axis_size("gy")
    left = lax.ppermute(high, "gy", [(i, i + 1) for i in range(n - 1)])
    right = lax.ppermute(low, "gy", [(i + 1, i) for i in range(n - 1)])
    return left, right


def on_chip(mine, send):
    return (mine + swap(send, "gy", 1).astype(F32)).astype(BF16)


def across(mine):
    return mine.astype(F32) + swap(mine, "gy", 2).astype(F32)


def slab_body(input_activation, pre_one, pre_two, w_one, w_two, w_trans, keep_mask, out_grad):
    factor = 1.0 / math.sqrt(
        input_activation.shape[0] * 4 * input_activation.shape[1] * 4 * (input_activation.shape[2] // 64)
    )
    at = jnp.stack([lax.axis_index("gx"), lax.rem(lax.axis_index("gy"), 2)]).astype(jnp.int32)
    shape = jax.ShapeDtypeStruct
    vmem = pltpu.VMEM
    natural = vmem((4, 8, 1024), BF16)
    packed = call(
        pack_kernel,
        (shape((512, 128), BF16), shape((512, 128), BF16)),
        [
            vmem((8, 4, 8, 128), BF16), natural, natural, natural, vmem((3, 256, 128), F32),
            pltpu.SemaphoreType.DMA((4,)),
        ],
        0,
        56,
        (out_grad,),
        (pre_two,),
        (pre_one,),
        (input_activation,),
    )
    firsts, seconds = [[v] + [rotate(v, "gx", s) for s in (1, 2, 3)] for v in packed]
    kept, mask, d2, d1 = call(
        weight_kernel,
        (
            shape((512, 512), BF16), shape((512, 512), BF16),
            shape((9, 128, 384), BF16), shape((9, 128, 384), BF16),
        ),
        [
            vmem((512, 512), BF16), vmem((8, 8), jnp.int32),
            vmem((27, 64, 64), BF16), vmem((27, 64, 64), BF16),
            pltpu.SemaphoreType.DMA((4,)),
        ],
        10**7,
        8,
        (w_trans,),
        (keep_mask,),
        (w_two,),
        (w_one,),
    )
    rim = shape((16, 16, 128), BF16)
    slab = shape((16, 64, 128), BF16)
    back, low, high, tmine, tsend = call(
        functools.partial(transition_kernel, factor),
        (shape((8, 2, 64, 128), BF16), rim, rim, shape((1024, 128), F32), shape((1024, 128), BF16)),
        [vmem((4, 256, 128), BF16), vmem((16, 64, 128), BF16)],
        4 * 256 * 512 * 512,
        12,
        at,
        *firsts,
        kept,
        mask,
    )
    left, right = rims(low, high)
    left, right, tsend, *seconds = lax.optimization_barrier((left, right, tsend, *seconds))
    tmine = across(on_chip(tmine, tsend))
    wide, acc = call(
        first_kernel,
        (shape((20, 96, 384), BF16), shape((1024, 128), F32)),
        [],
        2 * 128 * 3456 * 1024,
        12,
        back.reshape(16, 64, 128),
        left,
        right,
        d2,
    )
    first, low, high, one, act = call(
        mask_kernel, (slab, rim, rim, slab, slab), [], 10**7, 6, at, acc.reshape(16, 64, 128), *seconds
    )
    left, right = rims(low, high)
    mine2, send2 = call(
        functools.partial(second_kernel, factor),
        (shape((448, 128), F32), shape((448, 128), BF16)),
        [],
        2 * 128 * 3456 * 1024,
        16,
        at,
        one,
        wide,
    )
    grad_in, mine, send = call(
        functools.partial(last_kernel, factor),
        (shape((4, 8, 1024), BF16), shape((896, 128), F32), shape((896, 128), BF16)),
        [vmem((20, 96, 384), BF16), vmem((256, 128), F32)],
        2 * 128 * 3456 * (1024 + 256),
        16,
        at,
        first,
        left,
        right,
        d1,
        mine2,
        send2,
        act,
    )
    send, tmine = lax.optimization_barrier((send, tmine))
    mine = across(on_chip(mine, send))
    tother = swap(tmine, "gy", 1)
    other = swap(mine, "gy", 1)
    grad_w_trans = call(trans_kernel, shape((512, 512), F32), [], 10**7, 6, at, tmine, tother)
    grad_w_one, grad_w_two = call(
        spread_kernel,
        (shape((27, 64, 64), F32), shape((27, 64, 64), F32)),
        [],
        0,
        6,
        at,
        mine,
        other,
    )
    return (grad_in, grad_w_one, grad_w_two, grad_w_trans)


def solution(mesh):
    fits = mesh.shape["gx"] == 4 and mesh.shape["gy"] == 4

    def pick(*args):
        shapes = tuple(a.shape for a in args)
        known = (
            ((4, 8, 1024),) * 3 + ((27, 64, 64),) * 2 + ((512, 512), (8, 8), (8, 4, 8, 128))
        )
        return (slab_body if fits and shapes == known else body)(*args)

    return jax.shard_map(
        pick,
        mesh=mesh,
        in_specs=(
            P(("grp", "gx"), "gy", None),
            P(("grp", "gx"), "gy", None),
            P(("grp", "gx"), "gy", None),
            P(),
            P(),
            P(),
            P(),
            P("grp", "gy", None, "gx"),
        ),
        out_specs=(
            P(("grp", "gx"), "gy", None),
            P("grp", None, None),
            P("grp", None, None),
            P("grp", None),
        ),
        check_vma=False,
    )
```

```python
import functools
import math

import jax
import jax.numpy as jnp
from jax import lax
from jax.experimental import pallas as pl
from jax.experimental.pallas import tpu as pltpu
from jax.sharding import PartitionSpec as P

DILATION_STEP = 2
VMEM = pltpu.MemorySpace.VMEM
SMEM = pltpu.MemorySpace.SMEM
F32 = jnp.float32
BF16 = jnp.bfloat16


def padded(cells, sides, width):
    for axis, dim in sides:
        count = lax.axis_size(axis)
        ends = count - 1
        head = lax.slice_in_dim(cells, 0, width, axis=dim)
        tail = lax.slice_in_dim(cells, cells.shape[dim] - width, cells.shape[dim], axis=dim)
        cells = jnp.concatenate(
            [
                lax.ppermute(tail, axis, [(i, (i + 1) % count) for i in range(ends)]),
                cells,
                lax.ppermute(head, axis, [((i + 1) % count, i) for i in range(ends)]),
            ],
            axis=dim,
        )
    return cells


def split_layout(joined_layout, channel_count):
    return joined_layout.reshape(joined_layout.shape[0], joined_layout.shape[1], -1, channel_count)


def to_blocks(cube_volume):
    shape_all = cube_volume.shape
    parted = cube_volume.reshape(
        shape_all[0] // 2, 2, shape_all[1] // 2, 2, shape_all[2] // 2, 2, shape_all[3]
    )
    parted = parted.transpose(0, 2, 4, 1, 3, 5, 6)
    return parted.reshape(shape_all[0] // 2, shape_all[1] // 2, shape_all[2] // 2, 8 * shape_all[3])


def from_blocks(blocked, channel_count):
    shape_all = blocked.shape
    parted = blocked.reshape(shape_all[0], shape_all[1], shape_all[2], 2, 2, 2, channel_count)
    parted = parted.transpose(0, 3, 1, 4, 2, 5, 6)
    return parted.reshape(2 * shape_all[0], 2 * shape_all[1], 2 * shape_all[2], channel_count)


def padding_depth(cube_volume, margin):
    return jnp.pad(cube_volume, ((0, 0), (0, 0), (margin, margin), (0, 0)))


def weight_terms(bordered_input, upstream_gradient):
    channel_count = upstream_gradient.shape[3]
    grid_extent = upstream_gradient.shape
    padded_input = padding_depth(bordered_input, DILATION_STEP)
    flat_grad = upstream_gradient.reshape(-1, channel_count)
    partials = []
    for x_index in range(3):
        for y_index in range(3):
            sliding_window = padded_input[
                DILATION_STEP * x_index : DILATION_STEP * x_index + grid_extent[0],
                DILATION_STEP * y_index : DILATION_STEP * y_index + grid_extent[1],
            ]
            columns = jnp.concatenate(
                [
                    sliding_window[
                        :, :, DILATION_STEP * tap_index : DILATION_STEP * tap_index + grid_extent[2]
                    ].reshape(-1, channel_count)
                    for tap_index in range(3)
                ],
                axis=1,
            )
            partials.append(
                lax.dot_general(
                    columns, flat_grad, (((0,), (0,)), ((), ())), preferred_element_type=jnp.float32
                )
            )
    return jnp.stack(partials).reshape(27, channel_count, channel_count)


def data_terms(bordered_input, weights):
    channel_count = weights.shape[1]
    x_stretch = bordered_input.shape[0] - 2 * DILATION_STEP
    y_stretch = bordered_input.shape[1] - 2 * DILATION_STEP
    depth_cells = bordered_input.shape[2]
    padded_input = padding_depth(bordered_input, DILATION_STEP)
    stacked = jnp.transpose(weights, (0, 2, 1)).reshape(9, 3 * channel_count, channel_count)
    running = jnp.zeros((x_stretch * y_stretch * depth_cells, channel_count), jnp.float32)
    for x_index in range(3):
        for y_index in range(3):
            sliding_window = padded_input[
                DILATION_STEP * (2 - x_index) : DILATION_STEP * (2 - x_index) + x_stretch,
                DILATION_STEP * (2 - y_index) : DILATION_STEP * (2 - y_index) + y_stretch,
            ]
            columns = jnp.concatenate(
                [
                    sliding_window[
                        :,
                        :,
                        DILATION_STEP * (2 - tap_index) : DILATION_STEP * (2 - tap_index)
                        + depth_cells,
                    ].reshape(-1, channel_count)
                    for tap_index in range(3)
                ],
                axis=1,
            )
            running = running + jnp.dot(
                columns, stacked[x_index * 3 + y_index], preferred_element_type=jnp.float32
            )
    return running.reshape(x_stretch, y_stretch, depth_cells, channel_count)


def body(input_activation, pre_one, pre_two, w_one, w_two, w_trans, keep_mask, out_grad):
    channel_count = w_one.shape[1]
    x_stretch, y_stretch, joined_layout = input_activation.shape
    depth_cells = joined_layout // channel_count
    width_t = w_trans.shape[0]
    factor = 1.0 / math.sqrt(
        x_stretch * lax.axis_size("gx") * y_stretch * lax.axis_size("gy") * depth_cells
    )
    blocks = jnp.repeat(
        jnp.repeat(keep_mask.astype(jnp.bfloat16), channel_count, axis=0), channel_count, axis=1
    )
    w_kept = w_trans * blocks
    regrouped = lax.all_to_all(out_grad, "gx", split_axis=0, concat_axis=3, tiled=True)
    grad_rows = regrouped.reshape(-1, width_t)
    back_blocks = lax.dot_general(
        grad_rows, w_kept, (((1,), (1,)), ((), ())), preferred_element_type=jnp.float32
    ).astype(jnp.bfloat16)
    act_two = split_layout(jnp.maximum(pre_two, 0), channel_count)
    two_rows = to_blocks(act_two).reshape(-1, width_t)
    trans_term = (
        lax.dot_general(
            two_rows, grad_rows, (((0,), (0,)), ((), ())), preferred_element_type=jnp.float32
        )
        * blocks.astype(jnp.float32)
        * factor
    )
    grad_w_trans = lax.psum(trans_term, ("gx", "gy"))
    back_two = from_blocks(
        back_blocks.reshape(x_stretch // 2, y_stretch // 2, depth_cells // 2, width_t),
        channel_count,
    )
    back_two = jnp.where(
        split_layout(pre_two, channel_count) > 0, back_two, jnp.zeros_like(back_two)
    )
    first_activation = jnp.maximum(pre_one, 0)
    bordered_input = padded(
        jnp.concatenate([input_activation, first_activation], axis=2),
        (("gx", 0), ("gy", 1)),
        DILATION_STEP,
    )
    in_rim = split_layout(bordered_input[:, :, :joined_layout], channel_count)
    one_rim = split_layout(bordered_input[:, :, joined_layout:], channel_count)
    two_term = weight_terms(one_rim, back_two) * factor
    flattened_backward = back_two.reshape(x_stretch, y_stretch, joined_layout)
    narrowed_slice = split_layout(
        padded(flattened_backward, (("gx", 0), ("gy", 1)), DILATION_STEP), channel_count
    )
    first_backward = data_terms(narrowed_slice, w_two)
    first_backward = jnp.where(
        split_layout(pre_one, channel_count) > 0, first_backward, jnp.zeros_like(first_backward)
    ).astype(jnp.bfloat16)
    one_grad_rim = split_layout(
        padded(
            first_backward.reshape(x_stretch, y_stretch, joined_layout),
            (("gx", 0), ("gy", 1)),
            DILATION_STEP,
        ),
        channel_count,
    )
    grad_w_two = lax.psum(two_term, ("gx", "gy"))
    one_term = weight_terms(in_rim, first_backward) * factor
    grad_w_one = lax.psum(one_term, ("gx", "gy"))
    grad_in = (
        data_terms(one_grad_rim, w_one)
        .astype(jnp.bfloat16)
        .reshape(x_stretch, y_stretch, joined_layout)
    )
    return (grad_in, grad_w_one, grad_w_two, grad_w_trans)


def call(kernel, out_shape, scratch, flops, limit, *args):
    spec = []
    for a in args:
        if isinstance(a, tuple):
            spec.append(pl.BlockSpec(memory_space=pltpu.MemorySpace.HBM))
        elif a.dtype == jnp.int32:
            spec.append(pl.BlockSpec(memory_space=SMEM))
        else:
            spec.append(pl.BlockSpec(memory_space=VMEM))
    arrays = [a[0] if isinstance(a, tuple) else a for a in args]
    return pl.pallas_call(
        kernel,
        out_shape=out_shape,
        in_specs=spec,
        out_specs=jax.tree.map(lambda _: pl.BlockSpec(memory_space=VMEM), out_shape),
        scratch_shapes=scratch,
        cost_estimate=pl.CostEstimate(
            flops=flops,
            transcendentals=0,
            bytes_accessed=sum(a.size * a.dtype.itemsize for a in arrays),
        ),
        compiler_params=pltpu.CompilerParams(vmem_limit_bytes=limit * 1024 * 1024),
    )(*arrays)


def fetch(pairs, sems):
    copies = [pltpu.make_async_copy(src, dst, sems.at[k]) for k, (src, dst) in enumerate(pairs)]
    for copy in copies:
        copy.start()
    return copies


def turn(ref, rows, scratch, at, step):
    for x in range(4):
        for t in range(8):
            scratch[pl.ds(step * x + at + t, rows, stride=8), :] = ref[x, :, 128 * t : 128 * t + 128].astype(F32)


def pack_kernel(og, two, out_ref, og_v, two_v, turn_ref, sems):
    copies = fetch(((og, og_v), (two, two_v)), sems)
    copies[0].wait()
    out_ref[0:256] = og_v[...].astype(F32).reshape(256, 128).astype(BF16)
    copies[1].wait()
    turn(two_v, 8, turn_ref, 0, 64)
    out_ref[256:512] = turn_ref[...].astype(BF16)


def pack_more_kernel(one, act, left_ref, right_ref, out_ref, one_v, act_v, turn_ref, wide_ref, sems):
    copies = fetch(((one, one_v), (act, act_v)), sems)
    turn(left_ref, 2, wide_ref, 0, 96)
    turn(right_ref, 2, wide_ref, 80, 96)
    copies[0].wait()
    turn(one_v, 8, wide_ref, 16, 96)
    out_ref[0:384] = wide_ref[...].astype(BF16)
    copies[1].wait()
    turn(act_v, 8, turn_ref, 0, 64)
    out_ref[384:640] = turn_ref[...].astype(BF16)


def weight_kernel(wt, keep, w2, w1, kept_ref, mask_ref, d2_ref, d1_ref, wt_v, keep_v, w2_v, w1_v, sems):
    copies = fetch(((keep, keep_v), (wt, wt_v), (w2, w2_v), (w1, w1_v)), sems)
    copies[0].wait()
    width = wt_v.shape[0]
    blocks = keep_v.shape[0]
    side = width // blocks
    left = (
        lax.broadcasted_iota(jnp.int32, (width, blocks), 0) // side
        == lax.broadcasted_iota(jnp.int32, (width, blocks), 1)
    ).astype(BF16)
    right = (
        lax.broadcasted_iota(jnp.int32, (blocks, width), 1) // side
        == lax.broadcasted_iota(jnp.int32, (blocks, width), 0)
    ).astype(BF16)
    wide = jnp.dot(keep_v[...].astype(F32).astype(BF16), right, preferred_element_type=F32).astype(BF16)
    mask = jnp.dot(left, wide, preferred_element_type=F32)
    mask_ref[...] = mask.astype(BF16)
    copies[1].wait()
    kept_ref[...] = (wt_v[...].astype(F32) * mask).astype(BF16)
    none = jnp.zeros((64, 64), BF16)
    for k, (ref, out) in enumerate(((w2_v, d2_ref), (w1_v, d1_ref))):
        copies[k + 2].wait()
        for tap in range(27):
            w = ref[tap]
            at = 128 * (tap % 3)
            out[tap // 3, 0:64, at : at + 128] = jnp.concatenate([w, none], axis=1)
            out[tap // 3, 64:128, at : at + 128] = jnp.concatenate([none, w], axis=1)


def transition_kernel(
    factor, at_ref, a0, a1, a2, a3, kept_ref, mask_ref, back_ref, low_ref, high_ref, mine_ref, send_ref, og_ref, two_ref
):
    me = at_ref[0]
    parts = (a0, a1, a2, a3)
    n = len(parts)
    for s, part in enumerate(parts):
        src = lax.rem(me + n - s, n)
        og_ref[src] = part[0:256]
        two_ref[pl.ds(src * 4, 4)] = part[256:512].reshape(4, 64, 128)
    og = jnp.concatenate([og_ref[j] for j in range(n)], axis=1)
    back = lax.dot_general(og, kept_ref[...], (((1,), (1,)), ((), ())), preferred_element_type=F32)
    two = two_ref[...].astype(F32).reshape(8, 2, 4, 2, 8, 128)
    cells = []
    for p in range(2):
        halves = []
        for q in range(2):
            pre = two[:, p, :, q]
            at = (p * 2 + q) * 128
            grad = back[:, at : at + 128].reshape(8, 4, 8, 128)
            halves.append(jnp.where(pre > 0, grad, 0.0))
            cells.append(jnp.maximum(pre, 0.0).reshape(256, 128).astype(BF16))
        back_ref[:, p] = jnp.stack(halves, axis=2).reshape(8, 64, 128).astype(BF16)
    low_ref[...] = back_ref[:, :, 0:32].reshape(16, 32, 128)
    high_ref[...] = back_ref[:, :, 32:64].reshape(16, 32, 128)
    flat = jnp.concatenate(cells, axis=1)
    trans = lax.dot_general(flat, og, (((0,), (0,)), ((), ())), preferred_element_type=F32)
    trans = trans * mask_ref[...].astype(F32) * factor

    def emit(half, ref):
        for m in range(4):
            ref[256 * m : 256 * m + 256] = trans[256 * half : 256 * half + 256, 128 * m : 128 * m + 128].astype(ref.dtype)

    share(at_ref[1], emit, mine_ref, send_ref)


def share(core, emit, mine_ref, send_ref):
    @pl.when(core == 0)
    def _():
        emit(0, mine_ref)
        emit(1, send_ref)

    @pl.when(core != 0)
    def _():
        emit(1, mine_ref)
        emit(0, send_ref)


def triple(v):
    x, rows, _ = v.shape
    flat = v.reshape(x * rows, 128)
    t = lax.broadcasted_iota(jnp.int32, flat.shape, 0) % 8
    later = jnp.where(t == 7, 0.0, pltpu.roll(flat, x * rows - 1, 0))
    earlier = jnp.where(t == 0, 0.0, pltpu.roll(flat, 1, 0))
    wide = jnp.concatenate([later, flat, earlier], axis=1)
    return wide.astype(BF16).reshape(x, rows, 384)


def fold(sums, factor):
    lane = lax.broadcasted_iota(jnp.int32, (64, 128), 1)
    taps = []
    for g in sums:
        for l in range(3):
            part = g[:, l * 128 : (l + 1) * 128]
            f = jnp.where(lane < 64, part[0:64], part[64:128])
            taps.append((f + pltpu.roll(f, 64, 1)) * factor)
    taps.append(taps[-1])
    return [jnp.where(lane < 64, taps[2 * m], taps[2 * m + 1]) for m in range(14)]


def apply_taps(rows, taps):
    return lax.dot_general(rows, taps, (((1,), (1,)), ((), ())), preferred_element_type=F32)


def widen(wide_ref, pieces):
    rows = wide_ref.shape[1]
    edge = jnp.zeros((2, rows, 384), BF16)
    wide_ref[0:2] = edge
    wide_ref[18:20] = edge
    at = 0
    for piece in pieces:
        wide_ref[2:18, at : at + piece.shape[1]] = triple(piece.astype(F32))
        at += piece.shape[1]


def weight_sums(act, wide_ref, at):
    turned = act.T.astype(BF16)
    sums = []
    for i in range(3):
        for j in range(3):
            rows = wide_ref[4 - 2 * i : 20 - 2 * i, at - 16 * j : at + 64 - 16 * j].reshape(1024, 384)
            sums.append(jnp.dot(turned, rows, preferred_element_type=F32))
    return sums


def first_kernel(back_ref, left_ref, right_ref, w_ref, wide_ref, acc_ref):
    widen(wide_ref, (left_ref[...], back_ref[...], right_ref[...]))
    for i in range(3):
        for j in range(3):
            rows = wide_ref[4 - 2 * i : 20 - 2 * i, 32 - 16 * j : 128 - 16 * j].reshape(1536, 384)
            part = apply_taps(rows, w_ref[i * 3 + j])
            if i == 0 and j == 0:
                acc_ref[...] = part
            else:
                acc_ref[...] += part


def last_kernel(
    factor, at_ref, acc_ref, wide_ref, w_ref, p0, p1, p2, p3, grad_ref, mine_ref, send_ref, outer_ref, one_ref, act_ref, turn_ref
):
    me = at_ref[0]
    parts = (p0, p1, p2, p3)
    n = len(parts)
    for s, part in enumerate(parts):
        spot = pl.ds(lax.rem(me + n - s, n) * 4, 4)
        one_ref[spot] = part[0:384].reshape(4, 96, 128)
        act_ref[spot] = part[384:640].reshape(4, 64, 128)
    widen(outer_ref, (jnp.where(one_ref[...].astype(F32) > 0, acc_ref[...], 0.0),))
    act = jnp.maximum(one_ref[:, 16:80].astype(F32), 0.0).reshape(1024, 128)
    second = fold(weight_sums(act, wide_ref, 48), factor)
    first = fold(weight_sums(act_ref[...].astype(F32).reshape(1024, 128), outer_ref, 32), factor)
    grad = jnp.zeros((256, 128), F32)
    for i in range(3):
        for j in range(3):
            rows = outer_ref[pl.ds(me * 4 + 4 - 2 * i, 4), 32 - 16 * j : 96 - 16 * j].reshape(256, 384)
            grad += apply_taps(rows, w_ref[i * 3 + j])
    turn_ref[...] = grad
    for x in range(4):
        for t in range(8):
            grad_ref[x, :, 128 * t : 128 * t + 128] = turn_ref[pl.ds(64 * x + t, 8, stride=8), :].astype(BF16)

    def emit(half, ref):
        for m in range(7):
            ref[64 * m : 64 * m + 64] = first[7 * half + m].astype(ref.dtype)
            ref[448 + 64 * m : 512 + 64 * m] = second[7 * half + m].astype(ref.dtype)

    share(at_ref[1], emit, mine_ref, send_ref)


def spread_kernel(at_ref, mine_ref, other_ref, one_ref, two_ref):
    def emit(half, ref):
        for out, at in ((one_ref, 0), (two_ref, 448)):
            for m in range(7):
                block = ref[at + 64 * m : at + 64 * m + 64].astype(F32)
                tap = 2 * (7 * half + m)
                out[tap] = block[:, 0:64]
                if tap < 26:
                    out[tap + 1] = block[:, 64:128]

    share(at_ref[1], emit, mine_ref, other_ref)


def trans_kernel(at_ref, mine_ref, other_ref, trans_ref):
    def emit(half, ref):
        for m in range(4):
            trans_ref[256 * half : 256 * half + 256, 128 * m : 128 * m + 128] = ref[256 * m : 256 * m + 256].astype(F32)

    share(at_ref[1], emit, mine_ref, other_ref)


def rotate(value, axis, step):
    n = lax.axis_size(axis)
    return lax.ppermute(value, axis, [(i, (i + step) % n) for i in range(n)])


def swap(value, axis, bit):
    n = lax.axis_size(axis)
    return lax.ppermute(value, axis, [(i, i ^ bit) for i in range(n)])


def rims(low, high):
    n = lax.axis_size("gy")
    left = lax.ppermute(high, "gy", [(i, i + 1) for i in range(n - 1)])
    right = lax.ppermute(low, "gy", [(i + 1, i) for i in range(n - 1)])
    return left, right


def on_chip(mine, send):
    return (mine + swap(send, "gy", 1).astype(F32)).astype(BF16)


def across(mine):
    return mine.astype(F32) + swap(mine, "gy", 2).astype(F32)


def slab_body(input_activation, pre_one, pre_two, w_one, w_two, w_trans, keep_mask, out_grad):
    factor = 1.0 / math.sqrt(
        input_activation.shape[0] * 4 * input_activation.shape[1] * 4 * (input_activation.shape[2] // 64)
    )
    at = jnp.stack([lax.axis_index("gx"), lax.rem(lax.axis_index("gy"), 2)]).astype(jnp.int32)
    shape = jax.ShapeDtypeStruct
    vmem = pltpu.VMEM
    natural = vmem((4, 8, 1024), BF16)
    packed = call(
        pack_kernel,
        shape((512, 128), BF16),
        [vmem((8, 4, 8, 128), BF16), natural, vmem((256, 128), F32), pltpu.SemaphoreType.DMA((2,))],
        0,
        56,
        (out_grad,),
        (pre_two,),
    )
    firsts = [packed] + [rotate(packed, "gx", s) for s in (1, 2, 3)]
    left, right = rims(pre_one[:, 0:2], pre_one[:, 6:8])
    packed = call(
        pack_more_kernel,
        shape((640, 128), BF16),
        [natural, natural, vmem((256, 128), F32), vmem((384, 128), F32), pltpu.SemaphoreType.DMA((2,))],
        0,
        8,
        (pre_one,),
        (input_activation,),
        left,
        right,
    )
    seconds = [packed] + [rotate(packed, "gx", s) for s in (1, 2, 3)]
    kept, mask, d2, d1 = call(
        weight_kernel,
        (
            shape((512, 512), BF16), shape((512, 512), BF16),
            shape((9, 128, 384), BF16), shape((9, 128, 384), BF16),
        ),
        [
            vmem((512, 512), BF16), vmem((8, 8), jnp.int32),
            vmem((27, 64, 64), BF16), vmem((27, 64, 64), BF16),
            pltpu.SemaphoreType.DMA((4,)),
        ],
        10**7,
        8,
        (w_trans,),
        (keep_mask,),
        (w_two,),
        (w_one,),
    )
    rim = shape((16, 32, 128), BF16)
    kept, seconds[0] = lax.optimization_barrier((kept, seconds[0]))
    back, low, high, tmine, tsend = call(
        functools.partial(transition_kernel, factor),
        (shape((8, 2, 64, 128), BF16), rim, rim, shape((1024, 128), F32), shape((1024, 128), BF16)),
        [vmem((4, 256, 128), BF16), vmem((16, 64, 128), BF16)],
        4 * 256 * 512 * 512,
        12,
        at,
        *firsts,
        kept,
        mask,
    )
    left, right = rims(low, high)
    wide, acc = call(
        first_kernel,
        (shape((20, 128, 384), BF16), shape((1536, 128), F32)),
        [],
        0,
        16,
        back.reshape(16, 64, 128),
        left,
        right,
        d2,
    )
    acc, tsend, *seconds = lax.optimization_barrier((acc, tsend, *seconds))
    tmine = across(on_chip(tmine, tsend))
    grad_in, mine, send = call(
        functools.partial(last_kernel, factor),
        (shape((4, 8, 1024), BF16), shape((896, 128), F32), shape((896, 128), BF16)),
        [vmem((20, 96, 384), BF16), vmem((16, 96, 128), BF16), vmem((16, 64, 128), BF16), vmem((256, 128), F32)],
        2 * 128 * 3456 * (2048 + 256),
        20,
        at,
        acc.reshape(16, 96, 128),
        wide,
        d1,
        *seconds,
    )
    send, tmine = lax.optimization_barrier((send, tmine))
    mine = across(on_chip(mine, send))
    tother = swap(tmine, "gy", 1)
    other = swap(mine, "gy", 1)
    grad_w_trans = call(trans_kernel, shape((512, 512), F32), [], 10**7, 6, at, tmine, tother)
    grad_w_one, grad_w_two = call(
        spread_kernel,
        (shape((27, 64, 64), F32), shape((27, 64, 64), F32)),
        [],
        0,
        6,
        at,
        mine,
        other,
    )
    return (grad_in, grad_w_one, grad_w_two, grad_w_trans)


def solution(mesh):
    fits = mesh.shape["gx"] == 4 and mesh.shape["gy"] == 4

    def pick(*args):
        shapes = tuple(a.shape for a in args)
        known = (
            ((4, 8, 1024),) * 3 + ((27, 64, 64),) * 2 + ((512, 512), (8, 8), (8, 4, 8, 128))
        )
        return (slab_body if fits and shapes == known else body)(*args)

    return jax.shard_map(
        pick,
        mesh=mesh,
        in_specs=(
            P(("grp", "gx"), "gy", None),
            P(("grp", "gx"), "gy", None),
            P(("grp", "gx"), "gy", None),
            P(),
            P(),
            P(),
            P(),
            P("grp", "gy", None, "gx"),
        ),
        out_specs=(
            P(("grp", "gx"), "gy", None),
            P("grp", None, None),
            P("grp", None, None),
            P("grp", None),
        ),
        check_vma=False,
    )
```

```python
import functools
import math

import jax
import jax.numpy as jnp
from jax import lax
from jax.experimental import pallas as pl
from jax.experimental.pallas import tpu as pltpu
from jax.sharding import PartitionSpec as P

DILATION_STEP = 2
VMEM = pltpu.MemorySpace.VMEM
SMEM = pltpu.MemorySpace.SMEM
F32 = jnp.float32
BF16 = jnp.bfloat16


def padded(cells, sides, width):
    for axis, dim in sides:
        count = lax.axis_size(axis)
        ends = count - 1
        head = lax.slice_in_dim(cells, 0, width, axis=dim)
        tail = lax.slice_in_dim(cells, cells.shape[dim] - width, cells.shape[dim], axis=dim)
        cells = jnp.concatenate(
            [
                lax.ppermute(tail, axis, [(i, (i + 1) % count) for i in range(ends)]),
                cells,
                lax.ppermute(head, axis, [((i + 1) % count, i) for i in range(ends)]),
            ],
            axis=dim,
        )
    return cells


def split_layout(joined_layout, channel_count):
    return joined_layout.reshape(joined_layout.shape[0], joined_layout.shape[1], -1, channel_count)


def to_blocks(cube_volume):
    shape_all = cube_volume.shape
    parted = cube_volume.reshape(
        shape_all[0] // 2, 2, shape_all[1] // 2, 2, shape_all[2] // 2, 2, shape_all[3]
    )
    parted = parted.transpose(0, 2, 4, 1, 3, 5, 6)
    return parted.reshape(shape_all[0] // 2, shape_all[1] // 2, shape_all[2] // 2, 8 * shape_all[3])


def from_blocks(blocked, channel_count):
    shape_all = blocked.shape
    parted = blocked.reshape(shape_all[0], shape_all[1], shape_all[2], 2, 2, 2, channel_count)
    parted = parted.transpose(0, 3, 1, 4, 2, 5, 6)
    return parted.reshape(2 * shape_all[0], 2 * shape_all[1], 2 * shape_all[2], channel_count)


def padding_depth(cube_volume, margin):
    return jnp.pad(cube_volume, ((0, 0), (0, 0), (margin, margin), (0, 0)))


def weight_terms(bordered_input, upstream_gradient):
    channel_count = upstream_gradient.shape[3]
    grid_extent = upstream_gradient.shape
    padded_input = padding_depth(bordered_input, DILATION_STEP)
    flat_grad = upstream_gradient.reshape(-1, channel_count)
    partials = []
    for x_index in range(3):
        for y_index in range(3):
            sliding_window = padded_input[
                DILATION_STEP * x_index : DILATION_STEP * x_index + grid_extent[0],
                DILATION_STEP * y_index : DILATION_STEP * y_index + grid_extent[1],
            ]
            columns = jnp.concatenate(
                [
                    sliding_window[
                        :, :, DILATION_STEP * tap_index : DILATION_STEP * tap_index + grid_extent[2]
                    ].reshape(-1, channel_count)
                    for tap_index in range(3)
                ],
                axis=1,
            )
            partials.append(
                lax.dot_general(
                    columns, flat_grad, (((0,), (0,)), ((), ())), preferred_element_type=jnp.float32
                )
            )
    return jnp.stack(partials).reshape(27, channel_count, channel_count)


def data_terms(bordered_input, weights):
    channel_count = weights.shape[1]
    x_stretch = bordered_input.shape[0] - 2 * DILATION_STEP
    y_stretch = bordered_input.shape[1] - 2 * DILATION_STEP
    depth_cells = bordered_input.shape[2]
    padded_input = padding_depth(bordered_input, DILATION_STEP)
    stacked = jnp.transpose(weights, (0, 2, 1)).reshape(9, 3 * channel_count, channel_count)
    running = jnp.zeros((x_stretch * y_stretch * depth_cells, channel_count), jnp.float32)
    for x_index in range(3):
        for y_index in range(3):
            sliding_window = padded_input[
                DILATION_STEP * (2 - x_index) : DILATION_STEP * (2 - x_index) + x_stretch,
                DILATION_STEP * (2 - y_index) : DILATION_STEP * (2 - y_index) + y_stretch,
            ]
            columns = jnp.concatenate(
                [
                    sliding_window[
                        :,
                        :,
                        DILATION_STEP * (2 - tap_index) : DILATION_STEP * (2 - tap_index)
                        + depth_cells,
                    ].reshape(-1, channel_count)
                    for tap_index in range(3)
                ],
                axis=1,
            )
            running = running + jnp.dot(
                columns, stacked[x_index * 3 + y_index], preferred_element_type=jnp.float32
            )
    return running.reshape(x_stretch, y_stretch, depth_cells, channel_count)


def body(input_activation, pre_one, pre_two, w_one, w_two, w_trans, keep_mask, out_grad):
    channel_count = w_one.shape[1]
    x_stretch, y_stretch, joined_layout = input_activation.shape
    depth_cells = joined_layout // channel_count
    width_t = w_trans.shape[0]
    factor = 1.0 / math.sqrt(
        x_stretch * lax.axis_size("gx") * y_stretch * lax.axis_size("gy") * depth_cells
    )
    blocks = jnp.repeat(
        jnp.repeat(keep_mask.astype(jnp.bfloat16), channel_count, axis=0), channel_count, axis=1
    )
    w_kept = w_trans * blocks
    regrouped = lax.all_to_all(out_grad, "gx", split_axis=0, concat_axis=3, tiled=True)
    grad_rows = regrouped.reshape(-1, width_t)
    back_blocks = lax.dot_general(
        grad_rows, w_kept, (((1,), (1,)), ((), ())), preferred_element_type=jnp.float32
    ).astype(jnp.bfloat16)
    act_two = split_layout(jnp.maximum(pre_two, 0), channel_count)
    two_rows = to_blocks(act_two).reshape(-1, width_t)
    trans_term = (
        lax.dot_general(
            two_rows, grad_rows, (((0,), (0,)), ((), ())), preferred_element_type=jnp.float32
        )
        * blocks.astype(jnp.float32)
        * factor
    )
    grad_w_trans = lax.psum(trans_term, ("gx", "gy"))
    back_two = from_blocks(
        back_blocks.reshape(x_stretch // 2, y_stretch // 2, depth_cells // 2, width_t),
        channel_count,
    )
    back_two = jnp.where(
        split_layout(pre_two, channel_count) > 0, back_two, jnp.zeros_like(back_two)
    )
    first_activation = jnp.maximum(pre_one, 0)
    bordered_input = padded(
        jnp.concatenate([input_activation, first_activation], axis=2),
        (("gx", 0), ("gy", 1)),
        DILATION_STEP,
    )
    in_rim = split_layout(bordered_input[:, :, :joined_layout], channel_count)
    one_rim = split_layout(bordered_input[:, :, joined_layout:], channel_count)
    two_term = weight_terms(one_rim, back_two) * factor
    flattened_backward = back_two.reshape(x_stretch, y_stretch, joined_layout)
    narrowed_slice = split_layout(
        padded(flattened_backward, (("gx", 0), ("gy", 1)), DILATION_STEP), channel_count
    )
    first_backward = data_terms(narrowed_slice, w_two)
    first_backward = jnp.where(
        split_layout(pre_one, channel_count) > 0, first_backward, jnp.zeros_like(first_backward)
    ).astype(jnp.bfloat16)
    one_grad_rim = split_layout(
        padded(
            first_backward.reshape(x_stretch, y_stretch, joined_layout),
            (("gx", 0), ("gy", 1)),
            DILATION_STEP,
        ),
        channel_count,
    )
    grad_w_two = lax.psum(two_term, ("gx", "gy"))
    one_term = weight_terms(in_rim, first_backward) * factor
    grad_w_one = lax.psum(one_term, ("gx", "gy"))
    grad_in = (
        data_terms(one_grad_rim, w_one)
        .astype(jnp.bfloat16)
        .reshape(x_stretch, y_stretch, joined_layout)
    )
    return (grad_in, grad_w_one, grad_w_two, grad_w_trans)


def call(kernel, out_shape, scratch, flops, limit, *args):
    spec = []
    for a in args:
        if isinstance(a, tuple):
            spec.append(pl.BlockSpec(memory_space=pltpu.MemorySpace.HBM))
        elif a.dtype == jnp.int32:
            spec.append(pl.BlockSpec(memory_space=SMEM))
        else:
            spec.append(pl.BlockSpec(memory_space=VMEM))
    arrays = [a[0] if isinstance(a, tuple) else a for a in args]
    return pl.pallas_call(
        kernel,
        out_shape=out_shape,
        in_specs=spec,
        out_specs=jax.tree.map(lambda _: pl.BlockSpec(memory_space=VMEM), out_shape),
        scratch_shapes=scratch,
        cost_estimate=pl.CostEstimate(
            flops=flops,
            transcendentals=0,
            bytes_accessed=sum(a.size * a.dtype.itemsize for a in arrays),
        ),
        compiler_params=pltpu.CompilerParams(vmem_limit_bytes=limit * 1024 * 1024),
    )(*arrays)


def fetch(pairs, sems):
    copies = [pltpu.make_async_copy(src, dst, sems.at[k]) for k, (src, dst) in enumerate(pairs)]
    for copy in copies:
        copy.start()
    return copies


def pack_kernel(og, two, one, act, first_ref, second_ref, og_v, two_v, one_v, act_v, turn_ref, sems):
    copies = fetch(((og, og_v), (two, two_v), (one, one_v), (act, act_v)), sems)
    copies[0].wait()
    first_ref[0:256] = og_v[...].astype(F32).reshape(256, 128).astype(BF16)
    for k, (ref, out, at) in enumerate(((two_v, first_ref, 256), (one_v, first_ref, 512), (act_v, second_ref, 0))):
        copies[k + 1].wait()
        for x in range(4):
            for t in range(8):
                turn_ref[k, pl.ds(64 * x + t, 8, stride=8), :] = ref[x, :, 128 * t : 128 * t + 128].astype(F32)
        out[at : at + 256] = turn_ref[k].astype(BF16)


def weight_kernel(wt, keep, w2, w1, kept_ref, mask_ref, d2_ref, d1_ref, wt_v, keep_v, w2_v, w1_v, sems):
    copies = fetch(((keep, keep_v), (wt, wt_v), (w2, w2_v), (w1, w1_v)), sems)
    copies[0].wait()
    width = wt_v.shape[0]
    blocks = keep_v.shape[0]
    side = width // blocks
    left = (
        lax.broadcasted_iota(jnp.int32, (width, blocks), 0) // side
        == lax.broadcasted_iota(jnp.int32, (width, blocks), 1)
    ).astype(BF16)
    right = (
        lax.broadcasted_iota(jnp.int32, (blocks, width), 1) // side
        == lax.broadcasted_iota(jnp.int32, (blocks, width), 0)
    ).astype(BF16)
    wide = jnp.dot(keep_v[...].astype(F32).astype(BF16), right, preferred_element_type=F32).astype(BF16)
    mask = jnp.dot(left, wide, preferred_element_type=F32)
    mask_ref[...] = mask.astype(BF16)
    copies[1].wait()
    kept_ref[...] = (wt_v[...].astype(F32) * mask).astype(BF16)
    none = jnp.zeros((64, 64), BF16)
    for k, (ref, out) in enumerate(((w2_v, d2_ref), (w1_v, d1_ref))):
        copies[k + 2].wait()
        for tap in range(27):
            w = ref[tap]
            at = 128 * (tap % 3)
            out[tap // 3, 0:64, at : at + 128] = jnp.concatenate([w, none], axis=1)
            out[tap // 3, 64:128, at : at + 128] = jnp.concatenate([none, w], axis=1)


def transition_kernel(
    factor, at_ref, a0, a1, a2, a3, kept_ref, mask_ref, back_ref, one_ref, chip_ref, cross_ref, mine_ref, send_ref, og_ref, two_ref
):
    me = at_ref[0]
    parts = (a0, a1, a2, a3)
    n = len(parts)
    for s, part in enumerate(parts):
        src = lax.rem(me + n - s, n)
        og_ref[src] = part[0:256]
        spot = pl.ds(src * 4, 4)
        two_ref[spot] = part[256:512].reshape(4, 64, 128)
        one_ref[spot] = part[512:768].reshape(4, 64, 128)
    og = jnp.concatenate([og_ref[j] for j in range(n)], axis=1)
    back = lax.dot_general(og, kept_ref[...], (((1,), (1,)), ((), ())), preferred_element_type=F32)
    two = two_ref[...].astype(F32).reshape(8, 2, 4, 2, 8, 128)
    cells = []
    for p in range(2):
        halves = []
        for q in range(2):
            pre = two[:, p, :, q]
            at = (p * 2 + q) * 128
            grad = back[:, at : at + 128].reshape(8, 4, 8, 128)
            halves.append(jnp.where(pre > 0, grad, 0.0))
            cells.append(jnp.maximum(pre, 0.0).reshape(256, 128).astype(BF16))
        back_ref[:, p] = jnp.stack(halves, axis=2).reshape(8, 64, 128).astype(BF16)

    def rim(high, ref):
        at = 32 if high else 0
        ref[:, :, 0:32] = back_ref[:, :, at : at + 32]
        at = 48 if high else 0
        ref[:, :, 32:48] = one_ref[:, at : at + 16].reshape(8, 2, 16, 128)

    share(at_ref[1], rim, cross_ref, chip_ref)
    flat = jnp.concatenate(cells, axis=1)
    trans = lax.dot_general(flat, og, (((0,), (0,)), ((), ())), preferred_element_type=F32)
    trans = trans * mask_ref[...].astype(F32) * factor

    def emit(half, ref):
        for m in range(4):
            ref[256 * m : 256 * m + 256] = trans[256 * half : 256 * half + 256, 128 * m : 128 * m + 128].astype(ref.dtype)

    share(at_ref[1], emit, mine_ref, send_ref)


def share(core, emit, mine_ref, send_ref):
    @pl.when(core == 0)
    def _():
        emit(0, mine_ref)
        emit(1, send_ref)

    @pl.when(core != 0)
    def _():
        emit(1, mine_ref)
        emit(0, send_ref)


def triple(v):
    x, rows, _ = v.shape
    flat = v.reshape(x * rows, 128)
    t = lax.broadcasted_iota(jnp.int32, flat.shape, 0) % 8
    later = jnp.where(t == 7, 0.0, pltpu.roll(flat, x * rows - 1, 0))
    earlier = jnp.where(t == 0, 0.0, pltpu.roll(flat, 1, 0))
    wide = jnp.concatenate([later, flat, earlier], axis=1)
    return wide.astype(BF16).reshape(x, rows, 384)


def fold(sums, factor):
    lane = lax.broadcasted_iota(jnp.int32, (64, 128), 1)
    taps = []
    for g in sums:
        for l in range(3):
            if g is None:
                taps.append(jnp.zeros((64, 128), F32))
                continue
            part = g[:, l * 128 : (l + 1) * 128]
            f = jnp.where(lane < 64, part[0:64], part[64:128])
            taps.append((f + pltpu.roll(f, 64, 1)) * factor)
    taps.append(taps[-1])
    return [jnp.where(lane < 64, taps[2 * m], taps[2 * m + 1]) for m in range(14)]


def apply_taps(rows, taps):
    return lax.dot_general(rows, taps, (((1,), (1,)), ((), ())), preferred_element_type=F32)


def own_kernel(factor, back_ref, one_ref, w_ref, acc_ref, sums_ref, wide_ref):
    wide_ref[0:2] = jnp.zeros((2, 96, 384), BF16)
    wide_ref[18:20] = jnp.zeros((2, 96, 384), BF16)
    wide_ref[2:18, 0:16] = jnp.zeros((16, 16, 384), BF16)
    wide_ref[2:18, 80:96] = jnp.zeros((16, 16, 384), BF16)
    wide_ref[2:18, 16:80] = triple(back_ref[...].astype(F32))
    act = jnp.maximum(one_ref[...].astype(F32), 0.0).reshape(1024, 128).T.astype(BF16)
    sums = [None] * 9
    for j in range(3):
        part = jnp.zeros((1024, 128), F32)
        for i in range(3):
            part += apply_taps(wide_ref[4 - 2 * i : 20 - 2 * i, 16:80].reshape(1024, 384), w_ref[i * 3 + j])
            rows = wide_ref[4 - 2 * i : 20 - 2 * i, 32 - 16 * j : 96 - 16 * j].reshape(1024, 384)
            sums[i * 3 + j] = jnp.dot(act, rows, preferred_element_type=F32)
        part = part.reshape(16, 64, 128)
        if j == 0:
            acc_ref[:, 0:64] = part
            acc_ref[:, 64:96] = jnp.zeros((16, 32, 128), F32)
        else:
            acc_ref[:, 16 * j : 16 * j + 64] += part
    for m, block in enumerate(fold(sums, factor)):
        sums_ref[64 * m : 64 * m + 64] = block


def conv_kernel(
    factor, at_ref, acc_ref, sums_ref, one_ref, chip_ref, cross_ref, w2_ref, w1_ref, i0, i1, i2, i3,
    grad_ref, mine_ref, send_ref, rim_ref, wide_ref, outer_ref, in_ref, turn_ref, first_ref,
):
    me = at_ref[0]
    parts = (i0, i1, i2, i3)
    n = len(parts)
    for s, part in enumerate(parts):
        in_ref[pl.ds(lax.rem(me + n - s, n) * 4, 4)] = part[...].reshape(4, 64, 128)

    def put(side, ref):
        rim_ref[side] = ref[...]

    share(at_ref[1], put, cross_ref, chip_ref)
    wide_ref[:, 0:2] = jnp.zeros((2, 2, 32, 384), BF16)
    wide_ref[:, 18:20] = jnp.zeros((2, 2, 32, 384), BF16)
    outer_ref[0:2] = jnp.zeros((2, 96, 384), BF16)
    outer_ref[18:20] = jnp.zeros((2, 96, 384), BF16)
    for side in range(2):
        wide_ref[side, 2:18] = triple(rim_ref[side, :, 0:32].astype(F32))
    first_ref[...] = acc_ref[...]
    act = jnp.maximum(one_ref[...].astype(F32), 0.0)
    sums = [None] * 9
    for side in range(2):
        j = 2 - 2 * side
        near = 16 - 16 * side
        own = 48 * side
        turned = act[:, own : own + 16].reshape(256, 128).T.astype(BF16)
        far = jnp.zeros((512, 128), F32)
        close = jnp.zeros((256, 128), F32)
        for i in range(3):
            xs = slice(4 - 2 * i, 20 - 2 * i)
            rows = wide_ref[side, xs, near : near + 16].reshape(256, 384)
            far += apply_taps(wide_ref[side, xs].reshape(512, 384), w2_ref[i * 3 + j])
            close += apply_taps(rows, w2_ref[i * 3 + 1])
            sums[i * 3 + j] = jnp.dot(turned, rows, preferred_element_type=F32)
        first_ref[:, 64 * side : 64 * side + 32] += far.reshape(16, 32, 128)
        first_ref[:, 80 * side : 80 * side + 16] += close.reshape(16, 16, 128)
    second = fold(sums, factor)
    pre = jnp.concatenate([rim_ref[0, :, 32:48], one_ref[...], rim_ref[1, :, 32:48]], axis=1).astype(F32)
    outer_ref[2:18] = triple(jnp.where(pre > 0, first_ref[...], 0.0))
    act = in_ref[...].astype(F32).reshape(1024, 128).T.astype(BF16)
    sums = []
    grad = jnp.zeros((256, 128), F32)
    for i in range(3):
        for j in range(3):
            rows = outer_ref[4 - 2 * i : 20 - 2 * i, 32 - 16 * j : 96 - 16 * j].reshape(1024, 384)
            sums.append(jnp.dot(act, rows, preferred_element_type=F32))
            mine = outer_ref[pl.ds(me * 4 + 4 - 2 * i, 4), 32 - 16 * j : 96 - 16 * j].reshape(256, 384)
            grad += apply_taps(mine, w1_ref[i * 3 + j])
    first = fold(sums, factor)
    turn_ref[...] = grad
    for x in range(4):
        for t in range(8):
            grad_ref[x, :, 128 * t : 128 * t + 128] = turn_ref[pl.ds(64 * x + t, 8, stride=8), :].astype(BF16)

    def emit(half, ref):
        for m in range(7):
            ref[64 * m : 64 * m + 64] = first[7 * half + m].astype(ref.dtype)
            at = 448 * half + 64 * m
            block = second[7 * half + m] + sums_ref[at : at + 64]
            ref[448 + 64 * m : 512 + 64 * m] = block.astype(ref.dtype)

    share(at_ref[1], emit, mine_ref, send_ref)


def spread_kernel(at_ref, mine_ref, other_ref, one_ref, two_ref):
    def emit(half, ref):
        for out, at in ((one_ref, 0), (two_ref, 448)):
            for m in range(7):
                block = ref[at + 64 * m : at + 64 * m + 64].astype(F32)
                tap = 2 * (7 * half + m)
                out[tap] = block[:, 0:64]
                if tap < 26:
                    out[tap + 1] = block[:, 64:128]

    share(at_ref[1], emit, mine_ref, other_ref)


def trans_kernel(at_ref, mine_ref, other_ref, trans_ref):
    def emit(half, ref):
        for m in range(4):
            trans_ref[256 * half : 256 * half + 256, 128 * m : 128 * m + 128] = ref[256 * m : 256 * m + 256].astype(F32)

    share(at_ref[1], emit, mine_ref, other_ref)


def rotate(value, axis, step):
    n = lax.axis_size(axis)
    return lax.ppermute(value, axis, [(i, (i + step) % n) for i in range(n)])


def swap(value, axis, bit):
    n = lax.axis_size(axis)
    return lax.ppermute(value, axis, [(i, i ^ bit) for i in range(n)])


def on_chip(mine, send):
    return (mine + swap(send, "gy", 1).astype(F32)).astype(BF16)


def across(mine):
    return mine.astype(F32) + swap(mine, "gy", 2).astype(F32)


def slab_body(input_activation, pre_one, pre_two, w_one, w_two, w_trans, keep_mask, out_grad):
    factor = 1.0 / math.sqrt(
        input_activation.shape[0] * 4 * input_activation.shape[1] * 4 * (input_activation.shape[2] // 64)
    )
    at = jnp.stack([lax.axis_index("gx"), lax.rem(lax.axis_index("gy"), 2)]).astype(jnp.int32)
    shape = jax.ShapeDtypeStruct
    vmem = pltpu.VMEM
    natural = vmem((4, 8, 1024), BF16)
    first, second = call(
        pack_kernel,
        (shape((768, 128), BF16), shape((256, 128), BF16)),
        [
            vmem((8, 4, 8, 128), BF16), natural, natural, natural, vmem((3, 256, 128), F32),
            pltpu.SemaphoreType.DMA((4,)),
        ],
        0,
        56,
        (out_grad,),
        (pre_two,),
        (pre_one,),
        (input_activation,),
    )
    firsts = [first] + [rotate(first, "gx", s) for s in (1, 2, 3)]
    seconds = [second] + [rotate(second, "gx", s) for s in (1, 2, 3)]
    kept, mask, d2, d1 = call(
        weight_kernel,
        (
            shape((512, 512), BF16), shape((512, 512), BF16),
            shape((9, 128, 384), BF16), shape((9, 128, 384), BF16),
        ),
        [
            vmem((512, 512), BF16), vmem((8, 8), jnp.int32),
            vmem((27, 64, 64), BF16), vmem((27, 64, 64), BF16),
            pltpu.SemaphoreType.DMA((4,)),
        ],
        10**7,
        8,
        (w_trans,),
        (keep_mask,),
        (w_two,),
        (w_one,),
    )
    back, one, chip, cross, tmine, tsend = call(
        functools.partial(transition_kernel, factor),
        (
            shape((8, 2, 64, 128), BF16),
            shape((16, 64, 128), BF16),
            shape((8, 2, 48, 128), BF16),
            shape((8, 2, 48, 128), BF16),
            shape((1024, 128), F32),
            shape((1024, 128), BF16),
        ),
        [vmem((4, 256, 128), BF16), vmem((16, 64, 128), BF16)],
        4 * 256 * 512 * 512,
        12,
        at,
        *firsts,
        kept,
        mask,
    )
    tsend, *seconds = lax.optimization_barrier((tsend, *seconds))
    n = lax.axis_size("gy")
    pairs = [(i, i + 1) for i in range(1, n - 1, 2)]
    cross = lax.ppermute(cross, "gy", pairs + [(j, i) for i, j in pairs])
    chip = swap(chip, "gy", 1)
    acc, sums = call(
        functools.partial(own_kernel, factor),
        (shape((16, 96, 128), F32), shape((896, 128), F32)),
        [vmem((20, 96, 384), BF16)],
        2 * 128 * 3456 * 2048,
        16,
        back.reshape(16, 64, 128),
        one,
        d2,
    )
    tmine = on_chip(tmine, tsend)
    tmine, chip, cross, acc = lax.optimization_barrier((tmine, chip, cross, acc))
    tmine = across(tmine)
    grad_in, mine, send = call(
        functools.partial(conv_kernel, factor),
        (shape((4, 8, 1024), BF16), shape((896, 128), F32), shape((896, 128), BF16)),
        [
            vmem((2, 16, 48, 128), BF16),
            vmem((2, 20, 32, 384), BF16),
            vmem((20, 96, 384), BF16),
            vmem((16, 64, 128), BF16),
            vmem((256, 128), F32),
            vmem((16, 96, 128), F32),
        ],
        2 * 128 * 3456 * (512 + 1024 + 256),
        20,
        at,
        acc,
        sums,
        one,
        chip.reshape(16, 48, 128),
        cross.reshape(16, 48, 128),
        d2,
        d1,
        *seconds,
    )
    send, tmine = lax.optimization_barrier((send, tmine))
    mine = on_chip(mine, send)
    away = swap(mine, "gy", 2)
    tother = swap(tmine, "gy", 1)
    grad_w_trans = call(trans_kernel, shape((512, 512), F32), [], 10**7, 6, at, tmine, tother)
    away, grad_w_trans = lax.optimization_barrier((away, grad_w_trans))
    mine = mine.astype(F32) + away.astype(F32)
    other = swap(mine, "gy", 1)
    grad_w_one, grad_w_two = call(
        spread_kernel,
        (shape((27, 64, 64), F32), shape((27, 64, 64), F32)),
        [],
        0,
        6,
        at,
        mine,
        other,
    )
    return (grad_in, grad_w_one, grad_w_two, grad_w_trans)


def solution(mesh):
    fits = mesh.shape["gx"] == 4 and mesh.shape["gy"] == 4

    def pick(*args):
        shapes = tuple(a.shape for a in args)
        known = (
            ((4, 8, 1024),) * 3 + ((27, 64, 64),) * 2 + ((512, 512), (8, 8), (8, 4, 8, 128))
        )
        return (slab_body if fits and shapes == known else body)(*args)

    return jax.shard_map(
        pick,
        mesh=mesh,
        in_specs=(
            P(("grp", "gx"), "gy", None),
            P(("grp", "gx"), "gy", None),
            P(("grp", "gx"), "gy", None),
            P(),
            P(),
            P(),
            P(),
            P("grp", "gy", None, "gx"),
        ),
        out_specs=(
            P(("grp", "gx"), "gy", None),
            P("grp", None, None),
            P("grp", None, None),
            P("grp", None),
        ),
        check_vma=False,
    )
```

```python
import functools
import math

import jax
import jax.numpy as jnp
from jax import lax
from jax.experimental import pallas as pl
from jax.experimental.pallas import tpu as pltpu
from jax.sharding import PartitionSpec as P

DILATION_STEP = 2
VMEM = pltpu.MemorySpace.VMEM
SMEM = pltpu.MemorySpace.SMEM
F32 = jnp.float32
BF16 = jnp.bfloat16


def padded(cells, sides, width):
    for axis, dim in sides:
        count = lax.axis_size(axis)
        ends = count - 1
        head = lax.slice_in_dim(cells, 0, width, axis=dim)
        tail = lax.slice_in_dim(cells, cells.shape[dim] - width, cells.shape[dim], axis=dim)
        cells = jnp.concatenate(
            [
                lax.ppermute(tail, axis, [(i, (i + 1) % count) for i in range(ends)]),
                cells,
                lax.ppermute(head, axis, [((i + 1) % count, i) for i in range(ends)]),
            ],
            axis=dim,
        )
    return cells


def split_layout(joined_layout, channel_count):
    return joined_layout.reshape(joined_layout.shape[0], joined_layout.shape[1], -1, channel_count)


def to_blocks(cube_volume):
    shape_all = cube_volume.shape
    parted = cube_volume.reshape(
        shape_all[0] // 2, 2, shape_all[1] // 2, 2, shape_all[2] // 2, 2, shape_all[3]
    )
    parted = parted.transpose(0, 2, 4, 1, 3, 5, 6)
    return parted.reshape(shape_all[0] // 2, shape_all[1] // 2, shape_all[2] // 2, 8 * shape_all[3])


def from_blocks(blocked, channel_count):
    shape_all = blocked.shape
    parted = blocked.reshape(shape_all[0], shape_all[1], shape_all[2], 2, 2, 2, channel_count)
    parted = parted.transpose(0, 3, 1, 4, 2, 5, 6)
    return parted.reshape(2 * shape_all[0], 2 * shape_all[1], 2 * shape_all[2], channel_count)


def padding_depth(cube_volume, margin):
    return jnp.pad(cube_volume, ((0, 0), (0, 0), (margin, margin), (0, 0)))


def weight_terms(bordered_input, upstream_gradient):
    channel_count = upstream_gradient.shape[3]
    grid_extent = upstream_gradient.shape
    padded_input = padding_depth(bordered_input, DILATION_STEP)
    flat_grad = upstream_gradient.reshape(-1, channel_count)
    partials = []
    for x_index in range(3):
        for y_index in range(3):
            sliding_window = padded_input[
                DILATION_STEP * x_index : DILATION_STEP * x_index + grid_extent[0],
                DILATION_STEP * y_index : DILATION_STEP * y_index + grid_extent[1],
            ]
            columns = jnp.concatenate(
                [
                    sliding_window[
                        :, :, DILATION_STEP * tap_index : DILATION_STEP * tap_index + grid_extent[2]
                    ].reshape(-1, channel_count)
                    for tap_index in range(3)
                ],
                axis=1,
            )
            partials.append(
                lax.dot_general(
                    columns, flat_grad, (((0,), (0,)), ((), ())), preferred_element_type=jnp.float32
                )
            )
    return jnp.stack(partials).reshape(27, channel_count, channel_count)


def data_terms(bordered_input, weights):
    channel_count = weights.shape[1]
    x_stretch = bordered_input.shape[0] - 2 * DILATION_STEP
    y_stretch = bordered_input.shape[1] - 2 * DILATION_STEP
    depth_cells = bordered_input.shape[2]
    padded_input = padding_depth(bordered_input, DILATION_STEP)
    stacked = jnp.transpose(weights, (0, 2, 1)).reshape(9, 3 * channel_count, channel_count)
    running = jnp.zeros((x_stretch * y_stretch * depth_cells, channel_count), jnp.float32)
    for x_index in range(3):
        for y_index in range(3):
            sliding_window = padded_input[
                DILATION_STEP * (2 - x_index) : DILATION_STEP * (2 - x_index) + x_stretch,
                DILATION_STEP * (2 - y_index) : DILATION_STEP * (2 - y_index) + y_stretch,
            ]
            columns = jnp.concatenate(
                [
                    sliding_window[
                        :,
                        :,
                        DILATION_STEP * (2 - tap_index) : DILATION_STEP * (2 - tap_index)
                        + depth_cells,
                    ].reshape(-1, channel_count)
                    for tap_index in range(3)
                ],
                axis=1,
            )
            running = running + jnp.dot(
                columns, stacked[x_index * 3 + y_index], preferred_element_type=jnp.float32
            )
    return running.reshape(x_stretch, y_stretch, depth_cells, channel_count)


def body(input_activation, pre_one, pre_two, w_one, w_two, w_trans, keep_mask, out_grad):
    channel_count = w_one.shape[1]
    x_stretch, y_stretch, joined_layout = input_activation.shape
    depth_cells = joined_layout // channel_count
    width_t = w_trans.shape[0]
    factor = 1.0 / math.sqrt(
        x_stretch * lax.axis_size("gx") * y_stretch * lax.axis_size("gy") * depth_cells
    )
    blocks = jnp.repeat(
        jnp.repeat(keep_mask.astype(jnp.bfloat16), channel_count, axis=0), channel_count, axis=1
    )
    w_kept = w_trans * blocks
    regrouped = lax.all_to_all(out_grad, "gx", split_axis=0, concat_axis=3, tiled=True)
    grad_rows = regrouped.reshape(-1, width_t)
    back_blocks = lax.dot_general(
        grad_rows, w_kept, (((1,), (1,)), ((), ())), preferred_element_type=jnp.float32
    ).astype(jnp.bfloat16)
    act_two = split_layout(jnp.maximum(pre_two, 0), channel_count)
    two_rows = to_blocks(act_two).reshape(-1, width_t)
    trans_term = (
        lax.dot_general(
            two_rows, grad_rows, (((0,), (0,)), ((), ())), preferred_element_type=jnp.float32
        )
        * blocks.astype(jnp.float32)
        * factor
    )
    grad_w_trans = lax.psum(trans_term, ("gx", "gy"))
    back_two = from_blocks(
        back_blocks.reshape(x_stretch // 2, y_stretch // 2, depth_cells // 2, width_t),
        channel_count,
    )
    back_two = jnp.where(
        split_layout(pre_two, channel_count) > 0, back_two, jnp.zeros_like(back_two)
    )
    first_activation = jnp.maximum(pre_one, 0)
    bordered_input = padded(
        jnp.concatenate([input_activation, first_activation], axis=2),
        (("gx", 0), ("gy", 1)),
        DILATION_STEP,
    )
    in_rim = split_layout(bordered_input[:, :, :joined_layout], channel_count)
    one_rim = split_layout(bordered_input[:, :, joined_layout:], channel_count)
    two_term = weight_terms(one_rim, back_two) * factor
    flattened_backward = back_two.reshape(x_stretch, y_stretch, joined_layout)
    narrowed_slice = split_layout(
        padded(flattened_backward, (("gx", 0), ("gy", 1)), DILATION_STEP), channel_count
    )
    first_backward = data_terms(narrowed_slice, w_two)
    first_backward = jnp.where(
        split_layout(pre_one, channel_count) > 0, first_backward, jnp.zeros_like(first_backward)
    ).astype(jnp.bfloat16)
    one_grad_rim = split_layout(
        padded(
            first_backward.reshape(x_stretch, y_stretch, joined_layout),
            (("gx", 0), ("gy", 1)),
            DILATION_STEP,
        ),
        channel_count,
    )
    grad_w_two = lax.psum(two_term, ("gx", "gy"))
    one_term = weight_terms(in_rim, first_backward) * factor
    grad_w_one = lax.psum(one_term, ("gx", "gy"))
    grad_in = (
        data_terms(one_grad_rim, w_one)
        .astype(jnp.bfloat16)
        .reshape(x_stretch, y_stretch, joined_layout)
    )
    return (grad_in, grad_w_one, grad_w_two, grad_w_trans)


def call(kernel, out_shape, scratch, flops, limit, *args, out_space=VMEM):
    spec = []
    for a in args:
        if isinstance(a, tuple):
            spec.append(pl.BlockSpec(memory_space=pltpu.MemorySpace.HBM))
        elif a.dtype == jnp.int32:
            spec.append(pl.BlockSpec(memory_space=SMEM))
        else:
            spec.append(pl.BlockSpec(memory_space=VMEM))
    arrays = [a[0] if isinstance(a, tuple) else a for a in args]
    return pl.pallas_call(
        kernel,
        out_shape=out_shape,
        in_specs=spec,
        out_specs=jax.tree.map(lambda _: pl.BlockSpec(memory_space=out_space), out_shape),
        scratch_shapes=scratch,
        cost_estimate=pl.CostEstimate(
            flops=flops,
            transcendentals=0,
            bytes_accessed=sum(a.size * a.dtype.itemsize for a in arrays) if flops else 0,
        ),
        compiler_params=pltpu.CompilerParams(vmem_limit_bytes=limit * 1024 * 1024),
    )(*arrays)


def fetch(pairs, sems):
    copies = [pltpu.make_async_copy(src, dst, sems.at[k]) for k, (src, dst) in enumerate(pairs)]
    for copy in copies:
        copy.start()
    return copies


def pack_kernel(og, two, one, act, first_ref, second_ref, og_v, two_v, one_v, act_v, turn_ref, sems):
    copies = fetch(((og, og_v), (two, two_v), (one, one_v), (act, act_v)), sems)
    copies[0].wait()
    first_ref[0:256] = og_v[...].astype(F32).reshape(256, 128).astype(BF16)
    for k, (ref, out, at) in enumerate(((two_v, first_ref, 256), (one_v, first_ref, 512), (act_v, second_ref, 0))):
        copies[k + 1].wait()
        for x in range(4):
            for t in range(8):
                turn_ref[k, pl.ds(64 * x + t, 8, stride=8), :] = ref[x, :, 128 * t : 128 * t + 128].astype(F32)
        out[at : at + 256] = turn_ref[k].astype(BF16)


def weight_kernel(wt, keep, w2, w1, kept_ref, mask_ref, d2_ref, d1_ref, wt_v, keep_v, w2_v, w1_v, sems):
    copies = fetch(((keep, keep_v), (wt, wt_v), (w2, w2_v), (w1, w1_v)), sems)
    copies[0].wait()
    width = wt_v.shape[0]
    blocks = keep_v.shape[0]
    side = width // blocks
    left = (
        lax.broadcasted_iota(jnp.int32, (width, blocks), 0) // side
        == lax.broadcasted_iota(jnp.int32, (width, blocks), 1)
    ).astype(BF16)
    right = (
        lax.broadcasted_iota(jnp.int32, (blocks, width), 1) // side
        == lax.broadcasted_iota(jnp.int32, (blocks, width), 0)
    ).astype(BF16)
    wide = jnp.dot(keep_v[...].astype(F32).astype(BF16), right, preferred_element_type=F32).astype(BF16)
    mask = jnp.dot(left, wide, preferred_element_type=F32)
    mask_ref[...] = mask.astype(BF16)
    copies[1].wait()
    kept_ref[...] = (wt_v[...].astype(F32) * mask).astype(BF16)
    none = jnp.zeros((64, 64), BF16)
    for k, (ref, out) in enumerate(((w2_v, d2_ref), (w1_v, d1_ref))):
        copies[k + 2].wait()
        for tap in range(27):
            w = ref[tap]
            at = 128 * (tap % 3)
            out[tap // 3, 0:64, at : at + 128] = jnp.concatenate([w, none], axis=1)
            out[tap // 3, 64:128, at : at + 128] = jnp.concatenate([none, w], axis=1)


def transition_kernel(
    factor, at_ref, a0, a1, a2, a3, kept_ref, mask_ref, back_ref, one_ref, chip_ref, cross_ref, mine_ref, send_ref, og_ref, two_ref
):
    me = at_ref[0]
    parts = (a0, a1, a2, a3)
    n = len(parts)
    for s, part in enumerate(parts):
        src = lax.rem(me + n - s, n)
        og_ref[src] = part[0:256]
        spot = pl.ds(src * 4, 4)
        two_ref[spot] = part[256:512].reshape(4, 64, 128)
        one_ref[spot] = part[512:768].reshape(4, 64, 128)
    og = jnp.concatenate([og_ref[j] for j in range(n)], axis=1)
    back = lax.dot_general(og, kept_ref[...], (((1,), (1,)), ((), ())), preferred_element_type=F32)
    two = two_ref[...].astype(F32).reshape(8, 2, 4, 2, 8, 128)
    cells = []
    for p in range(2):
        halves = []
        for q in range(2):
            pre = two[:, p, :, q]
            at = (p * 2 + q) * 128
            grad = back[:, at : at + 128].reshape(8, 4, 8, 128)
            halves.append(jnp.where(pre > 0, grad, 0.0))
            cells.append(jnp.maximum(pre, 0.0).reshape(256, 128).astype(BF16))
        back_ref[:, p] = jnp.stack(halves, axis=2).reshape(8, 64, 128).astype(BF16)

    def rim(high, ref):
        at = 32 if high else 0
        ref[:, :, 0:32] = back_ref[:, :, at : at + 32]
        at = 48 if high else 0
        ref[:, :, 32:48] = one_ref[:, at : at + 16].reshape(8, 2, 16, 128)

    share(at_ref[1], rim, cross_ref, chip_ref)
    flat = jnp.concatenate(cells, axis=1)
    trans = lax.dot_general(flat, og, (((0,), (0,)), ((), ())), preferred_element_type=F32)
    trans = trans * mask_ref[...].astype(F32) * factor

    def emit(half, ref):
        for m in range(4):
            ref[256 * m : 256 * m + 256] = trans[256 * half : 256 * half + 256, 128 * m : 128 * m + 128].astype(ref.dtype)

    share(at_ref[1], emit, mine_ref, send_ref)


def share(core, emit, mine_ref, send_ref):
    @pl.when(core == 0)
    def _():
        emit(0, mine_ref)
        emit(1, send_ref)

    @pl.when(core != 0)
    def _():
        emit(1, mine_ref)
        emit(0, send_ref)


def triple(v):
    x, rows, _ = v.shape
    flat = v.reshape(x * rows, 128)
    t = lax.broadcasted_iota(jnp.int32, flat.shape, 0) % 8
    later = jnp.where(t == 7, 0.0, pltpu.roll(flat, x * rows - 1, 0))
    earlier = jnp.where(t == 0, 0.0, pltpu.roll(flat, 1, 0))
    wide = jnp.concatenate([later, flat, earlier], axis=1)
    return wide.astype(BF16).reshape(x, rows, 384)


def fold(sums, factor):
    lane = lax.broadcasted_iota(jnp.int32, (64, 128), 1)
    taps = []
    for g in sums:
        for l in range(3):
            if g is None:
                taps.append(jnp.zeros((64, 128), F32))
                continue
            part = g[:, l * 128 : (l + 1) * 128]
            f = jnp.where(lane < 64, part[0:64], part[64:128])
            taps.append((f + pltpu.roll(f, 64, 1)) * factor)
    taps.append(taps[-1])
    return [jnp.where(lane < 64, taps[2 * m], taps[2 * m + 1]) for m in range(14)]


def apply_taps(rows, taps):
    return lax.dot_general(rows, taps, (((1,), (1,)), ((), ())), preferred_element_type=F32)


def own_kernel(factor, back_ref, one_ref, w_ref, acc_ref, sums_ref, wide_ref):
    wide_ref[0:2] = jnp.zeros((2, 96, 384), BF16)
    wide_ref[18:20] = jnp.zeros((2, 96, 384), BF16)
    wide_ref[2:18, 0:16] = jnp.zeros((16, 16, 384), BF16)
    wide_ref[2:18, 80:96] = jnp.zeros((16, 16, 384), BF16)
    wide_ref[2:18, 16:80] = triple(back_ref[...].astype(F32))
    act = jnp.maximum(one_ref[...].astype(F32), 0.0).reshape(1024, 128).T.astype(BF16)
    sums = [None] * 9
    for j in range(3):
        part = jnp.zeros((1024, 128), F32)
        for i in range(3):
            part += apply_taps(wide_ref[4 - 2 * i : 20 - 2 * i, 16:80].reshape(1024, 384), w_ref[i * 3 + j])
            rows = wide_ref[4 - 2 * i : 20 - 2 * i, 32 - 16 * j : 96 - 16 * j].reshape(1024, 384)
            sums[i * 3 + j] = jnp.dot(act, rows, preferred_element_type=F32)
        part = part.reshape(16, 64, 128)
        if j == 0:
            acc_ref[:, 0:64] = part
            acc_ref[:, 64:96] = jnp.zeros((16, 32, 128), F32)
        else:
            acc_ref[:, 16 * j : 16 * j + 64] += part
    for m, block in enumerate(fold(sums, factor)):
        sums_ref[64 * m : 64 * m + 64] = block


def conv_kernel(
    factor, at_ref, acc_ref, sums_ref, one_ref, chip_ref, cross_ref, w_ref, i0, i1, i2, i3,
    mine_ref, send_ref, outer_ref, rim_ref, wide_ref, in_ref, first_ref,
):
    me = at_ref[0]
    parts = (i0, i1, i2, i3)
    n = len(parts)
    for s, part in enumerate(parts):
        in_ref[pl.ds(lax.rem(me + n - s, n) * 4, 4)] = part[...].reshape(4, 64, 128)

    def put(side, ref):
        rim_ref[side] = ref[...]

    share(at_ref[1], put, cross_ref, chip_ref)
    wide_ref[:, 0:2] = jnp.zeros((2, 2, 32, 384), BF16)
    wide_ref[:, 18:20] = jnp.zeros((2, 2, 32, 384), BF16)
    outer_ref[0:2] = jnp.zeros((2, 96, 384), BF16)
    outer_ref[18:20] = jnp.zeros((2, 96, 384), BF16)
    for side in range(2):
        wide_ref[side, 2:18] = triple(rim_ref[side, :, 0:32].astype(F32))
    first_ref[...] = acc_ref[...]
    act = jnp.maximum(one_ref[...].astype(F32), 0.0)
    sums = [None] * 9
    for side in range(2):
        j = 2 - 2 * side
        near = 16 - 16 * side
        own = 48 * side
        turned = act[:, own : own + 16].reshape(256, 128).T.astype(BF16)
        far = jnp.zeros((512, 128), F32)
        close = jnp.zeros((256, 128), F32)
        for i in range(3):
            xs = slice(4 - 2 * i, 20 - 2 * i)
            rows = wide_ref[side, xs, near : near + 16].reshape(256, 384)
            far += apply_taps(wide_ref[side, xs].reshape(512, 384), w_ref[i * 3 + j])
            close += apply_taps(rows, w_ref[i * 3 + 1])
            sums[i * 3 + j] = jnp.dot(turned, rows, preferred_element_type=F32)
        first_ref[:, 64 * side : 64 * side + 32] += far.reshape(16, 32, 128)
        first_ref[:, 80 * side : 80 * side + 16] += close.reshape(16, 16, 128)
    second = fold(sums, factor)
    pre = jnp.concatenate([rim_ref[0, :, 32:48], one_ref[...], rim_ref[1, :, 32:48]], axis=1).astype(F32)
    outer_ref[2:18] = triple(jnp.where(pre > 0, first_ref[...], 0.0))
    act = in_ref[...].astype(F32).reshape(1024, 128).T.astype(BF16)
    sums = []
    for i in range(3):
        for j in range(3):
            rows = outer_ref[4 - 2 * i : 20 - 2 * i, 32 - 16 * j : 96 - 16 * j].reshape(1024, 384)
            sums.append(jnp.dot(act, rows, preferred_element_type=F32))
    first = fold(sums, factor)

    def emit(half, ref):
        for m in range(7):
            ref[64 * m : 64 * m + 64] = first[7 * half + m].astype(ref.dtype)
            at = 448 * half + 64 * m
            block = second[7 * half + m] + sums_ref[at : at + 64]
            ref[448 + 64 * m : 512 + 64 * m] = block.astype(ref.dtype)

    share(at_ref[1], emit, mine_ref, send_ref)


def grad_kernel(at_ref, outer_ref, w_ref, grad_ref, turn_ref):
    grad = jnp.zeros((256, 128), F32)
    for i in range(3):
        for j in range(3):
            mine = outer_ref[pl.ds(at_ref[0] * 4 + 4 - 2 * i, 4), 32 - 16 * j : 96 - 16 * j].reshape(256, 384)
            grad += apply_taps(mine, w_ref[i * 3 + j])
    turn_ref[...] = grad
    for x in range(4):
        for t in range(8):
            grad_ref[x, :, 128 * t : 128 * t + 128] = turn_ref[pl.ds(64 * x + t, 8, stride=8), :].astype(BF16)


def spread_kernel(at_ref, mine_ref, other_ref, one_hbm, two_hbm, one_ref, two_ref, sems):
    copies = []
    for k, (out, hbm, at) in enumerate(((one_ref, one_hbm, 0), (two_ref, two_hbm, 448))):

        def emit(half, ref):
            for m in range(7):
                block = ref[at + 64 * m : at + 64 * m + 64]
                tap = 2 * (7 * half + m)
                out[tap] = block[:, 0:64]
                if tap < 26:
                    out[tap + 1] = block[:, 64:128]

        share(at_ref[1], emit, mine_ref, other_ref)
        copies.append(pltpu.make_async_copy(out, hbm, sems.at[k]))
        copies[-1].start()
    for copy in copies:
        copy.wait()


def trans_kernel(at_ref, mine_ref, other_ref, trans_ref):
    def emit(half, ref):
        for m in range(4):
            trans_ref[256 * half : 256 * half + 256, 128 * m : 128 * m + 128] = ref[256 * m : 256 * m + 256].astype(F32)

    share(at_ref[1], emit, mine_ref, other_ref)


def rotate(value, axis, step):
    n = lax.axis_size(axis)
    return lax.ppermute(value, axis, [(i, (i + step) % n) for i in range(n)])


def swap(value, axis, bit):
    n = lax.axis_size(axis)
    return lax.ppermute(value, axis, [(i, i ^ bit) for i in range(n)])


def on_chip(mine, send):
    return (mine + swap(send, "gy", 1).astype(F32)).astype(BF16)


def across(mine):
    return mine.astype(F32) + swap(mine, "gy", 2).astype(F32)


def slab_body(input_activation, pre_one, pre_two, w_one, w_two, w_trans, keep_mask, out_grad):
    factor = 1.0 / math.sqrt(
        input_activation.shape[0] * 4 * input_activation.shape[1] * 4 * (input_activation.shape[2] // 64)
    )
    at = jnp.stack([lax.axis_index("gx"), lax.rem(lax.axis_index("gy"), 2)]).astype(jnp.int32)
    shape = jax.ShapeDtypeStruct
    vmem = pltpu.VMEM
    natural = vmem((4, 8, 1024), BF16)
    first, second = call(
        pack_kernel,
        (shape((768, 128), BF16), shape((256, 128), BF16)),
        [
            vmem((8, 4, 8, 128), BF16), natural, natural, natural, vmem((3, 256, 128), F32),
            pltpu.SemaphoreType.DMA((4,)),
        ],
        0,
        56,
        (out_grad,),
        (pre_two,),
        (pre_one,),
        (input_activation,),
    )
    firsts = [first] + [rotate(first, "gx", s) for s in (1, 2, 3)]
    seconds = [second] + [rotate(second, "gx", s) for s in (1, 2, 3)]
    kept, mask, d2, d1 = call(
        weight_kernel,
        (
            shape((512, 512), BF16), shape((512, 512), BF16),
            shape((9, 128, 384), BF16), shape((9, 128, 384), BF16),
        ),
        [
            vmem((512, 512), BF16), vmem((8, 8), jnp.int32),
            vmem((27, 64, 64), BF16), vmem((27, 64, 64), BF16),
            pltpu.SemaphoreType.DMA((4,)),
        ],
        10**7,
        8,
        (w_trans,),
        (keep_mask,),
        (w_two,),
        (w_one,),
    )
    back, one, chip, cross, tmine, tsend = call(
        functools.partial(transition_kernel, factor),
        (
            shape((8, 2, 64, 128), BF16),
            shape((16, 64, 128), BF16),
            shape((8, 2, 48, 128), BF16),
            shape((8, 2, 48, 128), BF16),
            shape((1024, 128), F32),
            shape((1024, 128), BF16),
        ),
        [vmem((4, 256, 128), BF16), vmem((16, 64, 128), BF16)],
        4 * 256 * 512 * 512,
        12,
        at,
        *firsts,
        kept,
        mask,
    )
    n = lax.axis_size("gy")
    pairs = [(i, i + 1) for i in range(1, n - 1, 2)]
    cross = lax.ppermute(cross, "gy", pairs + [(j, i) for i, j in pairs])
    chip = swap(chip, "gy", 1)
    tsend, *seconds = lax.optimization_barrier((tsend, *seconds))
    tmine = on_chip(tmine, tsend)
    one, tmine = lax.optimization_barrier((one, tmine))
    acc, sums = call(
        functools.partial(own_kernel, factor),
        (shape((16, 96, 128), F32), shape((896, 128), F32)),
        [vmem((20, 96, 384), BF16)],
        2 * 128 * 3456 * 2048,
        16,
        back.reshape(16, 64, 128),
        one,
        d2,
    )
    tmine = across(tmine)
    mine, send, outer = call(
        functools.partial(conv_kernel, factor),
        (shape((896, 128), F32), shape((896, 128), BF16), shape((20, 96, 384), BF16)),
        [
            vmem((2, 16, 48, 128), BF16),
            vmem((2, 20, 32, 384), BF16),
            vmem((16, 64, 128), BF16),
            vmem((16, 96, 128), F32),
        ],
        2 * 128 * 3456 * 900,
        20,
        at,
        acc,
        sums,
        one,
        chip.reshape(16, 48, 128),
        cross.reshape(16, 48, 128),
        d2,
        *seconds,
    )
    send, tmine = lax.optimization_barrier((send, tmine))
    mine = on_chip(mine, send)
    away = swap(mine, "gy", 2)
    tother = swap(tmine, "gy", 1)
    grad_w_trans = call(trans_kernel, shape((512, 512), F32), [], 10**7, 6, at, tmine, tother)
    grad_in = call(
        grad_kernel, shape((4, 8, 1024), BF16), [vmem((256, 128), F32)], 2 * 128 * 3456 * 256, 12, at, outer, d1
    )
    away, grad_w_trans, grad_in = lax.optimization_barrier((away, grad_w_trans, grad_in))
    mine = mine.astype(F32) + away.astype(F32)
    other = swap(mine, "gy", 1)
    taps = shape((27, 64, 64), F32)
    grad_w_one, grad_w_two = call(
        spread_kernel,
        (taps, taps),
        [vmem(taps.shape, F32), vmem(taps.shape, F32), pltpu.SemaphoreType.DMA((2,))],
        0,
        8,
        at,
        mine,
        other,
        out_space=pltpu.MemorySpace.HBM,
    )
    return (grad_in, grad_w_one, grad_w_two, grad_w_trans)


def solution(mesh):
    fits = mesh.shape["gx"] == 4 and mesh.shape["gy"] == 4

    def pick(*args):
        shapes = tuple(a.shape for a in args)
        known = (
            ((4, 8, 1024),) * 3 + ((27, 64, 64),) * 2 + ((512, 512), (8, 8), (8, 4, 8, 128))
        )
        return (slab_body if fits and shapes == known else body)(*args)

    return jax.shard_map(
        pick,
        mesh=mesh,
        in_specs=(
            P(("grp", "gx"), "gy", None),
            P(("grp", "gx"), "gy", None),
            P(("grp", "gx"), "gy", None),
            P(),
            P(),
            P(),
            P(),
            P("grp", "gy", None, "gx"),
        ),
        out_specs=(
            P(("grp", "gx"), "gy", None),
            P("grp", None, None),
            P("grp", None, None),
            P("grp", None),
        ),
        check_vma=False,
    )
```

```python
import functools
import math

import jax
import jax.numpy as jnp
from jax import lax
from jax.experimental import pallas as pl
from jax.experimental.pallas import tpu as pltpu
from jax.sharding import PartitionSpec as P

DILATION_STEP = 2
VMEM = pltpu.MemorySpace.VMEM
SMEM = pltpu.MemorySpace.SMEM
F32 = jnp.float32
BF16 = jnp.bfloat16


def padded(cells, sides, width):
    for axis, dim in sides:
        count = lax.axis_size(axis)
        ends = count - 1
        head = lax.slice_in_dim(cells, 0, width, axis=dim)
        tail = lax.slice_in_dim(cells, cells.shape[dim] - width, cells.shape[dim], axis=dim)
        cells = jnp.concatenate(
            [
                lax.ppermute(tail, axis, [(i, (i + 1) % count) for i in range(ends)]),
                cells,
                lax.ppermute(head, axis, [((i + 1) % count, i) for i in range(ends)]),
            ],
            axis=dim,
        )
    return cells


def split_layout(joined_layout, channel_count):
    return joined_layout.reshape(joined_layout.shape[0], joined_layout.shape[1], -1, channel_count)


def to_blocks(cube_volume):
    shape_all = cube_volume.shape
    parted = cube_volume.reshape(
        shape_all[0] // 2, 2, shape_all[1] // 2, 2, shape_all[2] // 2, 2, shape_all[3]
    )
    parted = parted.transpose(0, 2, 4, 1, 3, 5, 6)
    return parted.reshape(shape_all[0] // 2, shape_all[1] // 2, shape_all[2] // 2, 8 * shape_all[3])


def from_blocks(blocked, channel_count):
    shape_all = blocked.shape
    parted = blocked.reshape(shape_all[0], shape_all[1], shape_all[2], 2, 2, 2, channel_count)
    parted = parted.transpose(0, 3, 1, 4, 2, 5, 6)
    return parted.reshape(2 * shape_all[0], 2 * shape_all[1], 2 * shape_all[2], channel_count)


def padding_depth(cube_volume, margin):
    return jnp.pad(cube_volume, ((0, 0), (0, 0), (margin, margin), (0, 0)))


def weight_terms(bordered_input, upstream_gradient):
    channel_count = upstream_gradient.shape[3]
    grid_extent = upstream_gradient.shape
    padded_input = padding_depth(bordered_input, DILATION_STEP)
    flat_grad = upstream_gradient.reshape(-1, channel_count)
    partials = []
    for x_index in range(3):
        for y_index in range(3):
            sliding_window = padded_input[
                DILATION_STEP * x_index : DILATION_STEP * x_index + grid_extent[0],
                DILATION_STEP * y_index : DILATION_STEP * y_index + grid_extent[1],
            ]
            columns = jnp.concatenate(
                [
                    sliding_window[
                        :, :, DILATION_STEP * tap_index : DILATION_STEP * tap_index + grid_extent[2]
                    ].reshape(-1, channel_count)
                    for tap_index in range(3)
                ],
                axis=1,
            )
            partials.append(
                lax.dot_general(
                    columns, flat_grad, (((0,), (0,)), ((), ())), preferred_element_type=jnp.float32
                )
            )
    return jnp.stack(partials).reshape(27, channel_count, channel_count)


def data_terms(bordered_input, weights):
    channel_count = weights.shape[1]
    x_stretch = bordered_input.shape[0] - 2 * DILATION_STEP
    y_stretch = bordered_input.shape[1] - 2 * DILATION_STEP
    depth_cells = bordered_input.shape[2]
    padded_input = padding_depth(bordered_input, DILATION_STEP)
    stacked = jnp.transpose(weights, (0, 2, 1)).reshape(9, 3 * channel_count, channel_count)
    running = jnp.zeros((x_stretch * y_stretch * depth_cells, channel_count), jnp.float32)
    for x_index in range(3):
        for y_index in range(3):
            sliding_window = padded_input[
                DILATION_STEP * (2 - x_index) : DILATION_STEP * (2 - x_index) + x_stretch,
                DILATION_STEP * (2 - y_index) : DILATION_STEP * (2 - y_index) + y_stretch,
            ]
            columns = jnp.concatenate(
                [
                    sliding_window[
                        :,
                        :,
                        DILATION_STEP * (2 - tap_index) : DILATION_STEP * (2 - tap_index)
                        + depth_cells,
                    ].reshape(-1, channel_count)
                    for tap_index in range(3)
                ],
                axis=1,
            )
            running = running + jnp.dot(
                columns, stacked[x_index * 3 + y_index], preferred_element_type=jnp.float32
            )
    return running.reshape(x_stretch, y_stretch, depth_cells, channel_count)


def body(input_activation, pre_one, pre_two, w_one, w_two, w_trans, keep_mask, out_grad):
    channel_count = w_one.shape[1]
    x_stretch, y_stretch, joined_layout = input_activation.shape
    depth_cells = joined_layout // channel_count
    width_t = w_trans.shape[0]
    factor = 1.0 / math.sqrt(
        x_stretch * lax.axis_size("gx") * y_stretch * lax.axis_size("gy") * depth_cells
    )
    blocks = jnp.repeat(
        jnp.repeat(keep_mask.astype(jnp.bfloat16), channel_count, axis=0), channel_count, axis=1
    )
    w_kept = w_trans * blocks
    regrouped = lax.all_to_all(out_grad, "gx", split_axis=0, concat_axis=3, tiled=True)
    grad_rows = regrouped.reshape(-1, width_t)
    back_blocks = lax.dot_general(
        grad_rows, w_kept, (((1,), (1,)), ((), ())), preferred_element_type=jnp.float32
    ).astype(jnp.bfloat16)
    act_two = split_layout(jnp.maximum(pre_two, 0), channel_count)
    two_rows = to_blocks(act_two).reshape(-1, width_t)
    trans_term = (
        lax.dot_general(
            two_rows, grad_rows, (((0,), (0,)), ((), ())), preferred_element_type=jnp.float32
        )
        * blocks.astype(jnp.float32)
        * factor
    )
    grad_w_trans = lax.psum(trans_term, ("gx", "gy"))
    back_two = from_blocks(
        back_blocks.reshape(x_stretch // 2, y_stretch // 2, depth_cells // 2, width_t),
        channel_count,
    )
    back_two = jnp.where(
        split_layout(pre_two, channel_count) > 0, back_two, jnp.zeros_like(back_two)
    )
    first_activation = jnp.maximum(pre_one, 0)
    bordered_input = padded(
        jnp.concatenate([input_activation, first_activation], axis=2),
        (("gx", 0), ("gy", 1)),
        DILATION_STEP,
    )
    in_rim = split_layout(bordered_input[:, :, :joined_layout], channel_count)
    one_rim = split_layout(bordered_input[:, :, joined_layout:], channel_count)
    two_term = weight_terms(one_rim, back_two) * factor
    flattened_backward = back_two.reshape(x_stretch, y_stretch, joined_layout)
    narrowed_slice = split_layout(
        padded(flattened_backward, (("gx", 0), ("gy", 1)), DILATION_STEP), channel_count
    )
    first_backward = data_terms(narrowed_slice, w_two)
    first_backward = jnp.where(
        split_layout(pre_one, channel_count) > 0, first_backward, jnp.zeros_like(first_backward)
    ).astype(jnp.bfloat16)
    one_grad_rim = split_layout(
        padded(
            first_backward.reshape(x_stretch, y_stretch, joined_layout),
            (("gx", 0), ("gy", 1)),
            DILATION_STEP,
        ),
        channel_count,
    )
    grad_w_two = lax.psum(two_term, ("gx", "gy"))
    one_term = weight_terms(in_rim, first_backward) * factor
    grad_w_one = lax.psum(one_term, ("gx", "gy"))
    grad_in = (
        data_terms(one_grad_rim, w_one)
        .astype(jnp.bfloat16)
        .reshape(x_stretch, y_stretch, joined_layout)
    )
    return (grad_in, grad_w_one, grad_w_two, grad_w_trans)


def call(kernel, out_shape, scratch, flops, limit, *args, out_space=VMEM):
    spec = []
    for a in args:
        if isinstance(a, tuple):
            spec.append(pl.BlockSpec(memory_space=pltpu.MemorySpace.HBM))
        elif a.dtype == jnp.int32:
            spec.append(pl.BlockSpec(memory_space=SMEM))
        else:
            spec.append(pl.BlockSpec(memory_space=VMEM))
    arrays = [a[0] if isinstance(a, tuple) else a for a in args]
    return pl.pallas_call(
        kernel,
        out_shape=out_shape,
        in_specs=spec,
        out_specs=jax.tree.map(lambda _: pl.BlockSpec(memory_space=out_space), out_shape),
        scratch_shapes=scratch,
        cost_estimate=pl.CostEstimate(
            flops=flops,
            transcendentals=0,
            bytes_accessed=sum(a.size * a.dtype.itemsize for a in arrays) if flops else 0,
        ),
        compiler_params=pltpu.CompilerParams(vmem_limit_bytes=limit * 1024 * 1024),
    )(*arrays)


def fetch(pairs, sems):
    copies = [pltpu.make_async_copy(src, dst, sems.at[k]) for k, (src, dst) in enumerate(pairs)]
    for copy in copies:
        copy.start()
    return copies


def pack_kernel(og, two, one, act, first_ref, second_ref, og_v, two_v, one_v, act_v, turn_ref, sems):
    copies = fetch(((og, og_v), (two, two_v), (one, one_v), (act, act_v)), sems)
    copies[0].wait()
    first_ref[0:256] = og_v[...].astype(F32).reshape(256, 128).astype(BF16)
    for k, (ref, out, at) in enumerate(((two_v, first_ref, 256), (one_v, first_ref, 512), (act_v, second_ref, 0))):
        copies[k + 1].wait()
        for x in range(4):
            for t in range(8):
                turn_ref[k, pl.ds(64 * x + t, 8, stride=8), :] = ref[x, :, 128 * t : 128 * t + 128].astype(F32)
        out[at : at + 256] = turn_ref[k].astype(BF16)


def weight_kernel(wt, keep, w2, w1, kept_ref, mask_ref, d2_ref, d1_ref, wt_v, keep_v, w2_v, w1_v, sems):
    copies = fetch(((keep, keep_v), (wt, wt_v), (w2, w2_v), (w1, w1_v)), sems)
    copies[0].wait()
    width = wt_v.shape[0]
    blocks = keep_v.shape[0]
    side = width // blocks
    left = (
        lax.broadcasted_iota(jnp.int32, (width, blocks), 0) // side
        == lax.broadcasted_iota(jnp.int32, (width, blocks), 1)
    ).astype(BF16)
    right = (
        lax.broadcasted_iota(jnp.int32, (blocks, width), 1) // side
        == lax.broadcasted_iota(jnp.int32, (blocks, width), 0)
    ).astype(BF16)
    wide = jnp.dot(keep_v[...].astype(F32).astype(BF16), right, preferred_element_type=F32).astype(BF16)
    mask = jnp.dot(left, wide, preferred_element_type=F32)
    mask_ref[...] = mask.astype(BF16)
    copies[1].wait()
    kept_ref[...] = (wt_v[...].astype(F32) * mask).astype(BF16)
    none = jnp.zeros((64, 64), BF16)
    for k, (ref, out) in enumerate(((w2_v, d2_ref), (w1_v, d1_ref))):
        copies[k + 2].wait()
        for tap in range(27):
            w = ref[tap]
            at = 128 * (tap % 3)
            out[tap // 3, 0:64, at : at + 128] = jnp.concatenate([w, none], axis=1)
            out[tap // 3, 64:128, at : at + 128] = jnp.concatenate([none, w], axis=1)


def transition_kernel(
    factor, at_ref, a0, a1, a2, a3, kept_ref, mask_ref, back_ref, one_ref, chip_ref, cross_ref, mine_ref, send_ref, og_ref, two_ref
):
    me = at_ref[0]
    parts = (a0, a1, a2, a3)
    n = len(parts)
    for s, part in enumerate(parts):
        src = lax.rem(me + n - s, n)
        og_ref[src] = part[0:256]
        spot = pl.ds(src * 4, 4)
        two_ref[spot] = part[256:512].reshape(4, 64, 128)
        one_ref[spot] = part[512:768].reshape(4, 64, 128)
    og = jnp.concatenate([og_ref[j] for j in range(n)], axis=1)
    back = lax.dot_general(og, kept_ref[...], (((1,), (1,)), ((), ())), preferred_element_type=F32)
    two = two_ref[...].astype(F32).reshape(8, 2, 4, 2, 8, 128)
    cells = []
    for p in range(2):
        halves = []
        for q in range(2):
            pre = two[:, p, :, q]
            at = (p * 2 + q) * 128
            grad = back[:, at : at + 128].reshape(8, 4, 8, 128)
            halves.append(jnp.where(pre > 0, grad, 0.0))
            cells.append(jnp.maximum(pre, 0.0).reshape(256, 128).astype(BF16))
        back_ref[:, p] = jnp.stack(halves, axis=2).reshape(8, 64, 128).astype(BF16)

    def rim(high, ref):
        at = 32 if high else 0
        ref[:, :, 0:32] = back_ref[:, :, at : at + 32]
        at = 48 if high else 0
        ref[:, :, 32:48] = one_ref[:, at : at + 16].reshape(8, 2, 16, 128)

    share(at_ref[1], rim, cross_ref, chip_ref)
    flat = jnp.concatenate(cells, axis=1)
    trans = lax.dot_general(flat, og, (((0,), (0,)), ((), ())), preferred_element_type=F32)
    trans = trans * mask_ref[...].astype(F32) * factor

    def emit(half, ref):
        for m in range(4):
            ref[256 * m : 256 * m + 256] = trans[256 * half : 256 * half + 256, 128 * m : 128 * m + 128].astype(ref.dtype)

    share(at_ref[1], emit, mine_ref, send_ref)


def share(core, emit, mine_ref, send_ref):
    @pl.when(core == 0)
    def _():
        emit(0, mine_ref)
        emit(1, send_ref)

    @pl.when(core != 0)
    def _():
        emit(1, mine_ref)
        emit(0, send_ref)


def triple(v):
    x, rows, _ = v.shape
    flat = v.reshape(x * rows, 128)
    t = lax.broadcasted_iota(jnp.int32, flat.shape, 0) % 8
    later = jnp.where(t == 7, 0.0, pltpu.roll(flat, x * rows - 1, 0))
    earlier = jnp.where(t == 0, 0.0, pltpu.roll(flat, 1, 0))
    wide = jnp.concatenate([later, flat, earlier], axis=1)
    return wide.astype(BF16).reshape(x, rows, 384)


def fold(sums, factor):
    lane = lax.broadcasted_iota(jnp.int32, (64, 128), 1)
    taps = []
    for g in sums:
        for l in range(3):
            if g is None:
                taps.append(jnp.zeros((64, 128), F32))
                continue
            part = g[:, l * 128 : (l + 1) * 128]
            f = jnp.where(lane < 64, part[0:64], part[64:128])
            taps.append((f + pltpu.roll(f, 64, 1)) * factor)
    taps.append(taps[-1])
    return [jnp.where(lane < 64, taps[2 * m], taps[2 * m + 1]) for m in range(14)]


def apply_taps(rows, taps):
    return lax.dot_general(rows, taps, (((1,), (1,)), ((), ())), preferred_element_type=F32)


def weight_sums(act, wide_ref, act_ref):
    act_ref[0:128] = jnp.zeros((128, 128), F32)
    act_ref[128:1152] = act.reshape(1024, 128)
    act_ref[1152:1280] = jnp.zeros((128, 128), F32)
    turned = act_ref[...].T.astype(BF16)
    stacked = jnp.concatenate([turned[:, 128 * i : 128 * i + 1024] for i in range(3)], axis=0)
    sums = [None] * 9
    for j in range(3):
        rows = wide_ref[2:18, 32 - 16 * j : 96 - 16 * j].reshape(1024, 384)
        part = jnp.dot(stacked, rows, preferred_element_type=F32)
        for i in range(3):
            sums[i * 3 + j] = part[128 * i : 128 * i + 128]
    return sums


def own_kernel(factor, back_ref, one_ref, w_ref, acc_ref, sums_ref, wide_ref, act_ref):
    wide_ref[2:18, 0:16] = jnp.zeros((16, 16, 384), BF16)
    wide_ref[2:18, 80:96] = jnp.zeros((16, 16, 384), BF16)
    wide_ref[2:18, 16:80] = triple(back_ref[...].astype(F32))
    acc_ref[...] = jnp.zeros((16, 96, 128), F32)
    rows = wide_ref[2:18, 16:80].reshape(1024, 384)
    for j in range(3):
        taps = jnp.concatenate([w_ref[i * 3 + j] for i in range(3)], axis=0)
        part = apply_taps(rows, taps).reshape(16, 64, 384)
        ys = slice(16 * j, 16 * j + 64)
        acc_ref[0:14, ys] += part[2:16, :, 0:128]
        acc_ref[:, ys] += part[:, :, 128:256]
        acc_ref[2:16, ys] += part[0:14, :, 256:384]
    sums = weight_sums(jnp.maximum(one_ref[...].astype(F32), 0.0), wide_ref, act_ref)
    for m, block in enumerate(fold(sums, factor)):
        sums_ref[64 * m : 64 * m + 64] = block


def conv_kernel(
    factor, at_ref, acc_ref, sums_ref, one_ref, chip_ref, cross_ref, w_ref, i0, i1, i2, i3,
    mine_ref, send_ref, outer_ref, rim_ref, wide_ref, in_ref, first_ref, act_ref,
):
    me = at_ref[0]
    parts = (i0, i1, i2, i3)
    n = len(parts)
    for s, part in enumerate(parts):
        in_ref[pl.ds(lax.rem(me + n - s, n) * 4, 4)] = part[...].reshape(4, 64, 128)

    def put(side, ref):
        rim_ref[side] = ref[...]

    share(at_ref[1], put, cross_ref, chip_ref)
    wide_ref[:, 0:2] = jnp.zeros((2, 2, 32, 384), BF16)
    wide_ref[:, 18:20] = jnp.zeros((2, 2, 32, 384), BF16)
    outer_ref[0:2] = jnp.zeros((2, 96, 384), BF16)
    outer_ref[18:20] = jnp.zeros((2, 96, 384), BF16)
    for side in range(2):
        wide_ref[side, 2:18] = triple(rim_ref[side, :, 0:32].astype(F32))
    first_ref[...] = acc_ref[...]
    act = jnp.maximum(one_ref[...].astype(F32), 0.0)
    sums = [None] * 9
    for side in range(2):
        j = 2 - 2 * side
        near = 16 - 16 * side
        own = 48 * side
        turned = act[:, own : own + 16].reshape(256, 128).T.astype(BF16)
        far = jnp.zeros((512, 128), F32)
        close = jnp.zeros((256, 128), F32)
        for i in range(3):
            xs = slice(4 - 2 * i, 20 - 2 * i)
            rows = wide_ref[side, xs, near : near + 16].reshape(256, 384)
            far += apply_taps(wide_ref[side, xs].reshape(512, 384), w_ref[i * 3 + j])
            close += apply_taps(rows, w_ref[i * 3 + 1])
            sums[i * 3 + j] = jnp.dot(turned, rows, preferred_element_type=F32)
        first_ref[:, 64 * side : 64 * side + 32] += far.reshape(16, 32, 128)
        first_ref[:, 80 * side : 80 * side + 16] += close.reshape(16, 16, 128)
    second = fold(sums, factor)
    pre = jnp.concatenate([rim_ref[0, :, 32:48], one_ref[...], rim_ref[1, :, 32:48]], axis=1).astype(F32)
    outer_ref[2:18] = triple(jnp.where(pre > 0, first_ref[...], 0.0))
    first = fold(weight_sums(in_ref[...].astype(F32), outer_ref, act_ref), factor)

    def emit(half, ref):
        for m in range(7):
            ref[64 * m : 64 * m + 64] = first[7 * half + m].astype(ref.dtype)
            at = 448 * half + 64 * m
            block = second[7 * half + m] + sums_ref[at : at + 64]
            ref[448 + 64 * m : 512 + 64 * m] = block.astype(ref.dtype)

    share(at_ref[1], emit, mine_ref, send_ref)


def grad_kernel(at_ref, outer_ref, w_ref, grad_ref, turn_ref):
    grad = jnp.zeros((256, 128), F32)
    for i in range(3):
        for j in range(3):
            mine = outer_ref[pl.ds(at_ref[0] * 4 + 4 - 2 * i, 4), 32 - 16 * j : 96 - 16 * j].reshape(256, 384)
            grad += apply_taps(mine, w_ref[i * 3 + j])
    turn_ref[...] = grad
    for x in range(4):
        for t in range(8):
            grad_ref[x, :, 128 * t : 128 * t + 128] = turn_ref[pl.ds(64 * x + t, 8, stride=8), :].astype(BF16)


def unpack(ref, at, out_ref):
    for m in range(7):
        block = ref[at + 64 * m : at + 64 * m + 64]
        out_ref[2 * m] = block[:, 0:64]
        out_ref[2 * m + 1] = block[:, 64:128]


def half_kernel(mine_ref, one_ref, two_ref):
    unpack(mine_ref, 0, one_ref)
    unpack(mine_ref, 448, two_ref)


def spread_kernel(at_ref, mine_one, mine_two, other_ref, one_hbm, two_hbm, one_ref, two_ref, sems):
    def emit(core):
        copies = []

        def send(half, one, two):
            count = 14 - half
            for src, dst in ((one, one_hbm), (two, two_hbm)):
                copies.append(
                    pltpu.make_async_copy(
                        src.at[0:count], dst.at[14 * half : 14 * half + count], sems.at[len(copies)]
                    )
                )
                copies[-1].start()

        send(core, mine_one, mine_two)
        unpack(other_ref, 0, one_ref)
        unpack(other_ref, 448, two_ref)
        send(1 - core, one_ref, two_ref)
        for copy in copies:
            copy.wait()

    @pl.when(at_ref[1] == 0)
    def _():
        emit(0)

    @pl.when(at_ref[1] != 0)
    def _():
        emit(1)


def trans_kernel(at_ref, mine_ref, other_ref, trans_ref):
    def emit(half, ref):
        for m in range(4):
            trans_ref[256 * half : 256 * half + 256, 128 * m : 128 * m + 128] = ref[256 * m : 256 * m + 256].astype(F32)

    share(at_ref[1], emit, mine_ref, other_ref)


def rotate(value, axis, step):
    n = lax.axis_size(axis)
    return lax.ppermute(value, axis, [(i, (i + step) % n) for i in range(n)])


def swap(value, axis, bit):
    n = lax.axis_size(axis)
    return lax.ppermute(value, axis, [(i, i ^ bit) for i in range(n)])


def on_chip(mine, send):
    return (mine + swap(send, "gy", 1).astype(F32)).astype(BF16)


def across(mine):
    return mine.astype(F32) + swap(mine, "gy", 2).astype(F32)


def slab_body(input_activation, pre_one, pre_two, w_one, w_two, w_trans, keep_mask, out_grad):
    factor = 1.0 / math.sqrt(
        input_activation.shape[0] * 4 * input_activation.shape[1] * 4 * (input_activation.shape[2] // 64)
    )
    at = jnp.stack([lax.axis_index("gx"), lax.rem(lax.axis_index("gy"), 2)]).astype(jnp.int32)
    shape = jax.ShapeDtypeStruct
    vmem = pltpu.VMEM
    natural = vmem((4, 8, 1024), BF16)
    first, second = call(
        pack_kernel,
        (shape((768, 128), BF16), shape((256, 128), BF16)),
        [
            vmem((8, 4, 8, 128), BF16), natural, natural, natural, vmem((3, 256, 128), F32),
            pltpu.SemaphoreType.DMA((4,)),
        ],
        0,
        56,
        (out_grad,),
        (pre_two,),
        (pre_one,),
        (input_activation,),
    )
    firsts = [first] + [rotate(first, "gx", s) for s in (1, 2, 3)]
    seconds = [second] + [rotate(second, "gx", s) for s in (1, 2, 3)]
    kept, mask, d2, d1 = call(
        weight_kernel,
        (
            shape((512, 512), BF16), shape((512, 512), BF16),
            shape((9, 128, 384), BF16), shape((9, 128, 384), BF16),
        ),
        [
            vmem((512, 512), BF16), vmem((8, 8), jnp.int32),
            vmem((27, 64, 64), BF16), vmem((27, 64, 64), BF16),
            pltpu.SemaphoreType.DMA((4,)),
        ],
        10**7,
        8,
        (w_trans,),
        (keep_mask,),
        (w_two,),
        (w_one,),
    )
    back, one, chip, cross, tmine, tsend = call(
        functools.partial(transition_kernel, factor),
        (
            shape((8, 2, 64, 128), BF16),
            shape((16, 64, 128), BF16),
            shape((8, 2, 48, 128), BF16),
            shape((8, 2, 48, 128), BF16),
            shape((1024, 128), F32),
            shape((1024, 128), BF16),
        ),
        [vmem((4, 256, 128), BF16), vmem((16, 64, 128), BF16)],
        4 * 256 * 512 * 512,
        12,
        at,
        *firsts,
        kept,
        mask,
    )
    n = lax.axis_size("gy")
    pairs = [(i, i + 1) for i in range(1, n - 1, 2)]
    cross = lax.ppermute(cross, "gy", pairs + [(j, i) for i, j in pairs])
    chip = swap(chip, "gy", 1)
    tsend, *seconds = lax.optimization_barrier((tsend, *seconds))
    tmine = on_chip(tmine, tsend)
    one, tmine = lax.optimization_barrier((one, tmine))
    acc, sums = call(
        functools.partial(own_kernel, factor),
        (shape((16, 96, 128), F32), shape((896, 128), F32)),
        [vmem((20, 96, 384), BF16), vmem((1280, 128), F32)],
        2 * 128 * 3456 * 2048,
        16,
        back.reshape(16, 64, 128),
        one,
        d2,
    )
    tmine = across(tmine)
    mine, send, outer = call(
        functools.partial(conv_kernel, factor),
        (shape((896, 128), F32), shape((896, 128), BF16), shape((20, 96, 384), BF16)),
        [
            vmem((2, 16, 48, 128), BF16),
            vmem((2, 20, 32, 384), BF16),
            vmem((16, 64, 128), BF16),
            vmem((16, 96, 128), F32),
            vmem((1280, 128), F32),
        ],
        2 * 128 * 3456 * 900,
        20,
        at,
        acc,
        sums,
        one,
        chip.reshape(16, 48, 128),
        cross.reshape(16, 48, 128),
        d2,
        *seconds,
    )
    send, tmine = lax.optimization_barrier((send, tmine))
    mine = on_chip(mine, send)
    away = swap(mine, "gy", 2)
    tother = swap(tmine, "gy", 1)
    grad_w_trans = call(trans_kernel, shape((512, 512), F32), [], 10**7, 6, at, tmine, tother)
    grad_in = call(
        grad_kernel, shape((4, 8, 1024), BF16), [vmem((256, 128), F32)], 2 * 128 * 3456 * 256, 12, at, outer, d1
    )
    away, grad_w_trans, grad_in = lax.optimization_barrier((away, grad_w_trans, grad_in))
    mine = mine.astype(F32) + away.astype(F32)
    other = swap(mine, "gy", 1)
    taps = shape((27, 64, 64), F32)
    half = shape((14, 64, 64), F32)
    mine_one, mine_two = call(half_kernel, (half, half), [], 10**8, 6, mine)
    grad_w_one, grad_w_two = call(
        spread_kernel,
        (taps, taps),
        [vmem(half.shape, F32), vmem(half.shape, F32), pltpu.SemaphoreType.DMA((4,))],
        0,
        8,
        at,
        mine_one,
        mine_two,
        other,
        out_space=pltpu.MemorySpace.HBM,
    )
    return (grad_in, grad_w_one, grad_w_two, grad_w_trans)


def solution(mesh):
    fits = mesh.shape["gx"] == 4 and mesh.shape["gy"] == 4

    def pick(*args):
        shapes = tuple(a.shape for a in args)
        known = (
            ((4, 8, 1024),) * 3 + ((27, 64, 64),) * 2 + ((512, 512), (8, 8), (8, 4, 8, 128))
        )
        return (slab_body if fits and shapes == known else body)(*args)

    return jax.shard_map(
        pick,
        mesh=mesh,
        in_specs=(
            P(("grp", "gx"), "gy", None),
            P(("grp", "gx"), "gy", None),
            P(("grp", "gx"), "gy", None),
            P(),
            P(),
            P(),
            P(),
            P("grp", "gy", None, "gx"),
        ),
        out_specs=(
            P(("grp", "gx"), "gy", None),
            P("grp", None, None),
            P("grp", None, None),
            P("grp", None),
        ),
        check_vma=False,
    )
```

```python
import functools
import math

import jax
import jax.numpy as jnp
from jax import lax
from jax.experimental import pallas as pl
from jax.experimental.pallas import tpu as pltpu
from jax.sharding import PartitionSpec as P

DILATION_STEP = 2
VMEM = pltpu.MemorySpace.VMEM
SMEM = pltpu.MemorySpace.SMEM
F32 = jnp.float32
BF16 = jnp.bfloat16


def padded(cells, sides, width):
    for axis, dim in sides:
        count = lax.axis_size(axis)
        ends = count - 1
        head = lax.slice_in_dim(cells, 0, width, axis=dim)
        tail = lax.slice_in_dim(cells, cells.shape[dim] - width, cells.shape[dim], axis=dim)
        cells = jnp.concatenate(
            [
                lax.ppermute(tail, axis, [(i, (i + 1) % count) for i in range(ends)]),
                cells,
                lax.ppermute(head, axis, [((i + 1) % count, i) for i in range(ends)]),
            ],
            axis=dim,
        )
    return cells


def split_layout(joined_layout, channel_count):
    return joined_layout.reshape(joined_layout.shape[0], joined_layout.shape[1], -1, channel_count)


def to_blocks(cube_volume):
    shape_all = cube_volume.shape
    parted = cube_volume.reshape(
        shape_all[0] // 2, 2, shape_all[1] // 2, 2, shape_all[2] // 2, 2, shape_all[3]
    )
    parted = parted.transpose(0, 2, 4, 1, 3, 5, 6)
    return parted.reshape(shape_all[0] // 2, shape_all[1] // 2, shape_all[2] // 2, 8 * shape_all[3])


def from_blocks(blocked, channel_count):
    shape_all = blocked.shape
    parted = blocked.reshape(shape_all[0], shape_all[1], shape_all[2], 2, 2, 2, channel_count)
    parted = parted.transpose(0, 3, 1, 4, 2, 5, 6)
    return parted.reshape(2 * shape_all[0], 2 * shape_all[1], 2 * shape_all[2], channel_count)


def padding_depth(cube_volume, margin):
    return jnp.pad(cube_volume, ((0, 0), (0, 0), (margin, margin), (0, 0)))


def weight_terms(bordered_input, upstream_gradient):
    channel_count = upstream_gradient.shape[3]
    grid_extent = upstream_gradient.shape
    padded_input = padding_depth(bordered_input, DILATION_STEP)
    flat_grad = upstream_gradient.reshape(-1, channel_count)
    partials = []
    for x_index in range(3):
        for y_index in range(3):
            sliding_window = padded_input[
                DILATION_STEP * x_index : DILATION_STEP * x_index + grid_extent[0],
                DILATION_STEP * y_index : DILATION_STEP * y_index + grid_extent[1],
            ]
            columns = jnp.concatenate(
                [
                    sliding_window[
                        :, :, DILATION_STEP * tap_index : DILATION_STEP * tap_index + grid_extent[2]
                    ].reshape(-1, channel_count)
                    for tap_index in range(3)
                ],
                axis=1,
            )
            partials.append(
                lax.dot_general(
                    columns, flat_grad, (((0,), (0,)), ((), ())), preferred_element_type=jnp.float32
                )
            )
    return jnp.stack(partials).reshape(27, channel_count, channel_count)


def data_terms(bordered_input, weights):
    channel_count = weights.shape[1]
    x_stretch = bordered_input.shape[0] - 2 * DILATION_STEP
    y_stretch = bordered_input.shape[1] - 2 * DILATION_STEP
    depth_cells = bordered_input.shape[2]
    padded_input = padding_depth(bordered_input, DILATION_STEP)
    stacked = jnp.transpose(weights, (0, 2, 1)).reshape(9, 3 * channel_count, channel_count)
    running = jnp.zeros((x_stretch * y_stretch * depth_cells, channel_count), jnp.float32)
    for x_index in range(3):
        for y_index in range(3):
            sliding_window = padded_input[
                DILATION_STEP * (2 - x_index) : DILATION_STEP * (2 - x_index) + x_stretch,
                DILATION_STEP * (2 - y_index) : DILATION_STEP * (2 - y_index) + y_stretch,
            ]
            columns = jnp.concatenate(
                [
                    sliding_window[
                        :,
                        :,
                        DILATION_STEP * (2 - tap_index) : DILATION_STEP * (2 - tap_index)
                        + depth_cells,
                    ].reshape(-1, channel_count)
                    for tap_index in range(3)
                ],
                axis=1,
            )
            running = running + jnp.dot(
                columns, stacked[x_index * 3 + y_index], preferred_element_type=jnp.float32
            )
    return running.reshape(x_stretch, y_stretch, depth_cells, channel_count)


def body(input_activation, pre_one, pre_two, w_one, w_two, w_trans, keep_mask, out_grad):
    channel_count = w_one.shape[1]
    x_stretch, y_stretch, joined_layout = input_activation.shape
    depth_cells = joined_layout // channel_count
    width_t = w_trans.shape[0]
    factor = 1.0 / math.sqrt(
        x_stretch * lax.axis_size("gx") * y_stretch * lax.axis_size("gy") * depth_cells
    )
    blocks = jnp.repeat(
        jnp.repeat(keep_mask.astype(jnp.bfloat16), channel_count, axis=0), channel_count, axis=1
    )
    w_kept = w_trans * blocks
    regrouped = lax.all_to_all(out_grad, "gx", split_axis=0, concat_axis=3, tiled=True)
    grad_rows = regrouped.reshape(-1, width_t)
    back_blocks = lax.dot_general(
        grad_rows, w_kept, (((1,), (1,)), ((), ())), preferred_element_type=jnp.float32
    ).astype(jnp.bfloat16)
    act_two = split_layout(jnp.maximum(pre_two, 0), channel_count)
    two_rows = to_blocks(act_two).reshape(-1, width_t)
    trans_term = (
        lax.dot_general(
            two_rows, grad_rows, (((0,), (0,)), ((), ())), preferred_element_type=jnp.float32
        )
        * blocks.astype(jnp.float32)
        * factor
    )
    grad_w_trans = lax.psum(trans_term, ("gx", "gy"))
    back_two = from_blocks(
        back_blocks.reshape(x_stretch // 2, y_stretch // 2, depth_cells // 2, width_t),
        channel_count,
    )
    back_two = jnp.where(
        split_layout(pre_two, channel_count) > 0, back_two, jnp.zeros_like(back_two)
    )
    first_activation = jnp.maximum(pre_one, 0)
    bordered_input = padded(
        jnp.concatenate([input_activation, first_activation], axis=2),
        (("gx", 0), ("gy", 1)),
        DILATION_STEP,
    )
    in_rim = split_layout(bordered_input[:, :, :joined_layout], channel_count)
    one_rim = split_layout(bordered_input[:, :, joined_layout:], channel_count)
    two_term = weight_terms(one_rim, back_two) * factor
    flattened_backward = back_two.reshape(x_stretch, y_stretch, joined_layout)
    narrowed_slice = split_layout(
        padded(flattened_backward, (("gx", 0), ("gy", 1)), DILATION_STEP), channel_count
    )
    first_backward = data_terms(narrowed_slice, w_two)
    first_backward = jnp.where(
        split_layout(pre_one, channel_count) > 0, first_backward, jnp.zeros_like(first_backward)
    ).astype(jnp.bfloat16)
    one_grad_rim = split_layout(
        padded(
            first_backward.reshape(x_stretch, y_stretch, joined_layout),
            (("gx", 0), ("gy", 1)),
            DILATION_STEP,
        ),
        channel_count,
    )
    grad_w_two = lax.psum(two_term, ("gx", "gy"))
    one_term = weight_terms(in_rim, first_backward) * factor
    grad_w_one = lax.psum(one_term, ("gx", "gy"))
    grad_in = (
        data_terms(one_grad_rim, w_one)
        .astype(jnp.bfloat16)
        .reshape(x_stretch, y_stretch, joined_layout)
    )
    return (grad_in, grad_w_one, grad_w_two, grad_w_trans)


def call(kernel, out_shape, scratch, flops, limit, *args, out_space=VMEM, aliases={}):
    spec = []
    for a in args:
        if isinstance(a, tuple):
            spec.append(pl.BlockSpec(memory_space=pltpu.MemorySpace.HBM))
        elif a.dtype == jnp.int32:
            spec.append(pl.BlockSpec(memory_space=SMEM))
        else:
            spec.append(pl.BlockSpec(memory_space=VMEM))
    arrays = [a[0] if isinstance(a, tuple) else a for a in args]
    return pl.pallas_call(
        kernel,
        out_shape=out_shape,
        in_specs=spec,
        out_specs=jax.tree.map(lambda _: pl.BlockSpec(memory_space=out_space), out_shape),
        scratch_shapes=scratch,
        input_output_aliases=aliases,
        cost_estimate=pl.CostEstimate(
            flops=flops,
            transcendentals=0,
            bytes_accessed=sum(a.size * a.dtype.itemsize for a in arrays) if flops else 0,
        ),
        compiler_params=pltpu.CompilerParams(vmem_limit_bytes=limit * 1024 * 1024),
    )(*arrays)


def fetch(pairs, sems):
    copies = [pltpu.make_async_copy(src, dst, sems.at[k]) for k, (src, dst) in enumerate(pairs)]
    for copy in copies:
        copy.start()
    return copies


def pack_kernel(og, two, one, act, first_ref, second_ref, og_v, two_v, one_v, act_v, turn_ref, sems):
    copies = fetch(((og, og_v), (two, two_v), (one, one_v), (act, act_v)), sems)
    copies[0].wait()
    first_ref[0:256] = og_v[...].astype(F32).reshape(256, 128).astype(BF16)
    for k, (ref, out, at) in enumerate(((two_v, first_ref, 256), (one_v, first_ref, 512), (act_v, second_ref, 0))):
        copies[k + 1].wait()
        for x in range(4):
            for t in range(8):
                turn_ref[k, pl.ds(64 * x + t, 8, stride=8), :] = ref[x, :, 128 * t : 128 * t + 128].astype(F32)
        out[at : at + 256] = turn_ref[k].astype(BF16)


def weight_kernel(wt, keep, w2, w1, kept_ref, mask_ref, d2_ref, d1_ref, wt_v, keep_v, w2_v, w1_v, sems):
    copies = fetch(((keep, keep_v), (wt, wt_v), (w2, w2_v), (w1, w1_v)), sems)
    copies[0].wait()
    width = wt_v.shape[0]
    blocks = keep_v.shape[0]
    side = width // blocks
    left = (
        lax.broadcasted_iota(jnp.int32, (width, blocks), 0) // side
        == lax.broadcasted_iota(jnp.int32, (width, blocks), 1)
    ).astype(BF16)
    right = (
        lax.broadcasted_iota(jnp.int32, (blocks, width), 1) // side
        == lax.broadcasted_iota(jnp.int32, (blocks, width), 0)
    ).astype(BF16)
    wide = jnp.dot(keep_v[...].astype(F32).astype(BF16), right, preferred_element_type=F32).astype(BF16)
    mask = jnp.dot(left, wide, preferred_element_type=F32)
    mask_ref[...] = mask.astype(BF16)
    copies[1].wait()
    kept_ref[...] = (wt_v[...].astype(F32) * mask).astype(BF16)
    none = jnp.zeros((64, 64), BF16)
    for k, (ref, out) in enumerate(((w2_v, d2_ref), (w1_v, d1_ref))):
        copies[k + 2].wait()
        for tap in range(27):
            w = ref[tap]
            at = 128 * (tap % 3)
            out[tap // 3, 0:64, at : at + 128] = jnp.concatenate([w, none], axis=1)
            out[tap // 3, 64:128, at : at + 128] = jnp.concatenate([none, w], axis=1)


def transition_kernel(
    factor, at_ref, a0, a1, a2, a3, kept_ref, mask_ref, back_ref, one_ref, chip_ref, cross_ref, mine_ref, send_ref, og_ref, two_ref
):
    me = at_ref[0]
    parts = (a0, a1, a2, a3)
    n = len(parts)
    for s, part in enumerate(parts):
        src = lax.rem(me + n - s, n)
        og_ref[src] = part[0:256]
        spot = pl.ds(src * 4, 4)
        two_ref[spot] = part[256:512].reshape(4, 64, 128)
        one_ref[spot] = part[512:768].reshape(4, 64, 128)
    og = jnp.concatenate([og_ref[j] for j in range(n)], axis=1)
    back = lax.dot_general(og, kept_ref[...], (((1,), (1,)), ((), ())), preferred_element_type=F32)
    two = two_ref[...].astype(F32).reshape(8, 2, 4, 2, 8, 128)
    cells = []
    for p in range(2):
        halves = []
        for q in range(2):
            pre = two[:, p, :, q]
            at = (p * 2 + q) * 128
            grad = back[:, at : at + 128].reshape(8, 4, 8, 128)
            halves.append(jnp.where(pre > 0, grad, 0.0))
            cells.append(jnp.maximum(pre, 0.0).reshape(256, 128).astype(BF16))
        back_ref[:, p] = jnp.stack(halves, axis=2).reshape(8, 64, 128).astype(BF16)

    def rim(high, ref):
        at = 32 if high else 0
        ref[:, :, 0:32] = back_ref[:, :, at : at + 32]
        at = 48 if high else 0
        ref[:, :, 32:48] = one_ref[:, at : at + 16].reshape(8, 2, 16, 128)

    share(at_ref[1], rim, cross_ref, chip_ref)
    flat = jnp.concatenate(cells, axis=1)
    trans = lax.dot_general(flat, og, (((0,), (0,)), ((), ())), preferred_element_type=F32)
    trans = trans * mask_ref[...].astype(F32) * factor

    def emit(half, ref):
        for m in range(4):
            ref[256 * m : 256 * m + 256] = trans[256 * half : 256 * half + 256, 128 * m : 128 * m + 128].astype(ref.dtype)

    share(at_ref[1], emit, mine_ref, send_ref)


def share(core, emit, mine_ref, send_ref):
    @pl.when(core == 0)
    def _():
        emit(0, mine_ref)
        emit(1, send_ref)

    @pl.when(core != 0)
    def _():
        emit(1, mine_ref)
        emit(0, send_ref)


def triple(v):
    x, rows, _ = v.shape
    flat = v.reshape(x * rows, 128)
    t = lax.broadcasted_iota(jnp.int32, flat.shape, 0) % 8
    later = jnp.where(t == 7, 0.0, pltpu.roll(flat, x * rows - 1, 0))
    earlier = jnp.where(t == 0, 0.0, pltpu.roll(flat, 1, 0))
    wide = jnp.concatenate([later, flat, earlier], axis=1)
    return wide.astype(BF16).reshape(x, rows, 384)


def fold(sums, factor):
    lane = lax.broadcasted_iota(jnp.int32, (64, 128), 1)
    taps = []
    for g in sums:
        for l in range(3):
            if g is None:
                taps.append(jnp.zeros((64, 128), F32))
                continue
            part = g[:, l * 128 : (l + 1) * 128]
            f = jnp.where(lane < 64, part[0:64], part[64:128])
            taps.append((f + pltpu.roll(f, 64, 1)) * factor)
    taps.append(taps[-1])
    return [jnp.where(lane < 64, taps[2 * m], taps[2 * m + 1]) for m in range(14)]


def apply_taps(rows, taps):
    return lax.dot_general(rows, taps, (((1,), (1,)), ((), ())), preferred_element_type=F32)


def weight_sums(act, wide_ref, act_ref):
    act_ref[0:128] = jnp.zeros((128, 128), F32)
    act_ref[128:1152] = act.reshape(1024, 128)
    act_ref[1152:1280] = jnp.zeros((128, 128), F32)
    turned = act_ref[...].T.astype(BF16)
    stacked = jnp.concatenate([turned[:, 128 * i : 128 * i + 1024] for i in range(3)], axis=0)
    sums = [None] * 9
    for j in range(3):
        rows = wide_ref[2:18, 32 - 16 * j : 96 - 16 * j].reshape(1024, 384)
        part = jnp.dot(stacked, rows, preferred_element_type=F32)
        for i in range(3):
            sums[i * 3 + j] = part[128 * i : 128 * i + 128]
    return sums


def own_kernel(factor, back_ref, one_ref, w_ref, acc_ref, sums_ref, wide_ref, act_ref):
    wide_ref[2:18, 0:16] = jnp.zeros((16, 16, 384), BF16)
    wide_ref[2:18, 80:96] = jnp.zeros((16, 16, 384), BF16)
    wide_ref[2:18, 16:80] = triple(back_ref[...].astype(F32))
    acc_ref[...] = jnp.zeros((16, 96, 128), F32)
    rows = wide_ref[2:18, 16:80].reshape(1024, 384)
    for j in range(3):
        taps = jnp.concatenate([w_ref[i * 3 + j] for i in range(3)], axis=0)
        part = apply_taps(rows, taps).reshape(16, 64, 384)
        ys = slice(16 * j, 16 * j + 64)
        acc_ref[0:14, ys] += part[2:16, :, 0:128]
        acc_ref[:, ys] += part[:, :, 128:256]
        acc_ref[2:16, ys] += part[0:14, :, 256:384]
    sums = weight_sums(jnp.maximum(one_ref[...].astype(F32), 0.0), wide_ref, act_ref)
    for m, block in enumerate(fold(sums, factor)):
        sums_ref[64 * m : 64 * m + 64] = block


def conv_kernel(
    factor, at_ref, acc_ref, sums_ref, one_ref, chip_ref, cross_ref, w_ref, i0, i1, i2, i3,
    mine_ref, send_ref, outer_ref, rim_ref, wide_ref, in_ref, first_ref, act_ref,
):
    me = at_ref[0]
    parts = (i0, i1, i2, i3)
    n = len(parts)
    for s, part in enumerate(parts):
        in_ref[pl.ds(lax.rem(me + n - s, n) * 4, 4)] = part[...].reshape(4, 64, 128)

    def put(side, ref):
        rim_ref[side] = ref[...]

    share(at_ref[1], put, cross_ref, chip_ref)
    wide_ref[:, 0:2] = jnp.zeros((2, 2, 32, 384), BF16)
    wide_ref[:, 18:20] = jnp.zeros((2, 2, 32, 384), BF16)
    outer_ref[0:2] = jnp.zeros((2, 96, 384), BF16)
    outer_ref[18:20] = jnp.zeros((2, 96, 384), BF16)
    for side in range(2):
        wide_ref[side, 2:18] = triple(rim_ref[side, :, 0:32].astype(F32))
    first_ref[...] = acc_ref[...]
    act = jnp.maximum(one_ref[...].astype(F32), 0.0)
    sums = [None] * 9
    for side in range(2):
        j = 2 - 2 * side
        near = 16 - 16 * side
        own = 48 * side
        turned = act[:, own : own + 16].reshape(256, 128).T.astype(BF16)
        far = jnp.zeros((512, 128), F32)
        close = jnp.zeros((256, 128), F32)
        for i in range(3):
            xs = slice(4 - 2 * i, 20 - 2 * i)
            rows = wide_ref[side, xs, near : near + 16].reshape(256, 384)
            far += apply_taps(wide_ref[side, xs].reshape(512, 384), w_ref[i * 3 + j])
            close += apply_taps(rows, w_ref[i * 3 + 1])
            sums[i * 3 + j] = jnp.dot(turned, rows, preferred_element_type=F32)
        first_ref[:, 64 * side : 64 * side + 32] += far.reshape(16, 32, 128)
        first_ref[:, 80 * side : 80 * side + 16] += close.reshape(16, 16, 128)
    second = fold(sums, factor)
    pre = jnp.concatenate([rim_ref[0, :, 32:48], one_ref[...], rim_ref[1, :, 32:48]], axis=1).astype(F32)
    outer_ref[2:18] = triple(jnp.where(pre > 0, first_ref[...], 0.0))
    first = fold(weight_sums(in_ref[...].astype(F32), outer_ref, act_ref), factor)

    def emit(half, ref):
        for m in range(7):
            ref[64 * m : 64 * m + 64] = first[7 * half + m].astype(ref.dtype)
            at = 448 * half + 64 * m
            block = second[7 * half + m] + sums_ref[at : at + 64]
            ref[448 + 64 * m : 512 + 64 * m] = block.astype(ref.dtype)

    share(at_ref[1], emit, mine_ref, send_ref)


def grad_kernel(at_ref, outer_ref, w_ref, grad_ref, turn_ref):
    grad = jnp.zeros((256, 128), F32)
    for i in range(3):
        for j in range(3):
            mine = outer_ref[pl.ds(at_ref[0] * 4 + 4 - 2 * i, 4), 32 - 16 * j : 96 - 16 * j].reshape(256, 384)
            grad += apply_taps(mine, w_ref[i * 3 + j])
    turn_ref[...] = grad
    for x in range(4):
        for t in range(8):
            grad_ref[x, :, 128 * t : 128 * t + 128] = turn_ref[pl.ds(64 * x + t, 8, stride=8), :].astype(BF16)


def spread(half, ref, hbm_refs, refs, sems):
    copies = []
    count = 14 - half
    for k, (hbm, out) in enumerate(zip(hbm_refs, refs)):
        for m in range(7):
            block = ref[448 * k + 64 * m : 448 * k + 64 * m + 64].astype(F32)
            out[2 * m] = block[:, 0:64]
            out[2 * m + 1] = block[:, 64:128]
        copies.append(
            pltpu.make_async_copy(out.at[0:count], hbm.at[14 * half : 14 * half + count], sems.at[k])
        )
        copies[-1].start()
    for copy in copies:
        copy.wait()


def half_kernel(at_ref, ref, one_hbm, two_hbm, one_ref, two_ref, sems):
    @pl.when(at_ref[1] == 0)
    def _():
        spread(0, ref, (one_hbm, two_hbm), (one_ref, two_ref), sems)

    @pl.when(at_ref[1] != 0)
    def _():
        spread(1, ref, (one_hbm, two_hbm), (one_ref, two_ref), sems)


def rest_kernel(at_ref, ref, one_in, two_in, one_hbm, two_hbm, one_ref, two_ref, sems):
    @pl.when(at_ref[1] == 0)
    def _():
        spread(1, ref, (one_hbm, two_hbm), (one_ref, two_ref), sems)

    @pl.when(at_ref[1] != 0)
    def _():
        spread(0, ref, (one_hbm, two_hbm), (one_ref, two_ref), sems)


def trans_kernel(at_ref, mine_ref, other_ref, trans_ref):
    def emit(half, ref):
        for m in range(4):
            trans_ref[256 * half : 256 * half + 256, 128 * m : 128 * m + 128] = ref[256 * m : 256 * m + 256].astype(F32)

    share(at_ref[1], emit, mine_ref, other_ref)


def rotate(value, axis, step):
    n = lax.axis_size(axis)
    return lax.ppermute(value, axis, [(i, (i + step) % n) for i in range(n)])


def swap(value, axis, bit):
    n = lax.axis_size(axis)
    return lax.ppermute(value, axis, [(i, i ^ bit) for i in range(n)])


def on_chip(mine, send):
    return (mine + swap(send, "gy", 1).astype(F32)).astype(BF16)


def across(mine):
    return mine.astype(F32) + swap(mine, "gy", 2).astype(F32)


def slab_body(input_activation, pre_one, pre_two, w_one, w_two, w_trans, keep_mask, out_grad):
    factor = 1.0 / math.sqrt(
        input_activation.shape[0] * 4 * input_activation.shape[1] * 4 * (input_activation.shape[2] // 64)
    )
    at = jnp.stack([lax.axis_index("gx"), lax.rem(lax.axis_index("gy"), 2)]).astype(jnp.int32)
    shape = jax.ShapeDtypeStruct
    vmem = pltpu.VMEM
    natural = vmem((4, 8, 1024), BF16)
    first, second = call(
        pack_kernel,
        (shape((768, 128), BF16), shape((256, 128), BF16)),
        [
            vmem((8, 4, 8, 128), BF16), natural, natural, natural, vmem((3, 256, 128), F32),
            pltpu.SemaphoreType.DMA((4,)),
        ],
        0,
        56,
        (out_grad,),
        (pre_two,),
        (pre_one,),
        (input_activation,),
    )
    firsts = [first] + [rotate(first, "gx", s) for s in (1, 2, 3)]
    seconds = [second] + [rotate(second, "gx", s) for s in (1, 2, 3)]
    kept, mask, d2, d1 = call(
        weight_kernel,
        (
            shape((512, 512), BF16), shape((512, 512), BF16),
            shape((9, 128, 384), BF16), shape((9, 128, 384), BF16),
        ),
        [
            vmem((512, 512), BF16), vmem((8, 8), jnp.int32),
            vmem((27, 64, 64), BF16), vmem((27, 64, 64), BF16),
            pltpu.SemaphoreType.DMA((4,)),
        ],
        10**7,
        8,
        (w_trans,),
        (keep_mask,),
        (w_two,),
        (w_one,),
    )
    back, one, chip, cross, tmine, tsend = call(
        functools.partial(transition_kernel, factor),
        (
            shape((8, 2, 64, 128), BF16),
            shape((16, 64, 128), BF16),
            shape((8, 2, 48, 128), BF16),
            shape((8, 2, 48, 128), BF16),
            shape((1024, 128), F32),
            shape((1024, 128), BF16),
        ),
        [vmem((4, 256, 128), BF16), vmem((16, 64, 128), BF16)],
        4 * 256 * 512 * 512,
        12,
        at,
        *firsts,
        kept,
        mask,
    )
    n = lax.axis_size("gy")
    pairs = [(i, i + 1) for i in range(1, n - 1, 2)]
    cross = lax.ppermute(cross, "gy", pairs + [(j, i) for i, j in pairs])
    chip = swap(chip, "gy", 1)
    tsend, *seconds = lax.optimization_barrier((tsend, *seconds))
    tmine = on_chip(tmine, tsend)
    one, tmine = lax.optimization_barrier((one, tmine))
    acc, sums = call(
        functools.partial(own_kernel, factor),
        (shape((16, 96, 128), F32), shape((896, 128), F32)),
        [vmem((20, 96, 384), BF16), vmem((1280, 128), F32)],
        2 * 128 * 3456 * 2048,
        16,
        back.reshape(16, 64, 128),
        one,
        d2,
    )
    tmine = across(tmine)
    mine, send, outer = call(
        functools.partial(conv_kernel, factor),
        (shape((896, 128), F32), shape((896, 128), BF16), shape((20, 96, 384), BF16)),
        [
            vmem((2, 16, 48, 128), BF16),
            vmem((2, 20, 32, 384), BF16),
            vmem((16, 64, 128), BF16),
            vmem((16, 96, 128), F32),
            vmem((1280, 128), F32),
        ],
        2 * 128 * 3456 * 900,
        20,
        at,
        acc,
        sums,
        one,
        chip.reshape(16, 48, 128),
        cross.reshape(16, 48, 128),
        d2,
        *seconds,
    )
    send, tmine = lax.optimization_barrier((send, tmine))
    mine = on_chip(mine, send)
    away = swap(mine, "gy", 2)
    tother = swap(tmine, "gy", 1)
    grad_w_trans = call(trans_kernel, shape((512, 512), F32), [], 10**7, 6, at, tmine, tother)
    grad_in = call(
        grad_kernel, shape((4, 8, 1024), BF16), [vmem((256, 128), F32)], 2 * 128 * 3456 * 256, 12, at, outer, d1
    )
    away, grad_w_trans, grad_in = lax.optimization_barrier((away, grad_w_trans, grad_in))
    mine = (mine.astype(F32) + away.astype(F32)).astype(BF16)
    other = swap(mine, "gy", 1)
    taps = shape((27, 64, 64), F32)
    scratch = [vmem((14, 64, 64), F32), vmem((14, 64, 64), F32), pltpu.SemaphoreType.DMA((2,))]
    hbm = pltpu.MemorySpace.HBM
    grad_w_one, grad_w_two = call(half_kernel, (taps, taps), scratch, 10**8, 6, at, mine, out_space=hbm)
    grad_w_one, grad_w_two = call(
        rest_kernel,
        (taps, taps),
        scratch,
        0,
        6,
        at,
        other,
        (grad_w_one,),
        (grad_w_two,),
        out_space=hbm,
        aliases={2: 0, 3: 1},
    )
    return (grad_in, grad_w_one, grad_w_two, grad_w_trans)


def solution(mesh):
    fits = mesh.shape["gx"] == 4 and mesh.shape["gy"] == 4

    def pick(*args):
        shapes = tuple(a.shape for a in args)
        known = (
            ((4, 8, 1024),) * 3 + ((27, 64, 64),) * 2 + ((512, 512), (8, 8), (8, 4, 8, 128))
        )
        return (slab_body if fits and shapes == known else body)(*args)

    return jax.shard_map(
        pick,
        mesh=mesh,
        in_specs=(
            P(("grp", "gx"), "gy", None),
            P(("grp", "gx"), "gy", None),
            P(("grp", "gx"), "gy", None),
            P(),
            P(),
            P(),
            P(),
            P("grp", "gy", None, "gx"),
        ),
        out_specs=(
            P(("grp", "gx"), "gy", None),
            P("grp", None, None),
            P("grp", None, None),
            P("grp", None),
        ),
        check_vma=False,
    )
```

```python
import functools
import math

import jax
import jax.numpy as jnp
from jax import lax
from jax.experimental import pallas as pl
from jax.experimental.pallas import tpu as pltpu
from jax.sharding import PartitionSpec as P

DILATION_STEP = 2
VMEM = pltpu.MemorySpace.VMEM
SMEM = pltpu.MemorySpace.SMEM
F32 = jnp.float32
BF16 = jnp.bfloat16


def padded(cells, sides, width):
    for axis, dim in sides:
        count = lax.axis_size(axis)
        ends = count - 1
        head = lax.slice_in_dim(cells, 0, width, axis=dim)
        tail = lax.slice_in_dim(cells, cells.shape[dim] - width, cells.shape[dim], axis=dim)
        cells = jnp.concatenate(
            [
                lax.ppermute(tail, axis, [(i, (i + 1) % count) for i in range(ends)]),
                cells,
                lax.ppermute(head, axis, [((i + 1) % count, i) for i in range(ends)]),
            ],
            axis=dim,
        )
    return cells


def split_layout(joined_layout, channel_count):
    return joined_layout.reshape(joined_layout.shape[0], joined_layout.shape[1], -1, channel_count)


def to_blocks(cube_volume):
    shape_all = cube_volume.shape
    parted = cube_volume.reshape(
        shape_all[0] // 2, 2, shape_all[1] // 2, 2, shape_all[2] // 2, 2, shape_all[3]
    )
    parted = parted.transpose(0, 2, 4, 1, 3, 5, 6)
    return parted.reshape(shape_all[0] // 2, shape_all[1] // 2, shape_all[2] // 2, 8 * shape_all[3])


def from_blocks(blocked, channel_count):
    shape_all = blocked.shape
    parted = blocked.reshape(shape_all[0], shape_all[1], shape_all[2], 2, 2, 2, channel_count)
    parted = parted.transpose(0, 3, 1, 4, 2, 5, 6)
    return parted.reshape(2 * shape_all[0], 2 * shape_all[1], 2 * shape_all[2], channel_count)


def padding_depth(cube_volume, margin):
    return jnp.pad(cube_volume, ((0, 0), (0, 0), (margin, margin), (0, 0)))


def weight_terms(bordered_input, upstream_gradient):
    channel_count = upstream_gradient.shape[3]
    grid_extent = upstream_gradient.shape
    padded_input = padding_depth(bordered_input, DILATION_STEP)
    flat_grad = upstream_gradient.reshape(-1, channel_count)
    partials = []
    for x_index in range(3):
        for y_index in range(3):
            sliding_window = padded_input[
                DILATION_STEP * x_index : DILATION_STEP * x_index + grid_extent[0],
                DILATION_STEP * y_index : DILATION_STEP * y_index + grid_extent[1],
            ]
            columns = jnp.concatenate(
                [
                    sliding_window[
                        :, :, DILATION_STEP * tap_index : DILATION_STEP * tap_index + grid_extent[2]
                    ].reshape(-1, channel_count)
                    for tap_index in range(3)
                ],
                axis=1,
            )
            partials.append(
                lax.dot_general(
                    columns, flat_grad, (((0,), (0,)), ((), ())), preferred_element_type=jnp.float32
                )
            )
    return jnp.stack(partials).reshape(27, channel_count, channel_count)


def data_terms(bordered_input, weights):
    channel_count = weights.shape[1]
    x_stretch = bordered_input.shape[0] - 2 * DILATION_STEP
    y_stretch = bordered_input.shape[1] - 2 * DILATION_STEP
    depth_cells = bordered_input.shape[2]
    padded_input = padding_depth(bordered_input, DILATION_STEP)
    stacked = jnp.transpose(weights, (0, 2, 1)).reshape(9, 3 * channel_count, channel_count)
    running = jnp.zeros((x_stretch * y_stretch * depth_cells, channel_count), jnp.float32)
    for x_index in range(3):
        for y_index in range(3):
            sliding_window = padded_input[
                DILATION_STEP * (2 - x_index) : DILATION_STEP * (2 - x_index) + x_stretch,
                DILATION_STEP * (2 - y_index) : DILATION_STEP * (2 - y_index) + y_stretch,
            ]
            columns = jnp.concatenate(
                [
                    sliding_window[
                        :,
                        :,
                        DILATION_STEP * (2 - tap_index) : DILATION_STEP * (2 - tap_index)
                        + depth_cells,
                    ].reshape(-1, channel_count)
                    for tap_index in range(3)
                ],
                axis=1,
            )
            running = running + jnp.dot(
                columns, stacked[x_index * 3 + y_index], preferred_element_type=jnp.float32
            )
    return running.reshape(x_stretch, y_stretch, depth_cells, channel_count)


def body(input_activation, pre_one, pre_two, w_one, w_two, w_trans, keep_mask, out_grad):
    channel_count = w_one.shape[1]
    x_stretch, y_stretch, joined_layout = input_activation.shape
    depth_cells = joined_layout // channel_count
    width_t = w_trans.shape[0]
    factor = 1.0 / math.sqrt(
        x_stretch * lax.axis_size("gx") * y_stretch * lax.axis_size("gy") * depth_cells
    )
    blocks = jnp.repeat(
        jnp.repeat(keep_mask.astype(jnp.bfloat16), channel_count, axis=0), channel_count, axis=1
    )
    w_kept = w_trans * blocks
    regrouped = lax.all_to_all(out_grad, "gx", split_axis=0, concat_axis=3, tiled=True)
    grad_rows = regrouped.reshape(-1, width_t)
    back_blocks = lax.dot_general(
        grad_rows, w_kept, (((1,), (1,)), ((), ())), preferred_element_type=jnp.float32
    ).astype(jnp.bfloat16)
    act_two = split_layout(jnp.maximum(pre_two, 0), channel_count)
    two_rows = to_blocks(act_two).reshape(-1, width_t)
    trans_term = (
        lax.dot_general(
            two_rows, grad_rows, (((0,), (0,)), ((), ())), preferred_element_type=jnp.float32
        )
        * blocks.astype(jnp.float32)
        * factor
    )
    grad_w_trans = lax.psum(trans_term, ("gx", "gy"))
    back_two = from_blocks(
        back_blocks.reshape(x_stretch // 2, y_stretch // 2, depth_cells // 2, width_t),
        channel_count,
    )
    back_two = jnp.where(
        split_layout(pre_two, channel_count) > 0, back_two, jnp.zeros_like(back_two)
    )
    first_activation = jnp.maximum(pre_one, 0)
    bordered_input = padded(
        jnp.concatenate([input_activation, first_activation], axis=2),
        (("gx", 0), ("gy", 1)),
        DILATION_STEP,
    )
    in_rim = split_layout(bordered_input[:, :, :joined_layout], channel_count)
    one_rim = split_layout(bordered_input[:, :, joined_layout:], channel_count)
    two_term = weight_terms(one_rim, back_two) * factor
    flattened_backward = back_two.reshape(x_stretch, y_stretch, joined_layout)
    narrowed_slice = split_layout(
        padded(flattened_backward, (("gx", 0), ("gy", 1)), DILATION_STEP), channel_count
    )
    first_backward = data_terms(narrowed_slice, w_two)
    first_backward = jnp.where(
        split_layout(pre_one, channel_count) > 0, first_backward, jnp.zeros_like(first_backward)
    ).astype(jnp.bfloat16)
    one_grad_rim = split_layout(
        padded(
            first_backward.reshape(x_stretch, y_stretch, joined_layout),
            (("gx", 0), ("gy", 1)),
            DILATION_STEP,
        ),
        channel_count,
    )
    grad_w_two = lax.psum(two_term, ("gx", "gy"))
    one_term = weight_terms(in_rim, first_backward) * factor
    grad_w_one = lax.psum(one_term, ("gx", "gy"))
    grad_in = (
        data_terms(one_grad_rim, w_one)
        .astype(jnp.bfloat16)
        .reshape(x_stretch, y_stretch, joined_layout)
    )
    return (grad_in, grad_w_one, grad_w_two, grad_w_trans)


def call(kernel, out_shape, scratch, flops, limit, *args, out_space=VMEM, aliases={}):
    spec = []
    for a in args:
        if isinstance(a, tuple):
            spec.append(pl.BlockSpec(memory_space=pltpu.MemorySpace.HBM))
        elif a.dtype == jnp.int32:
            spec.append(pl.BlockSpec(memory_space=SMEM))
        else:
            spec.append(pl.BlockSpec(memory_space=VMEM))
    arrays = [a[0] if isinstance(a, tuple) else a for a in args]
    return pl.pallas_call(
        kernel,
        out_shape=out_shape,
        in_specs=spec,
        out_specs=jax.tree.map(lambda _: pl.BlockSpec(memory_space=out_space), out_shape),
        scratch_shapes=scratch,
        input_output_aliases=aliases,
        cost_estimate=pl.CostEstimate(
            flops=flops,
            transcendentals=0,
            bytes_accessed=sum(a.size * a.dtype.itemsize for a in arrays) if flops else 0,
        ),
        compiler_params=pltpu.CompilerParams(vmem_limit_bytes=limit * 1024 * 1024),
    )(*arrays)


def fetch(pairs, sems):
    copies = [pltpu.make_async_copy(src, dst, sems.at[k]) for k, (src, dst) in enumerate(pairs)]
    for copy in copies:
        copy.start()
    return copies


def pack_kernel(og, two, one, act, first_ref, second_ref, og_v, two_v, one_v, act_v, turn_ref, sems):
    copies = fetch(((og, og_v), (two, two_v), (one, one_v), (act, act_v)), sems)
    copies[0].wait()
    first_ref[0:256] = og_v[...].astype(F32).reshape(256, 128).astype(BF16)
    for k, (ref, out, at) in enumerate(((two_v, first_ref, 256), (one_v, first_ref, 512), (act_v, second_ref, 0))):
        copies[k + 1].wait()
        for x in range(4):
            for t in range(8):
                turn_ref[k, pl.ds(64 * x + t, 8, stride=8), :] = ref[x, :, 128 * t : 128 * t + 128].astype(F32)
        out[at : at + 256] = turn_ref[k].astype(BF16)


def weight_kernel(wt, keep, w2, w1, kept_ref, mask_ref, d2_ref, d1_ref, wt_v, keep_v, w2_v, w1_v, sems):
    copies = fetch(((keep, keep_v), (wt, wt_v), (w2, w2_v), (w1, w1_v)), sems)
    copies[0].wait()
    width = wt_v.shape[0]
    blocks = keep_v.shape[0]
    side = width // blocks
    left = (
        lax.broadcasted_iota(jnp.int32, (width, blocks), 0) // side
        == lax.broadcasted_iota(jnp.int32, (width, blocks), 1)
    ).astype(BF16)
    right = (
        lax.broadcasted_iota(jnp.int32, (blocks, width), 1) // side
        == lax.broadcasted_iota(jnp.int32, (blocks, width), 0)
    ).astype(BF16)
    wide = jnp.dot(keep_v[...].astype(F32).astype(BF16), right, preferred_element_type=F32).astype(BF16)
    mask = jnp.dot(left, wide, preferred_element_type=F32)
    mask_ref[...] = mask.astype(BF16)
    copies[1].wait()
    kept_ref[...] = (wt_v[...].astype(F32) * mask).astype(BF16)
    none = jnp.zeros((64, 64), BF16)
    for k, (ref, out) in enumerate(((w2_v, d2_ref), (w1_v, d1_ref))):
        copies[k + 2].wait()
        for tap in range(27):
            w = ref[tap]
            at = 128 * (tap % 3)
            out[tap // 3, 0:64, at : at + 128] = jnp.concatenate([w, none], axis=1)
            out[tap // 3, 64:128, at : at + 128] = jnp.concatenate([none, w], axis=1)


def transition_kernel(
    factor, at_ref, a0, a1, a2, a3, kept_ref, mask_ref, back_ref, one_ref, chip_ref, cross_ref, mine_ref, send0_ref, send1_ref, og_ref, two_ref
):
    me = at_ref[0]
    parts = (a0, a1, a2, a3)
    n = len(parts)
    for s, part in enumerate(parts):
        src = lax.rem(me + n - s, n)
        og_ref[src] = part[0:256]
        spot = pl.ds(src * 4, 4)
        two_ref[spot] = part[256:512].reshape(4, 64, 128)
        one_ref[spot] = part[512:768].reshape(4, 64, 128)
    og = jnp.concatenate([og_ref[j] for j in range(n)], axis=1)
    back = lax.dot_general(og, kept_ref[...], (((1,), (1,)), ((), ())), preferred_element_type=F32)
    two = two_ref[...].astype(F32).reshape(8, 2, 4, 2, 8, 128)
    cells = []
    for p in range(2):
        halves = []
        for q in range(2):
            pre = two[:, p, :, q]
            at = (p * 2 + q) * 128
            grad = back[:, at : at + 128].reshape(8, 4, 8, 128)
            halves.append(jnp.where(pre > 0, grad, 0.0))
            cells.append(jnp.maximum(pre, 0.0).reshape(256, 128).astype(BF16))
        back_ref[:, p] = jnp.stack(halves, axis=2).reshape(8, 64, 128).astype(BF16)

    def rim(high, ref):
        at = 32 if high else 0
        ref[:, :, 0:32] = back_ref[:, :, at : at + 32]
        at = 48 if high else 0
        ref[:, :, 32:48] = one_ref[:, at : at + 16].reshape(8, 2, 16, 128)

    share(at_ref[1], rim, cross_ref, chip_ref)
    flat = jnp.concatenate(cells, axis=1)
    trans = lax.dot_general(flat, og, (((0,), (0,)), ((), ())), preferred_element_type=F32)
    trans = trans * mask_ref[...].astype(F32) * factor

    def emit(half, refs):
        for m in range(4):
            ref = refs[256 * m // refs[0].shape[0]]
            at = 256 * m % ref.shape[0]
            ref[at : at + 256] = trans[256 * half : 256 * half + 256, 128 * m : 128 * m + 128].astype(ref.dtype)

    share(at_ref[1], emit, (mine_ref,), (send0_ref, send1_ref))


def share(core, emit, mine_ref, send_ref):
    @pl.when(core == 0)
    def _():
        emit(0, mine_ref)
        emit(1, send_ref)

    @pl.when(core != 0)
    def _():
        emit(1, mine_ref)
        emit(0, send_ref)


def triple(v):
    x, rows, _ = v.shape
    flat = v.reshape(x * rows, 128)
    t = lax.broadcasted_iota(jnp.int32, flat.shape, 0) % 8
    later = jnp.where(t == 7, 0.0, pltpu.roll(flat, x * rows - 1, 0))
    earlier = jnp.where(t == 0, 0.0, pltpu.roll(flat, 1, 0))
    wide = jnp.concatenate([later, flat, earlier], axis=1)
    return wide.astype(BF16).reshape(x, rows, 384)


def fold(sums, factor):
    lane = lax.broadcasted_iota(jnp.int32, (64, 128), 1)
    taps = []
    for g in sums:
        for l in range(3):
            if g is None:
                taps.append(jnp.zeros((64, 128), F32))
                continue
            part = g[:, l * 128 : (l + 1) * 128]
            f = jnp.where(lane < 64, part[0:64], part[64:128])
            taps.append((f + pltpu.roll(f, 64, 1)) * factor)
    taps.append(taps[-1])
    return [jnp.where(lane < 64, taps[2 * m], taps[2 * m + 1]) for m in range(14)]


def apply_taps(rows, taps):
    return lax.dot_general(rows, taps, (((1,), (1,)), ((), ())), preferred_element_type=F32)


def weight_sums(act, wide_ref, act_ref):
    act_ref[0:128] = jnp.zeros((128, 128), F32)
    act_ref[128:1152] = act.reshape(1024, 128)
    act_ref[1152:1280] = jnp.zeros((128, 128), F32)
    turned = act_ref[...].T.astype(BF16)
    stacked = jnp.concatenate([turned[:, 128 * i : 128 * i + 1024] for i in range(3)], axis=0)
    sums = [None] * 9
    for j in range(3):
        rows = wide_ref[2:18, 32 - 16 * j : 96 - 16 * j].reshape(1024, 384)
        part = jnp.dot(stacked, rows, preferred_element_type=F32)
        for i in range(3):
            sums[i * 3 + j] = part[128 * i : 128 * i + 128]
    return sums


def own_kernel(factor, back_ref, one_ref, w_ref, acc_ref, sums_ref, wide_ref, act_ref):
    wide_ref[2:18, 0:16] = jnp.zeros((16, 16, 384), BF16)
    wide_ref[2:18, 80:96] = jnp.zeros((16, 16, 384), BF16)
    wide_ref[2:18, 16:80] = triple(back_ref[...].astype(F32))
    acc_ref[...] = jnp.zeros((16, 96, 128), F32)
    rows = wide_ref[2:18, 16:80].reshape(1024, 384)
    for j in range(3):
        taps = jnp.concatenate([w_ref[i * 3 + j] for i in range(3)], axis=0)
        part = apply_taps(rows, taps).reshape(16, 64, 384)
        ys = slice(16 * j, 16 * j + 64)
        acc_ref[0:14, ys] += part[2:16, :, 0:128]
        acc_ref[:, ys] += part[:, :, 128:256]
        acc_ref[2:16, ys] += part[0:14, :, 256:384]
    sums = weight_sums(jnp.maximum(one_ref[...].astype(F32), 0.0), wide_ref, act_ref)
    for m, block in enumerate(fold(sums, factor)):
        sums_ref[64 * m : 64 * m + 64] = block


def conv_kernel(
    factor, at_ref, acc_ref, sums_ref, one_ref, chip_ref, cross_ref, w_ref, i0, i1, i2, i3,
    mine_ref, send_ref, outer_ref, rim_ref, wide_ref, in_ref, first_ref, act_ref,
):
    me = at_ref[0]
    parts = (i0, i1, i2, i3)
    n = len(parts)
    for s, part in enumerate(parts):
        in_ref[pl.ds(lax.rem(me + n - s, n) * 4, 4)] = part[...].reshape(4, 64, 128)

    def put(side, ref):
        rim_ref[side] = ref[...]

    share(at_ref[1], put, cross_ref, chip_ref)
    wide_ref[:, 0:2] = jnp.zeros((2, 2, 32, 384), BF16)
    wide_ref[:, 18:20] = jnp.zeros((2, 2, 32, 384), BF16)
    outer_ref[0:2] = jnp.zeros((2, 96, 384), BF16)
    outer_ref[18:20] = jnp.zeros((2, 96, 384), BF16)
    for side in range(2):
        wide_ref[side, 2:18] = triple(rim_ref[side, :, 0:32].astype(F32))
    first_ref[...] = acc_ref[...]
    act = jnp.maximum(one_ref[...].astype(F32), 0.0)
    sums = [None] * 9
    for side in range(2):
        j = 2 - 2 * side
        near = 16 - 16 * side
        own = 48 * side
        turned = act[:, own : own + 16].reshape(256, 128).T.astype(BF16)
        far = jnp.zeros((512, 128), F32)
        close = jnp.zeros((256, 128), F32)
        for i in range(3):
            xs = slice(4 - 2 * i, 20 - 2 * i)
            rows = wide_ref[side, xs, near : near + 16].reshape(256, 384)
            far += apply_taps(wide_ref[side, xs].reshape(512, 384), w_ref[i * 3 + j])
            close += apply_taps(rows, w_ref[i * 3 + 1])
            sums[i * 3 + j] = jnp.dot(turned, rows, preferred_element_type=F32)
        first_ref[:, 64 * side : 64 * side + 32] += far.reshape(16, 32, 128)
        first_ref[:, 80 * side : 80 * side + 16] += close.reshape(16, 16, 128)
    second = fold(sums, factor)
    pre = jnp.concatenate([rim_ref[0, :, 32:48], one_ref[...], rim_ref[1, :, 32:48]], axis=1).astype(F32)
    outer_ref[2:18] = triple(jnp.where(pre > 0, first_ref[...], 0.0))
    first = fold(weight_sums(in_ref[...].astype(F32), outer_ref, act_ref), factor)

    def emit(half, ref):
        for m in range(7):
            ref[64 * m : 64 * m + 64] = first[7 * half + m].astype(ref.dtype)
            at = 448 * half + 64 * m
            block = second[7 * half + m] + sums_ref[at : at + 64]
            ref[448 + 64 * m : 512 + 64 * m] = block.astype(ref.dtype)

    share(at_ref[1], emit, mine_ref, send_ref)


def grad_kernel(at_ref, outer_ref, w_ref, grad_ref, turn_ref):
    grad = jnp.zeros((256, 128), F32)
    for i in range(3):
        for j in range(3):
            mine = outer_ref[pl.ds(at_ref[0] * 4 + 4 - 2 * i, 4), 32 - 16 * j : 96 - 16 * j].reshape(256, 384)
            grad += apply_taps(mine, w_ref[i * 3 + j])
    turn_ref[...] = grad
    for x in range(4):
        for t in range(8):
            grad_ref[x, :, 128 * t : 128 * t + 128] = turn_ref[pl.ds(64 * x + t, 8, stride=8), :].astype(BF16)


def spread(half, ref, hbm_refs, refs, sems):
    copies = []
    count = 14 - half
    for k, (hbm, out) in enumerate(zip(hbm_refs, refs)):
        for m in range(7):
            block = ref[448 * k + 64 * m : 448 * k + 64 * m + 64].astype(F32)
            out[2 * m] = block[:, 0:64]
            out[2 * m + 1] = block[:, 64:128]
        copies.append(
            pltpu.make_async_copy(out.at[0:count], hbm.at[14 * half : 14 * half + count], sems.at[k])
        )
        copies[-1].start()
    for copy in copies:
        copy.wait()


def half_kernel(at_ref, ref, one_hbm, two_hbm, one_ref, two_ref, sems):
    @pl.when(at_ref[1] == 0)
    def _():
        spread(0, ref, (one_hbm, two_hbm), (one_ref, two_ref), sems)

    @pl.when(at_ref[1] != 0)
    def _():
        spread(1, ref, (one_hbm, two_hbm), (one_ref, two_ref), sems)


def rest_kernel(at_ref, ref, one_in, two_in, one_hbm, two_hbm, one_ref, two_ref, sems):
    @pl.when(at_ref[1] == 0)
    def _():
        spread(1, ref, (one_hbm, two_hbm), (one_ref, two_ref), sems)

    @pl.when(at_ref[1] != 0)
    def _():
        spread(0, ref, (one_hbm, two_hbm), (one_ref, two_ref), sems)


def trans_kernel(at_ref, mine_ref, other_ref, trans_ref):
    def emit(half, ref):
        for m in range(4):
            trans_ref[256 * half : 256 * half + 256, 128 * m : 128 * m + 128] = ref[256 * m : 256 * m + 256].astype(F32)

    share(at_ref[1], emit, mine_ref, other_ref)


def rotate(value, axis, step):
    n = lax.axis_size(axis)
    return lax.ppermute(value, axis, [(i, (i + step) % n) for i in range(n)])


def swap(value, axis, bit):
    n = lax.axis_size(axis)
    return lax.ppermute(value, axis, [(i, i ^ bit) for i in range(n)])


def on_chip(mine, send):
    return (mine + swap(send, "gy", 1).astype(F32)).astype(BF16)


def across(mine):
    return mine.astype(F32) + swap(mine, "gy", 2).astype(F32)


def slab_body(input_activation, pre_one, pre_two, w_one, w_two, w_trans, keep_mask, out_grad):
    factor = 1.0 / math.sqrt(
        input_activation.shape[0] * 4 * input_activation.shape[1] * 4 * (input_activation.shape[2] // 64)
    )
    at = jnp.stack([lax.axis_index("gx"), lax.rem(lax.axis_index("gy"), 2)]).astype(jnp.int32)
    shape = jax.ShapeDtypeStruct
    vmem = pltpu.VMEM
    natural = vmem((4, 8, 1024), BF16)
    first, second = call(
        pack_kernel,
        (shape((768, 128), BF16), shape((256, 128), BF16)),
        [
            vmem((8, 4, 8, 128), BF16), natural, natural, natural, vmem((3, 256, 128), F32),
            pltpu.SemaphoreType.DMA((4,)),
        ],
        0,
        56,
        (out_grad,),
        (pre_two,),
        (pre_one,),
        (input_activation,),
    )
    firsts = [first] + [rotate(first, "gx", s) for s in (1, 2, 3)]
    seconds = [second] + [rotate(second, "gx", s) for s in (1, 2, 3)]
    kept, mask, d2, d1 = call(
        weight_kernel,
        (
            shape((512, 512), BF16), shape((512, 512), BF16),
            shape((9, 128, 384), BF16), shape((9, 128, 384), BF16),
        ),
        [
            vmem((512, 512), BF16), vmem((8, 8), jnp.int32),
            vmem((27, 64, 64), BF16), vmem((27, 64, 64), BF16),
            pltpu.SemaphoreType.DMA((4,)),
        ],
        10**7,
        8,
        (w_trans,),
        (keep_mask,),
        (w_two,),
        (w_one,),
    )
    back, one, chip, cross, tmine, *tsend = call(
        functools.partial(transition_kernel, factor),
        (
            shape((8, 2, 64, 128), BF16),
            shape((16, 64, 128), BF16),
            shape((8, 2, 48, 128), BF16),
            shape((8, 2, 48, 128), BF16),
            shape((1024, 128), F32),
            shape((512, 128), BF16),
            shape((512, 128), BF16),
        ),
        [vmem((4, 256, 128), BF16), vmem((16, 64, 128), BF16)],
        4 * 256 * 512 * 512,
        12,
        at,
        *firsts,
        kept,
        mask,
    )
    n = lax.axis_size("gy")
    pairs = [(i, i + 1) for i in range(1, n - 1, 2)]
    cross = lax.ppermute(cross, "gy", pairs + [(j, i) for i, j in pairs])
    chip = swap(chip, "gy", 1)
    *tsend, last = lax.optimization_barrier((*tsend, seconds[1:]))
    seconds = [seconds[0], *last]
    taken = jnp.concatenate([swap(piece, "gy", 1) for piece in tsend], axis=0)
    acc, sums = call(
        functools.partial(own_kernel, factor),
        (shape((16, 96, 128), F32), shape((896, 128), F32)),
        [vmem((20, 96, 384), BF16), vmem((1280, 128), F32)],
        2 * 128 * 3456 * 2048,
        16,
        back.reshape(16, 64, 128),
        one,
        d2,
    )
    tmine, chip, cross, acc = lax.optimization_barrier((tmine, chip, cross, acc))
    tmine = (tmine + taken.astype(F32)).astype(BF16)
    tmine = across(tmine)
    mine, send, outer = call(
        functools.partial(conv_kernel, factor),
        (shape((896, 128), F32), shape((896, 128), BF16), shape((20, 96, 384), BF16)),
        [
            vmem((2, 16, 48, 128), BF16),
            vmem((2, 20, 32, 384), BF16),
            vmem((16, 64, 128), BF16),
            vmem((16, 96, 128), F32),
            vmem((1280, 128), F32),
        ],
        2 * 128 * 3456 * 900,
        20,
        at,
        acc,
        sums,
        one,
        chip.reshape(16, 48, 128),
        cross.reshape(16, 48, 128),
        d2,
        *seconds,
    )
    send, tmine = lax.optimization_barrier((send, tmine))
    mine = on_chip(mine, send)
    away = swap(mine, "gy", 2)
    tother = swap(tmine, "gy", 1)
    grad_w_trans = call(trans_kernel, shape((512, 512), F32), [], 10**7, 6, at, tmine, tother)
    grad_in = call(
        grad_kernel, shape((4, 8, 1024), BF16), [vmem((256, 128), F32)], 2 * 128 * 3456 * 256, 12, at, outer, d1
    )
    away, grad_w_trans, grad_in = lax.optimization_barrier((away, grad_w_trans, grad_in))
    mine = (mine.astype(F32) + away.astype(F32)).astype(BF16)
    other = swap(mine, "gy", 1)
    taps = shape((27, 64, 64), F32)
    scratch = [vmem((14, 64, 64), F32), vmem((14, 64, 64), F32), pltpu.SemaphoreType.DMA((2,))]
    hbm = pltpu.MemorySpace.HBM
    grad_w_one, grad_w_two = call(half_kernel, (taps, taps), scratch, 10**8, 6, at, mine, out_space=hbm)
    grad_w_one, grad_w_two = call(
        rest_kernel,
        (taps, taps),
        scratch,
        0,
        6,
        at,
        other,
        (grad_w_one,),
        (grad_w_two,),
        out_space=hbm,
        aliases={2: 0, 3: 1},
    )
    return (grad_in, grad_w_one, grad_w_two, grad_w_trans)


def solution(mesh):
    fits = mesh.shape["gx"] == 4 and mesh.shape["gy"] == 4

    def pick(*args):
        shapes = tuple(a.shape for a in args)
        known = (
            ((4, 8, 1024),) * 3 + ((27, 64, 64),) * 2 + ((512, 512), (8, 8), (8, 4, 8, 128))
        )
        return (slab_body if fits and shapes == known else body)(*args)

    return jax.shard_map(
        pick,
        mesh=mesh,
        in_specs=(
            P(("grp", "gx"), "gy", None),
            P(("grp", "gx"), "gy", None),
            P(("grp", "gx"), "gy", None),
            P(),
            P(),
            P(),
            P(),
            P("grp", "gy", None, "gx"),
        ),
        out_specs=(
            P(("grp", "gx"), "gy", None),
            P("grp", None, None),
            P("grp", None, None),
            P("grp", None),
        ),
        check_vma=False,
    )
```

```python
import functools
import math

import jax
import jax.numpy as jnp
from jax import lax
from jax.experimental import pallas as pl
from jax.experimental.pallas import tpu as pltpu
from jax.sharding import PartitionSpec as P

DILATION_STEP = 2
VMEM = pltpu.MemorySpace.VMEM
SMEM = pltpu.MemorySpace.SMEM
F32 = jnp.float32
BF16 = jnp.bfloat16


def padded(cells, sides, width):
    for axis, dim in sides:
        count = lax.axis_size(axis)
        ends = count - 1
        head = lax.slice_in_dim(cells, 0, width, axis=dim)
        tail = lax.slice_in_dim(cells, cells.shape[dim] - width, cells.shape[dim], axis=dim)
        cells = jnp.concatenate(
            [
                lax.ppermute(tail, axis, [(i, (i + 1) % count) for i in range(ends)]),
                cells,
                lax.ppermute(head, axis, [((i + 1) % count, i) for i in range(ends)]),
            ],
            axis=dim,
        )
    return cells


def split_layout(joined_layout, channel_count):
    return joined_layout.reshape(joined_layout.shape[0], joined_layout.shape[1], -1, channel_count)


def to_blocks(cube_volume):
    shape_all = cube_volume.shape
    parted = cube_volume.reshape(
        shape_all[0] // 2, 2, shape_all[1] // 2, 2, shape_all[2] // 2, 2, shape_all[3]
    )
    parted = parted.transpose(0, 2, 4, 1, 3, 5, 6)
    return parted.reshape(shape_all[0] // 2, shape_all[1] // 2, shape_all[2] // 2, 8 * shape_all[3])


def from_blocks(blocked, channel_count):
    shape_all = blocked.shape
    parted = blocked.reshape(shape_all[0], shape_all[1], shape_all[2], 2, 2, 2, channel_count)
    parted = parted.transpose(0, 3, 1, 4, 2, 5, 6)
    return parted.reshape(2 * shape_all[0], 2 * shape_all[1], 2 * shape_all[2], channel_count)


def padding_depth(cube_volume, margin):
    return jnp.pad(cube_volume, ((0, 0), (0, 0), (margin, margin), (0, 0)))


def weight_terms(bordered_input, upstream_gradient):
    channel_count = upstream_gradient.shape[3]
    grid_extent = upstream_gradient.shape
    padded_input = padding_depth(bordered_input, DILATION_STEP)
    flat_grad = upstream_gradient.reshape(-1, channel_count)
    partials = []
    for x_index in range(3):
        for y_index in range(3):
            sliding_window = padded_input[
                DILATION_STEP * x_index : DILATION_STEP * x_index + grid_extent[0],
                DILATION_STEP * y_index : DILATION_STEP * y_index + grid_extent[1],
            ]
            columns = jnp.concatenate(
                [
                    sliding_window[
                        :, :, DILATION_STEP * tap_index : DILATION_STEP * tap_index + grid_extent[2]
                    ].reshape(-1, channel_count)
                    for tap_index in range(3)
                ],
                axis=1,
            )
            partials.append(
                lax.dot_general(
                    columns, flat_grad, (((0,), (0,)), ((), ())), preferred_element_type=jnp.float32
                )
            )
    return jnp.stack(partials).reshape(27, channel_count, channel_count)


def data_terms(bordered_input, weights):
    channel_count = weights.shape[1]
    x_stretch = bordered_input.shape[0] - 2 * DILATION_STEP
    y_stretch = bordered_input.shape[1] - 2 * DILATION_STEP
    depth_cells = bordered_input.shape[2]
    padded_input = padding_depth(bordered_input, DILATION_STEP)
    stacked = jnp.transpose(weights, (0, 2, 1)).reshape(9, 3 * channel_count, channel_count)
    running = jnp.zeros((x_stretch * y_stretch * depth_cells, channel_count), jnp.float32)
    for x_index in range(3):
        for y_index in range(3):
            sliding_window = padded_input[
                DILATION_STEP * (2 - x_index) : DILATION_STEP * (2 - x_index) + x_stretch,
                DILATION_STEP * (2 - y_index) : DILATION_STEP * (2 - y_index) + y_stretch,
            ]
            columns = jnp.concatenate(
                [
                    sliding_window[
                        :,
                        :,
                        DILATION_STEP * (2 - tap_index) : DILATION_STEP * (2 - tap_index)
                        + depth_cells,
                    ].reshape(-1, channel_count)
                    for tap_index in range(3)
                ],
                axis=1,
            )
            running = running + jnp.dot(
                columns, stacked[x_index * 3 + y_index], preferred_element_type=jnp.float32
            )
    return running.reshape(x_stretch, y_stretch, depth_cells, channel_count)


def body(input_activation, pre_one, pre_two, w_one, w_two, w_trans, keep_mask, out_grad):
    channel_count = w_one.shape[1]
    x_stretch, y_stretch, joined_layout = input_activation.shape
    depth_cells = joined_layout // channel_count
    width_t = w_trans.shape[0]
    factor = 1.0 / math.sqrt(
        x_stretch * lax.axis_size("gx") * y_stretch * lax.axis_size("gy") * depth_cells
    )
    blocks = jnp.repeat(
        jnp.repeat(keep_mask.astype(jnp.bfloat16), channel_count, axis=0), channel_count, axis=1
    )
    w_kept = w_trans * blocks
    regrouped = lax.all_to_all(out_grad, "gx", split_axis=0, concat_axis=3, tiled=True)
    grad_rows = regrouped.reshape(-1, width_t)
    back_blocks = lax.dot_general(
        grad_rows, w_kept, (((1,), (1,)), ((), ())), preferred_element_type=jnp.float32
    ).astype(jnp.bfloat16)
    act_two = split_layout(jnp.maximum(pre_two, 0), channel_count)
    two_rows = to_blocks(act_two).reshape(-1, width_t)
    trans_term = (
        lax.dot_general(
            two_rows, grad_rows, (((0,), (0,)), ((), ())), preferred_element_type=jnp.float32
        )
        * blocks.astype(jnp.float32)
        * factor
    )
    grad_w_trans = lax.psum(trans_term, ("gx", "gy"))
    back_two = from_blocks(
        back_blocks.reshape(x_stretch // 2, y_stretch // 2, depth_cells // 2, width_t),
        channel_count,
    )
    back_two = jnp.where(
        split_layout(pre_two, channel_count) > 0, back_two, jnp.zeros_like(back_two)
    )
    first_activation = jnp.maximum(pre_one, 0)
    bordered_input = padded(
        jnp.concatenate([input_activation, first_activation], axis=2),
        (("gx", 0), ("gy", 1)),
        DILATION_STEP,
    )
    in_rim = split_layout(bordered_input[:, :, :joined_layout], channel_count)
    one_rim = split_layout(bordered_input[:, :, joined_layout:], channel_count)
    two_term = weight_terms(one_rim, back_two) * factor
    flattened_backward = back_two.reshape(x_stretch, y_stretch, joined_layout)
    narrowed_slice = split_layout(
        padded(flattened_backward, (("gx", 0), ("gy", 1)), DILATION_STEP), channel_count
    )
    first_backward = data_terms(narrowed_slice, w_two)
    first_backward = jnp.where(
        split_layout(pre_one, channel_count) > 0, first_backward, jnp.zeros_like(first_backward)
    ).astype(jnp.bfloat16)
    one_grad_rim = split_layout(
        padded(
            first_backward.reshape(x_stretch, y_stretch, joined_layout),
            (("gx", 0), ("gy", 1)),
            DILATION_STEP,
        ),
        channel_count,
    )
    grad_w_two = lax.psum(two_term, ("gx", "gy"))
    one_term = weight_terms(in_rim, first_backward) * factor
    grad_w_one = lax.psum(one_term, ("gx", "gy"))
    grad_in = (
        data_terms(one_grad_rim, w_one)
        .astype(jnp.bfloat16)
        .reshape(x_stretch, y_stretch, joined_layout)
    )
    return (grad_in, grad_w_one, grad_w_two, grad_w_trans)


def call(kernel, out_shape, scratch, flops, limit, *args, out_space=VMEM, aliases={}):
    spec = []
    for a in args:
        if isinstance(a, tuple):
            spec.append(pl.BlockSpec(memory_space=pltpu.MemorySpace.HBM))
        elif a.dtype == jnp.int32:
            spec.append(pl.BlockSpec(memory_space=SMEM))
        else:
            spec.append(pl.BlockSpec(memory_space=VMEM))
    arrays = [a[0] if isinstance(a, tuple) else a for a in args]
    return pl.pallas_call(
        kernel,
        out_shape=out_shape,
        in_specs=spec,
        out_specs=jax.tree.map(lambda _: pl.BlockSpec(memory_space=out_space), out_shape),
        scratch_shapes=scratch,
        input_output_aliases=aliases,
        cost_estimate=pl.CostEstimate(
            flops=flops,
            transcendentals=0,
            bytes_accessed=sum(a.size * a.dtype.itemsize for a in arrays) if flops else 0,
        ),
        compiler_params=pltpu.CompilerParams(vmem_limit_bytes=limit * 1024 * 1024),
    )(*arrays)


def fetch(pairs, sems):
    copies = [pltpu.make_async_copy(src, dst, sems.at[k]) for k, (src, dst) in enumerate(pairs)]
    for copy in copies:
        copy.start()
    return copies


def pack_kernel(og, two, one, act, first_ref, og_v, two_v, one_v, act_v, turn_ref, sems):
    copies = fetch(((og, og_v), (two, two_v), (one, one_v), (act, act_v)), sems)
    copies[0].wait()
    first_ref[0:256] = og_v[...].astype(F32).reshape(256, 128).astype(BF16)
    for k, (ref, at) in enumerate(((two_v, 256), (one_v, 512), (act_v, 768))):
        copies[k + 1].wait()
        for x in range(4):
            for t in range(8):
                turn_ref[k, pl.ds(64 * x + t, 8, stride=8), :] = ref[x, :, 128 * t : 128 * t + 128].astype(F32)
        first_ref[at : at + 256] = turn_ref[k].astype(BF16)


def weight_kernel(wt, keep, w2, w1, kept_ref, mask_ref, d2_ref, d1_ref, wt_v, keep_v, w2_v, w1_v, sems):
    copies = fetch(((keep, keep_v), (wt, wt_v), (w2, w2_v), (w1, w1_v)), sems)
    copies[0].wait()
    width = wt_v.shape[0]
    blocks = keep_v.shape[0]
    side = width // blocks
    left = (
        lax.broadcasted_iota(jnp.int32, (width, blocks), 0) // side
        == lax.broadcasted_iota(jnp.int32, (width, blocks), 1)
    ).astype(BF16)
    right = (
        lax.broadcasted_iota(jnp.int32, (blocks, width), 1) // side
        == lax.broadcasted_iota(jnp.int32, (blocks, width), 0)
    ).astype(BF16)
    wide = jnp.dot(keep_v[...].astype(F32).astype(BF16), right, preferred_element_type=F32).astype(BF16)
    mask = jnp.dot(left, wide, preferred_element_type=F32)
    mask_ref[...] = mask.astype(BF16)
    copies[1].wait()
    kept_ref[...] = (wt_v[...].astype(F32) * mask).astype(BF16)
    none = jnp.zeros((64, 64), BF16)
    for k, (ref, out) in enumerate(((w2_v, d2_ref), (w1_v, d1_ref))):
        copies[k + 2].wait()
        for tap in range(27):
            w = ref[tap]
            at = 128 * (tap % 3)
            out[tap // 3, 0:64, at : at + 128] = jnp.concatenate([w, none], axis=1)
            out[tap // 3, 64:128, at : at + 128] = jnp.concatenate([none, w], axis=1)


def transition_kernel(
    factor, at_ref, a0, a1, a2, a3, kept_ref, mask_ref, back_ref, one_ref, chip_ref, cross_ref, mine_ref, send_ref, og_ref, two_ref
):
    me = at_ref[0]
    parts = (a0, a1, a2, a3)
    n = len(parts)
    for s, part in enumerate(parts):
        src = lax.rem(me + n - s, n)
        og_ref[src] = part[0:256]
        spot = pl.ds(src * 4, 4)
        two_ref[spot] = part[256:512].reshape(4, 64, 128)
        one_ref[spot] = part[512:768].reshape(4, 64, 128)
    og = jnp.concatenate([og_ref[j] for j in range(n)], axis=1)
    back = lax.dot_general(og, kept_ref[...], (((1,), (1,)), ((), ())), preferred_element_type=F32)
    two = two_ref[...].astype(F32).reshape(8, 2, 4, 2, 8, 128)
    cells = []
    for p in range(2):
        halves = []
        for q in range(2):
            pre = two[:, p, :, q]
            at = (p * 2 + q) * 128
            grad = back[:, at : at + 128].reshape(8, 4, 8, 128)
            halves.append(jnp.where(pre > 0, grad, 0.0))
            cells.append(jnp.maximum(pre, 0.0).reshape(256, 128).astype(BF16))
        back_ref[:, p] = jnp.stack(halves, axis=2).reshape(8, 64, 128).astype(BF16)

    def rim(high, ref):
        at = 32 if high else 0
        ref[:, :, 0:32] = back_ref[:, :, at : at + 32]
        at = 48 if high else 0
        ref[:, :, 32:48] = one_ref[:, at : at + 16].reshape(8, 2, 16, 128)

    share(at_ref[1], rim, cross_ref, chip_ref)
    flat = jnp.concatenate(cells, axis=1)
    trans = lax.dot_general(flat, og, (((0,), (0,)), ((), ())), preferred_element_type=F32)
    trans = trans * mask_ref[...].astype(F32) * factor

    def emit(half, ref):
        for m in range(4):
            ref[256 * m : 256 * m + 256] = trans[256 * half : 256 * half + 256, 128 * m : 128 * m + 128].astype(ref.dtype)

    share(at_ref[1], emit, mine_ref, send_ref)


def share(core, emit, mine_ref, send_ref):
    @pl.when(core == 0)
    def _():
        emit(0, mine_ref)
        emit(1, send_ref)

    @pl.when(core != 0)
    def _():
        emit(1, mine_ref)
        emit(0, send_ref)


def triple(v):
    x, rows, _ = v.shape
    flat = v.reshape(x * rows, 128)
    t = lax.broadcasted_iota(jnp.int32, flat.shape, 0) % 8
    later = jnp.where(t == 7, 0.0, pltpu.roll(flat, x * rows - 1, 0))
    earlier = jnp.where(t == 0, 0.0, pltpu.roll(flat, 1, 0))
    wide = jnp.concatenate([later, flat, earlier], axis=1)
    return wide.astype(BF16).reshape(x, rows, 384)


def fold(sums, factor):
    lane = lax.broadcasted_iota(jnp.int32, (64, 128), 1)
    taps = []
    for g in sums:
        for l in range(3):
            if g is None:
                taps.append(jnp.zeros((64, 128), F32))
                continue
            part = g[:, l * 128 : (l + 1) * 128]
            f = jnp.where(lane < 64, part[0:64], part[64:128])
            taps.append((f + pltpu.roll(f, 64, 1)) * factor)
    taps.append(taps[-1])
    return [jnp.where(lane < 64, taps[2 * m], taps[2 * m + 1]) for m in range(14)]


def apply_taps(rows, taps):
    return lax.dot_general(rows, taps, (((1,), (1,)), ((), ())), preferred_element_type=F32)


def weight_sums(act, wide_ref, act_ref):
    act_ref[0:128] = jnp.zeros((128, 128), F32)
    act_ref[128:1152] = act.reshape(1024, 128)
    act_ref[1152:1280] = jnp.zeros((128, 128), F32)
    turned = act_ref[...].T.astype(BF16)
    stacked = jnp.concatenate([turned[:, 128 * i : 128 * i + 1024] for i in range(3)], axis=0)
    sums = [None] * 9
    for j in range(3):
        rows = wide_ref[2:18, 32 - 16 * j : 96 - 16 * j].reshape(1024, 384)
        part = jnp.dot(stacked, rows, preferred_element_type=F32)
        for i in range(3):
            sums[i * 3 + j] = part[128 * i : 128 * i + 128]
    return sums


def own_kernel(factor, back_ref, one_ref, w_ref, acc_ref, sums_ref, wide_ref, act_ref):
    wide_ref[2:18, 0:16] = jnp.zeros((16, 16, 384), BF16)
    wide_ref[2:18, 80:96] = jnp.zeros((16, 16, 384), BF16)
    wide_ref[2:18, 16:80] = triple(back_ref[...].astype(F32))
    acc_ref[...] = jnp.zeros((16, 96, 128), F32)
    rows = wide_ref[2:18, 16:80].reshape(1024, 384)
    for j in range(3):
        taps = jnp.concatenate([w_ref[i * 3 + j] for i in range(3)], axis=0)
        part = apply_taps(rows, taps).reshape(16, 64, 384)
        ys = slice(16 * j, 16 * j + 64)
        acc_ref[0:14, ys] += part[2:16, :, 0:128]
        acc_ref[:, ys] += part[:, :, 128:256]
        acc_ref[2:16, ys] += part[0:14, :, 256:384]
    sums = weight_sums(jnp.maximum(one_ref[...].astype(F32), 0.0), wide_ref, act_ref)
    for m, block in enumerate(fold(sums, factor)):
        sums_ref[64 * m : 64 * m + 64] = block


def conv_kernel(
    factor, at_ref, acc_ref, sums_ref, one_ref, chip_ref, cross_ref, w_ref, i0, i1, i2, i3,
    mine_ref, send_ref, outer_ref, rim_ref, wide_ref, in_ref, first_ref, act_ref,
):
    me = at_ref[0]
    parts = (i0, i1, i2, i3)
    n = len(parts)
    for s, part in enumerate(parts):
        in_ref[pl.ds(lax.rem(me + n - s, n) * 4, 4)] = part[768:1024].reshape(4, 64, 128)

    def put(side, ref):
        rim_ref[side] = ref[...]

    share(at_ref[1], put, cross_ref, chip_ref)
    wide_ref[:, 0:2] = jnp.zeros((2, 2, 32, 384), BF16)
    wide_ref[:, 18:20] = jnp.zeros((2, 2, 32, 384), BF16)
    outer_ref[0:2] = jnp.zeros((2, 96, 384), BF16)
    outer_ref[18:20] = jnp.zeros((2, 96, 384), BF16)
    for side in range(2):
        wide_ref[side, 2:18] = triple(rim_ref[side, :, 0:32].astype(F32))
    first_ref[...] = acc_ref[...]
    act = jnp.maximum(one_ref[...].astype(F32), 0.0)
    sums = [None] * 9
    for side in range(2):
        j = 2 - 2 * side
        near = 16 - 16 * side
        own = 48 * side
        turned = act[:, own : own + 16].reshape(256, 128).T.astype(BF16)
        far = jnp.zeros((512, 128), F32)
        close = jnp.zeros((256, 128), F32)
        for i in range(3):
            xs = slice(4 - 2 * i, 20 - 2 * i)
            rows = wide_ref[side, xs, near : near + 16].reshape(256, 384)
            far += apply_taps(wide_ref[side, xs].reshape(512, 384), w_ref[i * 3 + j])
            close += apply_taps(rows, w_ref[i * 3 + 1])
            sums[i * 3 + j] = jnp.dot(turned, rows, preferred_element_type=F32)
        first_ref[:, 64 * side : 64 * side + 32] += far.reshape(16, 32, 128)
        first_ref[:, 80 * side : 80 * side + 16] += close.reshape(16, 16, 128)
    second = fold(sums, factor)
    pre = jnp.concatenate([rim_ref[0, :, 32:48], one_ref[...], rim_ref[1, :, 32:48]], axis=1).astype(F32)
    outer_ref[2:18] = triple(jnp.where(pre > 0, first_ref[...], 0.0))
    first = fold(weight_sums(in_ref[...].astype(F32), outer_ref, act_ref), factor)

    def emit(half, ref):
        for m in range(7):
            ref[64 * m : 64 * m + 64] = first[7 * half + m].astype(ref.dtype)
            at = 448 * half + 64 * m
            block = second[7 * half + m] + sums_ref[at : at + 64]
            ref[448 + 64 * m : 512 + 64 * m] = block.astype(ref.dtype)

    share(at_ref[1], emit, mine_ref, send_ref)


def grad_kernel(at_ref, outer_ref, w_ref, grad_ref, turn_ref):
    grad = jnp.zeros((256, 128), F32)
    for i in range(3):
        for j in range(3):
            mine = outer_ref[pl.ds(at_ref[0] * 4 + 4 - 2 * i, 4), 32 - 16 * j : 96 - 16 * j].reshape(256, 384)
            grad += apply_taps(mine, w_ref[i * 3 + j])
    turn_ref[...] = grad
    for x in range(4):
        for t in range(8):
            grad_ref[x, :, 128 * t : 128 * t + 128] = turn_ref[pl.ds(64 * x + t, 8, stride=8), :].astype(BF16)


def spread(half, ref, hbm_refs, refs, sems):
    copies = []
    count = 14 - half
    for k, (hbm, out) in enumerate(zip(hbm_refs, refs)):
        for m in range(7):
            block = ref[448 * k + 64 * m : 448 * k + 64 * m + 64].astype(F32)
            out[2 * m] = block[:, 0:64]
            out[2 * m + 1] = block[:, 64:128]
        copies.append(
            pltpu.make_async_copy(out.at[0:count], hbm.at[14 * half : 14 * half + count], sems.at[k])
        )
        copies[-1].start()
    for copy in copies:
        copy.wait()


def half_kernel(at_ref, ref, one_hbm, two_hbm, one_ref, two_ref, sems):
    @pl.when(at_ref[1] == 0)
    def _():
        spread(0, ref, (one_hbm, two_hbm), (one_ref, two_ref), sems)

    @pl.when(at_ref[1] != 0)
    def _():
        spread(1, ref, (one_hbm, two_hbm), (one_ref, two_ref), sems)


def rest_kernel(at_ref, ref, one_in, two_in, one_hbm, two_hbm, one_ref, two_ref, sems):
    @pl.when(at_ref[1] == 0)
    def _():
        spread(1, ref, (one_hbm, two_hbm), (one_ref, two_ref), sems)

    @pl.when(at_ref[1] != 0)
    def _():
        spread(0, ref, (one_hbm, two_hbm), (one_ref, two_ref), sems)


def trans_kernel(at_ref, mine_ref, other_ref, trans_ref):
    def emit(half, ref):
        for m in range(4):
            trans_ref[256 * half : 256 * half + 256, 128 * m : 128 * m + 128] = ref[256 * m : 256 * m + 256].astype(F32)

    share(at_ref[1], emit, mine_ref, other_ref)


def rotate(value, axis, step):
    n = lax.axis_size(axis)
    return lax.ppermute(value, axis, [(i, (i + step) % n) for i in range(n)])


def swap(value, axis, bit):
    n = lax.axis_size(axis)
    return lax.ppermute(value, axis, [(i, i ^ bit) for i in range(n)])


def on_chip(mine, send):
    return (mine + swap(send, "gy", 1).astype(F32)).astype(BF16)


def across(mine):
    return mine.astype(F32) + swap(mine, "gy", 2).astype(F32)


def slab_body(input_activation, pre_one, pre_two, w_one, w_two, w_trans, keep_mask, out_grad):
    factor = 1.0 / math.sqrt(
        input_activation.shape[0] * 4 * input_activation.shape[1] * 4 * (input_activation.shape[2] // 64)
    )
    at = jnp.stack([lax.axis_index("gx"), lax.rem(lax.axis_index("gy"), 2)]).astype(jnp.int32)
    shape = jax.ShapeDtypeStruct
    vmem = pltpu.VMEM
    natural = vmem((4, 8, 1024), BF16)
    first = call(
        pack_kernel,
        shape((1024, 128), BF16),
        [
            vmem((8, 4, 8, 128), BF16), natural, natural, natural, vmem((3, 256, 128), F32),
            pltpu.SemaphoreType.DMA((4,)),
        ],
        0,
        56,
        (out_grad,),
        (pre_two,),
        (pre_one,),
        (input_activation,),
    )
    firsts = [first] + [rotate(first, "gx", s) for s in (1, 2, 3)]
    kept, mask, d2, d1 = call(
        weight_kernel,
        (
            shape((512, 512), BF16), shape((512, 512), BF16),
            shape((9, 128, 384), BF16), shape((9, 128, 384), BF16),
        ),
        [
            vmem((512, 512), BF16), vmem((8, 8), jnp.int32),
            vmem((27, 64, 64), BF16), vmem((27, 64, 64), BF16),
            pltpu.SemaphoreType.DMA((4,)),
        ],
        10**7,
        8,
        (w_trans,),
        (keep_mask,),
        (w_two,),
        (w_one,),
    )
    back, one, chip, cross, tmine, tsend = call(
        functools.partial(transition_kernel, factor),
        (
            shape((8, 2, 64, 128), BF16),
            shape((16, 64, 128), BF16),
            shape((8, 2, 48, 128), BF16),
            shape((8, 2, 48, 128), BF16),
            shape((1024, 128), F32),
            shape((1024, 128), BF16),
        ),
        [vmem((4, 256, 128), BF16), vmem((16, 64, 128), BF16)],
        4 * 256 * 512 * 512,
        12,
        at,
        *firsts,
        kept,
        mask,
    )
    n = lax.axis_size("gy")
    pairs = [(i, i + 1) for i in range(1, n - 1, 2)]
    cross = lax.ppermute(cross, "gy", pairs + [(j, i) for i, j in pairs])
    chip = swap(chip, "gy", 1)
    tmine = on_chip(tmine, tsend)
    one, tmine = lax.optimization_barrier((one, tmine))
    acc, sums = call(
        functools.partial(own_kernel, factor),
        (shape((16, 96, 128), F32), shape((896, 128), F32)),
        [vmem((20, 96, 384), BF16), vmem((1280, 128), F32)],
        2 * 128 * 3456 * 2048,
        16,
        back.reshape(16, 64, 128),
        one,
        d2,
    )
    tmine = across(tmine)
    mine, send, outer = call(
        functools.partial(conv_kernel, factor),
        (shape((896, 128), F32), shape((896, 128), BF16), shape((20, 96, 384), BF16)),
        [
            vmem((2, 16, 48, 128), BF16),
            vmem((2, 20, 32, 384), BF16),
            vmem((16, 64, 128), BF16),
            vmem((16, 96, 128), F32),
            vmem((1280, 128), F32),
        ],
        2 * 128 * 3456 * 900,
        20,
        at,
        acc,
        sums,
        one,
        chip.reshape(16, 48, 128),
        cross.reshape(16, 48, 128),
        d2,
        *firsts,
    )
    send, tmine = lax.optimization_barrier((send, tmine))
    mine = on_chip(mine, send)
    away = swap(mine, "gy", 2)
    tother = swap(tmine, "gy", 1)
    grad_w_trans = call(trans_kernel, shape((512, 512), F32), [], 10**7, 6, at, tmine, tother)
    grad_in = call(
        grad_kernel, shape((4, 8, 1024), BF16), [vmem((256, 128), F32)], 2 * 128 * 3456 * 256, 12, at, outer, d1
    )
    away, grad_w_trans, grad_in = lax.optimization_barrier((away, grad_w_trans, grad_in))
    mine = (mine.astype(F32) + away.astype(F32)).astype(BF16)
    other = swap(mine, "gy", 1)
    taps = shape((27, 64, 64), F32)
    scratch = [vmem((14, 64, 64), F32), vmem((14, 64, 64), F32), pltpu.SemaphoreType.DMA((2,))]
    hbm = pltpu.MemorySpace.HBM
    grad_w_one, grad_w_two = call(half_kernel, (taps, taps), scratch, 10**8, 6, at, mine, out_space=hbm)
    grad_w_one, grad_w_two = call(
        rest_kernel,
        (taps, taps),
        scratch,
        0,
        6,
        at,
        other,
        (grad_w_one,),
        (grad_w_two,),
        out_space=hbm,
        aliases={2: 0, 3: 1},
    )
    return (grad_in, grad_w_one, grad_w_two, grad_w_trans)


def solution(mesh):
    fits = mesh.shape["gx"] == 4 and mesh.shape["gy"] == 4

    def pick(*args):
        shapes = tuple(a.shape for a in args)
        known = (
            ((4, 8, 1024),) * 3 + ((27, 64, 64),) * 2 + ((512, 512), (8, 8), (8, 4, 8, 128))
        )
        return (slab_body if fits and shapes == known else body)(*args)

    return jax.shard_map(
        pick,
        mesh=mesh,
        in_specs=(
            P(("grp", "gx"), "gy", None),
            P(("grp", "gx"), "gy", None),
            P(("grp", "gx"), "gy", None),
            P(),
            P(),
            P(),
            P(),
            P("grp", "gy", None, "gx"),
        ),
        out_specs=(
            P(("grp", "gx"), "gy", None),
            P("grp", None, None),
            P("grp", None, None),
            P("grp", None),
        ),
        check_vma=False,
    )
```

```python
import functools
import math

import jax
import jax.numpy as jnp
from jax import lax
from jax.experimental import pallas as pl
from jax.experimental.pallas import tpu as pltpu
from jax.sharding import PartitionSpec as P

DILATION_STEP = 2
VMEM = pltpu.MemorySpace.VMEM
SMEM = pltpu.MemorySpace.SMEM
F32 = jnp.float32
BF16 = jnp.bfloat16


def padded(cells, sides, width):
    for axis, dim in sides:
        count = lax.axis_size(axis)
        ends = count - 1
        head = lax.slice_in_dim(cells, 0, width, axis=dim)
        tail = lax.slice_in_dim(cells, cells.shape[dim] - width, cells.shape[dim], axis=dim)
        cells = jnp.concatenate(
            [
                lax.ppermute(tail, axis, [(i, (i + 1) % count) for i in range(ends)]),
                cells,
                lax.ppermute(head, axis, [((i + 1) % count, i) for i in range(ends)]),
            ],
            axis=dim,
        )
    return cells


def split_layout(joined_layout, channel_count):
    return joined_layout.reshape(joined_layout.shape[0], joined_layout.shape[1], -1, channel_count)


def to_blocks(cube_volume):
    shape_all = cube_volume.shape
    parted = cube_volume.reshape(
        shape_all[0] // 2, 2, shape_all[1] // 2, 2, shape_all[2] // 2, 2, shape_all[3]
    )
    parted = parted.transpose(0, 2, 4, 1, 3, 5, 6)
    return parted.reshape(shape_all[0] // 2, shape_all[1] // 2, shape_all[2] // 2, 8 * shape_all[3])


def from_blocks(blocked, channel_count):
    shape_all = blocked.shape
    parted = blocked.reshape(shape_all[0], shape_all[1], shape_all[2], 2, 2, 2, channel_count)
    parted = parted.transpose(0, 3, 1, 4, 2, 5, 6)
    return parted.reshape(2 * shape_all[0], 2 * shape_all[1], 2 * shape_all[2], channel_count)


def padding_depth(cube_volume, margin):
    return jnp.pad(cube_volume, ((0, 0), (0, 0), (margin, margin), (0, 0)))


def weight_terms(bordered_input, upstream_gradient):
    channel_count = upstream_gradient.shape[3]
    grid_extent = upstream_gradient.shape
    padded_input = padding_depth(bordered_input, DILATION_STEP)
    flat_grad = upstream_gradient.reshape(-1, channel_count)
    partials = []
    for x_index in range(3):
        for y_index in range(3):
            sliding_window = padded_input[
                DILATION_STEP * x_index : DILATION_STEP * x_index + grid_extent[0],
                DILATION_STEP * y_index : DILATION_STEP * y_index + grid_extent[1],
            ]
            columns = jnp.concatenate(
                [
                    sliding_window[
                        :, :, DILATION_STEP * tap_index : DILATION_STEP * tap_index + grid_extent[2]
                    ].reshape(-1, channel_count)
                    for tap_index in range(3)
                ],
                axis=1,
            )
            partials.append(
                lax.dot_general(
                    columns, flat_grad, (((0,), (0,)), ((), ())), preferred_element_type=jnp.float32
                )
            )
    return jnp.stack(partials).reshape(27, channel_count, channel_count)


def data_terms(bordered_input, weights):
    channel_count = weights.shape[1]
    x_stretch = bordered_input.shape[0] - 2 * DILATION_STEP
    y_stretch = bordered_input.shape[1] - 2 * DILATION_STEP
    depth_cells = bordered_input.shape[2]
    padded_input = padding_depth(bordered_input, DILATION_STEP)
    stacked = jnp.transpose(weights, (0, 2, 1)).reshape(9, 3 * channel_count, channel_count)
    running = jnp.zeros((x_stretch * y_stretch * depth_cells, channel_count), jnp.float32)
    for x_index in range(3):
        for y_index in range(3):
            sliding_window = padded_input[
                DILATION_STEP * (2 - x_index) : DILATION_STEP * (2 - x_index) + x_stretch,
                DILATION_STEP * (2 - y_index) : DILATION_STEP * (2 - y_index) + y_stretch,
            ]
            columns = jnp.concatenate(
                [
                    sliding_window[
                        :,
                        :,
                        DILATION_STEP * (2 - tap_index) : DILATION_STEP * (2 - tap_index)
                        + depth_cells,
                    ].reshape(-1, channel_count)
                    for tap_index in range(3)
                ],
                axis=1,
            )
            running = running + jnp.dot(
                columns, stacked[x_index * 3 + y_index], preferred_element_type=jnp.float32
            )
    return running.reshape(x_stretch, y_stretch, depth_cells, channel_count)


def body(input_activation, pre_one, pre_two, w_one, w_two, w_trans, keep_mask, out_grad):
    channel_count = w_one.shape[1]
    x_stretch, y_stretch, joined_layout = input_activation.shape
    depth_cells = joined_layout // channel_count
    width_t = w_trans.shape[0]
    factor = 1.0 / math.sqrt(
        x_stretch * lax.axis_size("gx") * y_stretch * lax.axis_size("gy") * depth_cells
    )
    blocks = jnp.repeat(
        jnp.repeat(keep_mask.astype(jnp.bfloat16), channel_count, axis=0), channel_count, axis=1
    )
    w_kept = w_trans * blocks
    regrouped = lax.all_to_all(out_grad, "gx", split_axis=0, concat_axis=3, tiled=True)
    grad_rows = regrouped.reshape(-1, width_t)
    back_blocks = lax.dot_general(
        grad_rows, w_kept, (((1,), (1,)), ((), ())), preferred_element_type=jnp.float32
    ).astype(jnp.bfloat16)
    act_two = split_layout(jnp.maximum(pre_two, 0), channel_count)
    two_rows = to_blocks(act_two).reshape(-1, width_t)
    trans_term = (
        lax.dot_general(
            two_rows, grad_rows, (((0,), (0,)), ((), ())), preferred_element_type=jnp.float32
        )
        * blocks.astype(jnp.float32)
        * factor
    )
    grad_w_trans = lax.psum(trans_term, ("gx", "gy"))
    back_two = from_blocks(
        back_blocks.reshape(x_stretch // 2, y_stretch // 2, depth_cells // 2, width_t),
        channel_count,
    )
    back_two = jnp.where(
        split_layout(pre_two, channel_count) > 0, back_two, jnp.zeros_like(back_two)
    )
    first_activation = jnp.maximum(pre_one, 0)
    bordered_input = padded(
        jnp.concatenate([input_activation, first_activation], axis=2),
        (("gx", 0), ("gy", 1)),
        DILATION_STEP,
    )
    in_rim = split_layout(bordered_input[:, :, :joined_layout], channel_count)
    one_rim = split_layout(bordered_input[:, :, joined_layout:], channel_count)
    two_term = weight_terms(one_rim, back_two) * factor
    flattened_backward = back_two.reshape(x_stretch, y_stretch, joined_layout)
    narrowed_slice = split_layout(
        padded(flattened_backward, (("gx", 0), ("gy", 1)), DILATION_STEP), channel_count
    )
    first_backward = data_terms(narrowed_slice, w_two)
    first_backward = jnp.where(
        split_layout(pre_one, channel_count) > 0, first_backward, jnp.zeros_like(first_backward)
    ).astype(jnp.bfloat16)
    one_grad_rim = split_layout(
        padded(
            first_backward.reshape(x_stretch, y_stretch, joined_layout),
            (("gx", 0), ("gy", 1)),
            DILATION_STEP,
        ),
        channel_count,
    )
    grad_w_two = lax.psum(two_term, ("gx", "gy"))
    one_term = weight_terms(in_rim, first_backward) * factor
    grad_w_one = lax.psum(one_term, ("gx", "gy"))
    grad_in = (
        data_terms(one_grad_rim, w_one)
        .astype(jnp.bfloat16)
        .reshape(x_stretch, y_stretch, joined_layout)
    )
    return (grad_in, grad_w_one, grad_w_two, grad_w_trans)


def call(kernel, out_shape, scratch, flops, limit, *args, out_space=VMEM, aliases={}):
    spec = []
    for a in args:
        if isinstance(a, tuple):
            spec.append(pl.BlockSpec(memory_space=pltpu.MemorySpace.HBM))
        elif a.dtype == jnp.int32:
            spec.append(pl.BlockSpec(memory_space=SMEM))
        else:
            spec.append(pl.BlockSpec(memory_space=VMEM))
    arrays = [a[0] if isinstance(a, tuple) else a for a in args]
    return pl.pallas_call(
        kernel,
        out_shape=out_shape,
        in_specs=spec,
        out_specs=jax.tree.map(lambda _: pl.BlockSpec(memory_space=out_space), out_shape),
        scratch_shapes=scratch,
        input_output_aliases=aliases,
        cost_estimate=pl.CostEstimate(
            flops=flops,
            transcendentals=0,
            bytes_accessed=sum(a.size * a.dtype.itemsize for a in arrays) if flops else 0,
        ),
        compiler_params=pltpu.CompilerParams(vmem_limit_bytes=limit * 1024 * 1024),
    )(*arrays)


def fetch(pairs, sems):
    copies = [pltpu.make_async_copy(src, dst, sems.at[k]) for k, (src, dst) in enumerate(pairs)]
    for copy in copies:
        copy.start()
    return copies


def pack_kernel(og, two, one, act, first_ref, second_ref, og_v, two_v, one_v, act_v, turn_ref, sems):
    copies = fetch(((og, og_v), (two, two_v), (one, one_v), (act, act_v)), sems)
    copies[0].wait()
    first_ref[0:256] = og_v[...].astype(F32).reshape(256, 128).astype(BF16)
    for k, (ref, out, at) in enumerate(((two_v, first_ref, 256), (one_v, first_ref, 512), (act_v, second_ref, 0))):
        copies[k + 1].wait()
        for x in range(4):
            for t in range(8):
                turn_ref[k, pl.ds(64 * x + t, 8, stride=8), :] = ref[x, :, 128 * t : 128 * t + 128].astype(F32)
        out[at : at + 256] = turn_ref[k].astype(BF16)


def weight_kernel(wt, keep, w2, w1, kept_ref, mask_ref, d2_ref, d1_ref, wt_v, keep_v, w2_v, w1_v, sems):
    copies = fetch(((keep, keep_v), (wt, wt_v), (w2, w2_v), (w1, w1_v)), sems)
    copies[0].wait()
    width = wt_v.shape[0]
    blocks = keep_v.shape[0]
    side = width // blocks
    left = (
        lax.broadcasted_iota(jnp.int32, (width, blocks), 0) // side
        == lax.broadcasted_iota(jnp.int32, (width, blocks), 1)
    ).astype(BF16)
    right = (
        lax.broadcasted_iota(jnp.int32, (blocks, width), 1) // side
        == lax.broadcasted_iota(jnp.int32, (blocks, width), 0)
    ).astype(BF16)
    wide = jnp.dot(keep_v[...].astype(F32).astype(BF16), right, preferred_element_type=F32).astype(BF16)
    mask = jnp.dot(left, wide, preferred_element_type=F32)
    mask_ref[...] = mask.astype(BF16)
    copies[1].wait()
    kept_ref[...] = (wt_v[...].astype(F32) * mask).astype(BF16)
    none = jnp.zeros((64, 64), BF16)
    for k, (ref, out) in enumerate(((w2_v, d2_ref), (w1_v, d1_ref))):
        copies[k + 2].wait()
        for tap in range(27):
            w = ref[tap]
            at = 128 * (tap % 3)
            out[tap // 3, 0:64, at : at + 128] = jnp.concatenate([w, none], axis=1)
            out[tap // 3, 64:128, at : at + 128] = jnp.concatenate([none, w], axis=1)


def transition_kernel(
    factor, at_ref, a0, a1, a2, a3, kept_ref, mask_ref, back_ref, one_ref, chip_ref, cross_ref, mine_ref, send_ref, og_ref, two_ref
):
    me = at_ref[0]
    parts = (a0, a1, a2, a3)
    n = len(parts)
    for s, part in enumerate(parts):
        src = lax.rem(me + n - s, n)
        og_ref[src] = part[0:256]
        spot = pl.ds(src * 4, 4)
        two_ref[spot] = part[256:512].reshape(4, 64, 128)
        one_ref[spot] = part[512:768].reshape(4, 64, 128)
    og = jnp.concatenate([og_ref[j] for j in range(n)], axis=1)
    back = lax.dot_general(og, kept_ref[...], (((1,), (1,)), ((), ())), preferred_element_type=F32)
    two = two_ref[...].astype(F32).reshape(8, 2, 4, 2, 8, 128)
    cells = []
    for p in range(2):
        halves = []
        for q in range(2):
            pre = two[:, p, :, q]
            at = (p * 2 + q) * 128
            grad = back[:, at : at + 128].reshape(8, 4, 8, 128)
            halves.append(jnp.where(pre > 0, grad, 0.0))
            cells.append(jnp.maximum(pre, 0.0).reshape(256, 128).astype(BF16))
        back_ref[:, p] = jnp.stack(halves, axis=2).reshape(8, 64, 128).astype(BF16)

    def rim(high, ref):
        at = 32 if high else 0
        ref[:, :, 0:32] = back_ref[:, :, at : at + 32]
        at = 48 if high else 0
        ref[:, :, 32:48] = one_ref[:, at : at + 16].reshape(8, 2, 16, 128)

    share(at_ref[1], rim, cross_ref, chip_ref)
    flat = jnp.concatenate(cells, axis=1)
    trans = lax.dot_general(flat, og, (((0,), (0,)), ((), ())), preferred_element_type=F32)
    trans = trans * mask_ref[...].astype(F32) * factor

    def emit(half, ref):
        for m in range(4):
            ref[256 * m : 256 * m + 256] = trans[256 * half : 256 * half + 256, 128 * m : 128 * m + 128].astype(ref.dtype)

    share(at_ref[1], emit, mine_ref, send_ref)


def share(core, emit, mine_ref, send_ref):
    @pl.when(core == 0)
    def _():
        emit(0, mine_ref)
        emit(1, send_ref)

    @pl.when(core != 0)
    def _():
        emit(1, mine_ref)
        emit(0, send_ref)


def triple(v):
    x, rows, _ = v.shape
    flat = v.reshape(x * rows, 128)
    t = lax.broadcasted_iota(jnp.int32, flat.shape, 0) % 8
    later = jnp.where(t == 7, 0.0, pltpu.roll(flat, x * rows - 1, 0))
    earlier = jnp.where(t == 0, 0.0, pltpu.roll(flat, 1, 0))
    wide = jnp.concatenate([later, flat, earlier], axis=1)
    return wide.astype(BF16).reshape(x, rows, 384)


def fold(sums, factor):
    lane = lax.broadcasted_iota(jnp.int32, (64, 128), 1)
    taps = []
    for g in sums:
        for l in range(3):
            if g is None:
                taps.append(jnp.zeros((64, 128), F32))
                continue
            part = g[:, l * 128 : (l + 1) * 128]
            f = jnp.where(lane < 64, part[0:64], part[64:128])
            taps.append((f + pltpu.roll(f, 64, 1)) * factor)
    taps.append(taps[-1])
    return [jnp.where(lane < 64, taps[2 * m], taps[2 * m + 1]) for m in range(14)]


def apply_taps(rows, taps):
    return lax.dot_general(rows, taps, (((1,), (1,)), ((), ())), preferred_element_type=F32)


def stack(act, act_ref):
    act_ref[0:128] = jnp.zeros((128, 128), F32)
    act_ref[128:1152] = act.reshape(1024, 128)
    act_ref[1152:1280] = jnp.zeros((128, 128), F32)
    turned = act_ref[...].T.astype(BF16)
    return jnp.concatenate([turned[:, 128 * i : 128 * i + 1024] for i in range(3)], axis=0)


def weight_sums(stacked, wide_ref):
    sums = [None] * 9
    for j in range(3):
        rows = wide_ref[2:18, 32 - 16 * j : 96 - 16 * j].reshape(1024, 384)
        part = jnp.dot(stacked, rows, preferred_element_type=F32)
        for i in range(3):
            sums[i * 3 + j] = part[128 * i : 128 * i + 128]
    return sums


def own_kernel(
    factor, at_ref, back_ref, one_ref, w_ref, i0, i1, i2, i3, acc_ref, sums_ref, stack_ref, wide_ref, act_ref, in_ref
):
    wide_ref[2:18, 0:16] = jnp.zeros((16, 16, 384), BF16)
    wide_ref[2:18, 80:96] = jnp.zeros((16, 16, 384), BF16)
    wide_ref[2:18, 16:80] = triple(back_ref[...].astype(F32))
    acc_ref[...] = jnp.zeros((16, 96, 128), F32)
    rows = wide_ref[2:18, 16:80].reshape(1024, 384)
    for j in range(3):
        taps = jnp.concatenate([w_ref[i * 3 + j] for i in range(3)], axis=0)
        part = apply_taps(rows, taps).reshape(16, 64, 384)
        ys = slice(16 * j, 16 * j + 64)
        acc_ref[0:14, ys] += part[2:16, :, 0:128]
        acc_ref[:, ys] += part[:, :, 128:256]
        acc_ref[2:16, ys] += part[0:14, :, 256:384]
    sums = weight_sums(stack(jnp.maximum(one_ref[...].astype(F32), 0.0), act_ref), wide_ref)
    for m, block in enumerate(fold(sums, factor)):
        sums_ref[64 * m : 64 * m + 64] = block
    me = at_ref[0]
    parts = (i0, i1, i2, i3)
    n = len(parts)
    for s, part in enumerate(parts):
        in_ref[pl.ds(lax.rem(me + n - s, n) * 4, 4)] = part[...].reshape(4, 64, 128)
    stack_ref[...] = stack(in_ref[...].astype(F32), act_ref)


def conv_kernel(
    factor, at_ref, acc_ref, sums_ref, one_ref, chip_ref, cross_ref, w_ref, stack_ref,
    mine_ref, send_ref, outer_ref, rim_ref, wide_ref, first_ref,
):

    def put(side, ref):
        rim_ref[side] = ref[...]

    share(at_ref[1], put, cross_ref, chip_ref)
    wide_ref[:, 0:2] = jnp.zeros((2, 2, 32, 384), BF16)
    wide_ref[:, 18:20] = jnp.zeros((2, 2, 32, 384), BF16)
    outer_ref[0:2] = jnp.zeros((2, 96, 384), BF16)
    outer_ref[18:20] = jnp.zeros((2, 96, 384), BF16)
    for side in range(2):
        wide_ref[side, 2:18] = triple(rim_ref[side, :, 0:32].astype(F32))
    first_ref[...] = acc_ref[...]
    act = jnp.maximum(one_ref[...].astype(F32), 0.0)
    sums = [None] * 9
    for side in range(2):
        j = 2 - 2 * side
        near = 16 - 16 * side
        own = 48 * side
        turned = act[:, own : own + 16].reshape(256, 128).T.astype(BF16)
        far = jnp.zeros((512, 128), F32)
        close = jnp.zeros((256, 128), F32)
        for i in range(3):
            xs = slice(4 - 2 * i, 20 - 2 * i)
            rows = wide_ref[side, xs, near : near + 16].reshape(256, 384)
            far += apply_taps(wide_ref[side, xs].reshape(512, 384), w_ref[i * 3 + j])
            close += apply_taps(rows, w_ref[i * 3 + 1])
            sums[i * 3 + j] = jnp.dot(turned, rows, preferred_element_type=F32)
        first_ref[:, 64 * side : 64 * side + 32] += far.reshape(16, 32, 128)
        first_ref[:, 80 * side : 80 * side + 16] += close.reshape(16, 16, 128)
    second = fold(sums, factor)
    pre = jnp.concatenate([rim_ref[0, :, 32:48], one_ref[...], rim_ref[1, :, 32:48]], axis=1).astype(F32)
    outer_ref[2:18] = triple(jnp.where(pre > 0, first_ref[...], 0.0))
    first = fold(weight_sums(stack_ref[...], outer_ref), factor)

    def emit(half, ref):
        for m in range(7):
            ref[64 * m : 64 * m + 64] = first[7 * half + m].astype(ref.dtype)
            at = 448 * half + 64 * m
            block = second[7 * half + m] + sums_ref[at : at + 64]
            ref[448 + 64 * m : 512 + 64 * m] = block.astype(ref.dtype)

    share(at_ref[1], emit, mine_ref, send_ref)


def grad_kernel(at_ref, outer_ref, w_ref, grad_ref, turn_ref):
    grad = jnp.zeros((256, 128), F32)
    for i in range(3):
        for j in range(3):
            mine = outer_ref[pl.ds(at_ref[0] * 4 + 4 - 2 * i, 4), 32 - 16 * j : 96 - 16 * j].reshape(256, 384)
            grad += apply_taps(mine, w_ref[i * 3 + j])
    turn_ref[...] = grad
    for x in range(4):
        for t in range(8):
            grad_ref[x, :, 128 * t : 128 * t + 128] = turn_ref[pl.ds(64 * x + t, 8, stride=8), :].astype(BF16)


def spread(half, ref, hbm_refs, refs, sems):
    copies = []
    count = 14 - half
    for k, (hbm, out) in enumerate(zip(hbm_refs, refs)):
        for m in range(7):
            block = ref[448 * k + 64 * m : 448 * k + 64 * m + 64].astype(F32)
            out[2 * m] = block[:, 0:64]
            out[2 * m + 1] = block[:, 64:128]
        copies.append(
            pltpu.make_async_copy(out.at[0:count], hbm.at[14 * half : 14 * half + count], sems.at[k])
        )
        copies[-1].start()
    for copy in copies:
        copy.wait()


def half_kernel(at_ref, ref, one_hbm, two_hbm, one_ref, two_ref, sems):
    @pl.when(at_ref[1] == 0)
    def _():
        spread(0, ref, (one_hbm, two_hbm), (one_ref, two_ref), sems)

    @pl.when(at_ref[1] != 0)
    def _():
        spread(1, ref, (one_hbm, two_hbm), (one_ref, two_ref), sems)


def rest_kernel(at_ref, ref, one_in, two_in, one_hbm, two_hbm, one_ref, two_ref, sems):
    @pl.when(at_ref[1] == 0)
    def _():
        spread(1, ref, (one_hbm, two_hbm), (one_ref, two_ref), sems)

    @pl.when(at_ref[1] != 0)
    def _():
        spread(0, ref, (one_hbm, two_hbm), (one_ref, two_ref), sems)


def trans_kernel(at_ref, mine_ref, other_ref, trans_ref):
    def emit(half, ref):
        for m in range(4):
            trans_ref[256 * half : 256 * half + 256, 128 * m : 128 * m + 128] = ref[256 * m : 256 * m + 256].astype(F32)

    share(at_ref[1], emit, mine_ref, other_ref)


def rotate(value, axis, step):
    n = lax.axis_size(axis)
    return lax.ppermute(value, axis, [(i, (i + step) % n) for i in range(n)])


def swap(value, axis, bit):
    n = lax.axis_size(axis)
    return lax.ppermute(value, axis, [(i, i ^ bit) for i in range(n)])


def on_chip(mine, send):
    return (mine + swap(send, "gy", 1).astype(F32)).astype(BF16)


def across(mine):
    return mine.astype(F32) + swap(mine, "gy", 2).astype(F32)


def slab_body(input_activation, pre_one, pre_two, w_one, w_two, w_trans, keep_mask, out_grad):
    factor = 1.0 / math.sqrt(
        input_activation.shape[0] * 4 * input_activation.shape[1] * 4 * (input_activation.shape[2] // 64)
    )
    at = jnp.stack([lax.axis_index("gx"), lax.rem(lax.axis_index("gy"), 2)]).astype(jnp.int32)
    shape = jax.ShapeDtypeStruct
    vmem = pltpu.VMEM
    natural = vmem((4, 8, 1024), BF16)
    first, second = call(
        pack_kernel,
        (shape((768, 128), BF16), shape((256, 128), BF16)),
        [
            vmem((8, 4, 8, 128), BF16), natural, natural, natural, vmem((3, 256, 128), F32),
            pltpu.SemaphoreType.DMA((4,)),
        ],
        0,
        56,
        (out_grad,),
        (pre_two,),
        (pre_one,),
        (input_activation,),
    )
    firsts = [first] + [rotate(first, "gx", s) for s in (1, 2, 3)]
    seconds = [second] + [rotate(second, "gx", s) for s in (1, 2, 3)]
    kept, mask, d2, d1 = call(
        weight_kernel,
        (
            shape((512, 512), BF16), shape((512, 512), BF16),
            shape((9, 128, 384), BF16), shape((9, 128, 384), BF16),
        ),
        [
            vmem((512, 512), BF16), vmem((8, 8), jnp.int32),
            vmem((27, 64, 64), BF16), vmem((27, 64, 64), BF16),
            pltpu.SemaphoreType.DMA((4,)),
        ],
        10**7,
        8,
        (w_trans,),
        (keep_mask,),
        (w_two,),
        (w_one,),
    )
    back, one, chip, cross, tmine, tsend = call(
        functools.partial(transition_kernel, factor),
        (
            shape((8, 2, 64, 128), BF16),
            shape((16, 64, 128), BF16),
            shape((8, 2, 48, 128), BF16),
            shape((8, 2, 48, 128), BF16),
            shape((1024, 128), F32),
            shape((1024, 128), BF16),
        ),
        [vmem((4, 256, 128), BF16), vmem((16, 64, 128), BF16)],
        4 * 256 * 512 * 512,
        12,
        at,
        *firsts,
        kept,
        mask,
    )
    n = lax.axis_size("gy")
    pairs = [(i, i + 1) for i in range(1, n - 1, 2)]
    cross = lax.ppermute(cross, "gy", pairs + [(j, i) for i, j in pairs])
    chip = swap(chip, "gy", 1)
    tsend, *seconds = lax.optimization_barrier((tsend, *seconds))
    tmine = on_chip(tmine, tsend)
    one, tmine = lax.optimization_barrier((one, tmine))
    acc, sums, stacked = call(
        functools.partial(own_kernel, factor),
        (shape((16, 96, 128), F32), shape((896, 128), F32), shape((384, 1024), BF16)),
        [vmem((20, 96, 384), BF16), vmem((1280, 128), F32), vmem((16, 64, 128), BF16)],
        2 * 128 * 3456 * 2048,
        16,
        at,
        back.reshape(16, 64, 128),
        one,
        d2,
        *seconds,
    )
    tmine = across(tmine)
    mine, send, outer = call(
        functools.partial(conv_kernel, factor),
        (shape((896, 128), F32), shape((896, 128), BF16), shape((20, 96, 384), BF16)),
        [
            vmem((2, 16, 48, 128), BF16),
            vmem((2, 20, 32, 384), BF16),
            vmem((16, 96, 128), F32),
        ],
        2 * 128 * 3456 * 900,
        20,
        at,
        acc,
        sums,
        one,
        chip.reshape(16, 48, 128),
        cross.reshape(16, 48, 128),
        d2,
        stacked,
    )
    send, tmine = lax.optimization_barrier((send, tmine))
    mine = on_chip(mine, send)
    away = swap(mine, "gy", 2)
    tother = swap(tmine, "gy", 1)
    grad_w_trans = call(trans_kernel, shape((512, 512), F32), [], 10**7, 6, at, tmine, tother)
    grad_in = call(
        grad_kernel, shape((4, 8, 1024), BF16), [vmem((256, 128), F32)], 2 * 128 * 3456 * 256, 12, at, outer, d1
    )
    away, grad_w_trans, grad_in = lax.optimization_barrier((away, grad_w_trans, grad_in))
    mine = (mine.astype(F32) + away.astype(F32)).astype(BF16)
    other = swap(mine, "gy", 1)
    taps = shape((27, 64, 64), F32)
    scratch = [vmem((14, 64, 64), F32), vmem((14, 64, 64), F32), pltpu.SemaphoreType.DMA((2,))]
    hbm = pltpu.MemorySpace.HBM
    grad_w_one, grad_w_two = call(half_kernel, (taps, taps), scratch, 10**8, 6, at, mine, out_space=hbm)
    grad_w_one, grad_w_two = call(
        rest_kernel,
        (taps, taps),
        scratch,
        0,
        6,
        at,
        other,
        (grad_w_one,),
        (grad_w_two,),
        out_space=hbm,
        aliases={2: 0, 3: 1},
    )
    return (grad_in, grad_w_one, grad_w_two, grad_w_trans)


def solution(mesh):
    fits = mesh.shape["gx"] == 4 and mesh.shape["gy"] == 4

    def pick(*args):
        shapes = tuple(a.shape for a in args)
        known = (
            ((4, 8, 1024),) * 3 + ((27, 64, 64),) * 2 + ((512, 512), (8, 8), (8, 4, 8, 128))
        )
        return (slab_body if fits and shapes == known else body)(*args)

    return jax.shard_map(
        pick,
        mesh=mesh,
        in_specs=(
            P(("grp", "gx"), "gy", None),
            P(("grp", "gx"), "gy", None),
            P(("grp", "gx"), "gy", None),
            P(),
            P(),
            P(),
            P(),
            P("grp", "gy", None, "gx"),
        ),
        out_specs=(
            P(("grp", "gx"), "gy", None),
            P("grp", None, None),
            P("grp", None, None),
            P("grp", None),
        ),
        check_vma=False,
    )
```

```python
import functools
import math

import jax
import jax.numpy as jnp
from jax import lax
from jax.experimental import pallas as pl
from jax.experimental.pallas import tpu as pltpu
from jax.sharding import PartitionSpec as P

DILATION_STEP = 2
VMEM = pltpu.MemorySpace.VMEM
SMEM = pltpu.MemorySpace.SMEM
F32 = jnp.float32
BF16 = jnp.bfloat16


def padded(cells, sides, width):
    for axis, dim in sides:
        count = lax.axis_size(axis)
        ends = count - 1
        head = lax.slice_in_dim(cells, 0, width, axis=dim)
        tail = lax.slice_in_dim(cells, cells.shape[dim] - width, cells.shape[dim], axis=dim)
        cells = jnp.concatenate(
            [
                lax.ppermute(tail, axis, [(i, (i + 1) % count) for i in range(ends)]),
                cells,
                lax.ppermute(head, axis, [((i + 1) % count, i) for i in range(ends)]),
            ],
            axis=dim,
        )
    return cells


def split_layout(joined_layout, channel_count):
    return joined_layout.reshape(joined_layout.shape[0], joined_layout.shape[1], -1, channel_count)


def to_blocks(cube_volume):
    shape_all = cube_volume.shape
    parted = cube_volume.reshape(
        shape_all[0] // 2, 2, shape_all[1] // 2, 2, shape_all[2] // 2, 2, shape_all[3]
    )
    parted = parted.transpose(0, 2, 4, 1, 3, 5, 6)
    return parted.reshape(shape_all[0] // 2, shape_all[1] // 2, shape_all[2] // 2, 8 * shape_all[3])


def from_blocks(blocked, channel_count):
    shape_all = blocked.shape
    parted = blocked.reshape(shape_all[0], shape_all[1], shape_all[2], 2, 2, 2, channel_count)
    parted = parted.transpose(0, 3, 1, 4, 2, 5, 6)
    return parted.reshape(2 * shape_all[0], 2 * shape_all[1], 2 * shape_all[2], channel_count)


def padding_depth(cube_volume, margin):
    return jnp.pad(cube_volume, ((0, 0), (0, 0), (margin, margin), (0, 0)))


def weight_terms(bordered_input, upstream_gradient):
    channel_count = upstream_gradient.shape[3]
    grid_extent = upstream_gradient.shape
    padded_input = padding_depth(bordered_input, DILATION_STEP)
    flat_grad = upstream_gradient.reshape(-1, channel_count)
    partials = []
    for x_index in range(3):
        for y_index in range(3):
            sliding_window = padded_input[
                DILATION_STEP * x_index : DILATION_STEP * x_index + grid_extent[0],
                DILATION_STEP * y_index : DILATION_STEP * y_index + grid_extent[1],
            ]
            columns = jnp.concatenate(
                [
                    sliding_window[
                        :, :, DILATION_STEP * tap_index : DILATION_STEP * tap_index + grid_extent[2]
                    ].reshape(-1, channel_count)
                    for tap_index in range(3)
                ],
                axis=1,
            )
            partials.append(
                lax.dot_general(
                    columns, flat_grad, (((0,), (0,)), ((), ())), preferred_element_type=jnp.float32
                )
            )
    return jnp.stack(partials).reshape(27, channel_count, channel_count)


def data_terms(bordered_input, weights):
    channel_count = weights.shape[1]
    x_stretch = bordered_input.shape[0] - 2 * DILATION_STEP
    y_stretch = bordered_input.shape[1] - 2 * DILATION_STEP
    depth_cells = bordered_input.shape[2]
    padded_input = padding_depth(bordered_input, DILATION_STEP)
    stacked = jnp.transpose(weights, (0, 2, 1)).reshape(9, 3 * channel_count, channel_count)
    running = jnp.zeros((x_stretch * y_stretch * depth_cells, channel_count), jnp.float32)
    for x_index in range(3):
        for y_index in range(3):
            sliding_window = padded_input[
                DILATION_STEP * (2 - x_index) : DILATION_STEP * (2 - x_index) + x_stretch,
                DILATION_STEP * (2 - y_index) : DILATION_STEP * (2 - y_index) + y_stretch,
            ]
            columns = jnp.concatenate(
                [
                    sliding_window[
                        :,
                        :,
                        DILATION_STEP * (2 - tap_index) : DILATION_STEP * (2 - tap_index)
                        + depth_cells,
                    ].reshape(-1, channel_count)
                    for tap_index in range(3)
                ],
                axis=1,
            )
            running = running + jnp.dot(
                columns, stacked[x_index * 3 + y_index], preferred_element_type=jnp.float32
            )
    return running.reshape(x_stretch, y_stretch, depth_cells, channel_count)


def body(input_activation, pre_one, pre_two, w_one, w_two, w_trans, keep_mask, out_grad):
    channel_count = w_one.shape[1]
    x_stretch, y_stretch, joined_layout = input_activation.shape
    depth_cells = joined_layout // channel_count
    width_t = w_trans.shape[0]
    factor = 1.0 / math.sqrt(
        x_stretch * lax.axis_size("gx") * y_stretch * lax.axis_size("gy") * depth_cells
    )
    blocks = jnp.repeat(
        jnp.repeat(keep_mask.astype(jnp.bfloat16), channel_count, axis=0), channel_count, axis=1
    )
    w_kept = w_trans * blocks
    regrouped = lax.all_to_all(out_grad, "gx", split_axis=0, concat_axis=3, tiled=True)
    grad_rows = regrouped.reshape(-1, width_t)
    back_blocks = lax.dot_general(
        grad_rows, w_kept, (((1,), (1,)), ((), ())), preferred_element_type=jnp.float32
    ).astype(jnp.bfloat16)
    act_two = split_layout(jnp.maximum(pre_two, 0), channel_count)
    two_rows = to_blocks(act_two).reshape(-1, width_t)
    trans_term = (
        lax.dot_general(
            two_rows, grad_rows, (((0,), (0,)), ((), ())), preferred_element_type=jnp.float32
        )
        * blocks.astype(jnp.float32)
        * factor
    )
    grad_w_trans = lax.psum(trans_term, ("gx", "gy"))
    back_two = from_blocks(
        back_blocks.reshape(x_stretch // 2, y_stretch // 2, depth_cells // 2, width_t),
        channel_count,
    )
    back_two = jnp.where(
        split_layout(pre_two, channel_count) > 0, back_two, jnp.zeros_like(back_two)
    )
    first_activation = jnp.maximum(pre_one, 0)
    bordered_input = padded(
        jnp.concatenate([input_activation, first_activation], axis=2),
        (("gx", 0), ("gy", 1)),
        DILATION_STEP,
    )
    in_rim = split_layout(bordered_input[:, :, :joined_layout], channel_count)
    one_rim = split_layout(bordered_input[:, :, joined_layout:], channel_count)
    two_term = weight_terms(one_rim, back_two) * factor
    flattened_backward = back_two.reshape(x_stretch, y_stretch, joined_layout)
    narrowed_slice = split_layout(
        padded(flattened_backward, (("gx", 0), ("gy", 1)), DILATION_STEP), channel_count
    )
    first_backward = data_terms(narrowed_slice, w_two)
    first_backward = jnp.where(
        split_layout(pre_one, channel_count) > 0, first_backward, jnp.zeros_like(first_backward)
    ).astype(jnp.bfloat16)
    one_grad_rim = split_layout(
        padded(
            first_backward.reshape(x_stretch, y_stretch, joined_layout),
            (("gx", 0), ("gy", 1)),
            DILATION_STEP,
        ),
        channel_count,
    )
    grad_w_two = lax.psum(two_term, ("gx", "gy"))
    one_term = weight_terms(in_rim, first_backward) * factor
    grad_w_one = lax.psum(one_term, ("gx", "gy"))
    grad_in = (
        data_terms(one_grad_rim, w_one)
        .astype(jnp.bfloat16)
        .reshape(x_stretch, y_stretch, joined_layout)
    )
    return (grad_in, grad_w_one, grad_w_two, grad_w_trans)


def call(kernel, out_shape, scratch, flops, limit, *args, out_space=VMEM, aliases={}):
    spec = []
    for a in args:
        if isinstance(a, tuple):
            spec.append(pl.BlockSpec(memory_space=pltpu.MemorySpace.HBM))
        elif a.dtype == jnp.int32:
            spec.append(pl.BlockSpec(memory_space=SMEM))
        else:
            spec.append(pl.BlockSpec(memory_space=VMEM))
    arrays = [a[0] if isinstance(a, tuple) else a for a in args]
    return pl.pallas_call(
        kernel,
        out_shape=out_shape,
        in_specs=spec,
        out_specs=jax.tree.map(lambda _: pl.BlockSpec(memory_space=out_space), out_shape),
        scratch_shapes=scratch,
        input_output_aliases=aliases,
        cost_estimate=pl.CostEstimate(
            flops=flops,
            transcendentals=0,
            bytes_accessed=sum(a.size * a.dtype.itemsize for a in arrays) if flops else 0,
        ),
        compiler_params=pltpu.CompilerParams(vmem_limit_bytes=limit * 1024 * 1024),
    )(*arrays)


def fetch(pairs, sems):
    copies = [pltpu.make_async_copy(src, dst, sems.at[k]) for k, (src, dst) in enumerate(pairs)]
    for copy in copies:
        copy.start()
    return copies


def pack_kernel(og, two, one, act, first_hbm, second_hbm, og_v, two_v, one_v, act_v, turn_ref, out_ref, sems, out_sems):
    copies = fetch(((og, og_v), (two, two_v), (one, one_v), (act, act_v)), sems)
    sent = []

    def send(k, hbm, at):
        sent.append(pltpu.make_async_copy(out_ref.at[k], hbm.at[at : at + 256], out_sems.at[k]))
        sent[-1].start()

    copies[0].wait()
    out_ref[0] = og_v[...].astype(F32).reshape(256, 128).astype(BF16)
    send(0, first_hbm, 0)
    for k, (ref, hbm, at) in enumerate(((two_v, first_hbm, 256), (one_v, first_hbm, 512), (act_v, second_hbm, 0))):
        copies[k + 1].wait()
        for x in range(4):
            for t in range(8):
                turn_ref[k, pl.ds(64 * x + t, 8, stride=8), :] = ref[x, :, 128 * t : 128 * t + 128].astype(F32)
        out_ref[k + 1] = turn_ref[k].astype(BF16)
        send(k + 1, hbm, at)
    for copy in sent:
        copy.wait()


def weight_kernel(wt, keep, w2, w1, kept_ref, mask_ref, d2_ref, d1_ref, wt_v, keep_v, w2_v, w1_v, sems):
    copies = fetch(((keep, keep_v), (wt, wt_v), (w2, w2_v), (w1, w1_v)), sems)
    copies[0].wait()
    width = wt_v.shape[0]
    blocks = keep_v.shape[0]
    side = width // blocks
    left = (
        lax.broadcasted_iota(jnp.int32, (width, blocks), 0) // side
        == lax.broadcasted_iota(jnp.int32, (width, blocks), 1)
    ).astype(BF16)
    right = (
        lax.broadcasted_iota(jnp.int32, (blocks, width), 1) // side
        == lax.broadcasted_iota(jnp.int32, (blocks, width), 0)
    ).astype(BF16)
    wide = jnp.dot(keep_v[...].astype(F32).astype(BF16), right, preferred_element_type=F32).astype(BF16)
    mask = jnp.dot(left, wide, preferred_element_type=F32)
    mask_ref[...] = mask.astype(BF16)
    copies[1].wait()
    kept_ref[...] = (wt_v[...].astype(F32) * mask).astype(BF16)
    none = jnp.zeros((64, 64), BF16)
    for k, (ref, out) in enumerate(((w2_v, d2_ref), (w1_v, d1_ref))):
        copies[k + 2].wait()
        for tap in range(27):
            w = ref[tap]
            at = 128 * (tap % 3)
            out[tap // 3, 0:64, at : at + 128] = jnp.concatenate([w, none], axis=1)
            out[tap // 3, 64:128, at : at + 128] = jnp.concatenate([none, w], axis=1)


def transition_kernel(
    factor, at_ref, a0, a1, a2, a3, kept_ref, mask_ref, back_ref, one_ref, chip_ref, cross_ref, mine_ref, send_ref, og_ref, two_ref
):
    me = at_ref[0]
    parts = (a0, a1, a2, a3)
    n = len(parts)
    for s, part in enumerate(parts):
        src = lax.rem(me + n - s, n)
        og_ref[src] = part[0:256]
        spot = pl.ds(src * 4, 4)
        two_ref[spot] = part[256:512].reshape(4, 64, 128)
        one_ref[spot] = part[512:768].reshape(4, 64, 128)
    og = jnp.concatenate([og_ref[j] for j in range(n)], axis=1)
    back = lax.dot_general(og, kept_ref[...], (((1,), (1,)), ((), ())), preferred_element_type=F32)
    two = two_ref[...].astype(F32).reshape(8, 2, 4, 2, 8, 128)
    cells = []
    for p in range(2):
        halves = []
        for q in range(2):
            pre = two[:, p, :, q]
            at = (p * 2 + q) * 128
            grad = back[:, at : at + 128].reshape(8, 4, 8, 128)
            halves.append(jnp.where(pre > 0, grad, 0.0))
            cells.append(jnp.maximum(pre, 0.0).reshape(256, 128).astype(BF16))
        back_ref[:, p] = jnp.stack(halves, axis=2).reshape(8, 64, 128).astype(BF16)

    def rim(high, ref):
        at = 32 if high else 0
        ref[:, :, 0:32] = back_ref[:, :, at : at + 32]
        at = 48 if high else 0
        ref[:, :, 32:48] = one_ref[:, at : at + 16].reshape(8, 2, 16, 128)

    share(at_ref[1], rim, cross_ref, chip_ref)
    flat = jnp.concatenate(cells, axis=1)
    trans = lax.dot_general(flat, og, (((0,), (0,)), ((), ())), preferred_element_type=F32)
    trans = trans * mask_ref[...].astype(F32) * factor

    def emit(half, ref):
        for m in range(4):
            ref[256 * m : 256 * m + 256] = trans[256 * half : 256 * half + 256, 128 * m : 128 * m + 128].astype(ref.dtype)

    share(at_ref[1], emit, mine_ref, send_ref)


def share(core, emit, mine_ref, send_ref):
    @pl.when(core == 0)
    def _():
        emit(0, mine_ref)
        emit(1, send_ref)

    @pl.when(core != 0)
    def _():
        emit(1, mine_ref)
        emit(0, send_ref)


def triple(v):
    x, rows, _ = v.shape
    flat = v.reshape(x * rows, 128)
    t = lax.broadcasted_iota(jnp.int32, flat.shape, 0) % 8
    later = jnp.where(t == 7, 0.0, pltpu.roll(flat, x * rows - 1, 0))
    earlier = jnp.where(t == 0, 0.0, pltpu.roll(flat, 1, 0))
    wide = jnp.concatenate([later, flat, earlier], axis=1)
    return wide.astype(BF16).reshape(x, rows, 384)


def fold(sums, factor):
    lane = lax.broadcasted_iota(jnp.int32, (64, 128), 1)
    taps = []
    for g in sums:
        for l in range(3):
            if g is None:
                taps.append(jnp.zeros((64, 128), F32))
                continue
            part = g[:, l * 128 : (l + 1) * 128]
            f = jnp.where(lane < 64, part[0:64], part[64:128])
            taps.append((f + pltpu.roll(f, 64, 1)) * factor)
    taps.append(taps[-1])
    return [jnp.where(lane < 64, taps[2 * m], taps[2 * m + 1]) for m in range(14)]


def apply_taps(rows, taps):
    return lax.dot_general(rows, taps, (((1,), (1,)), ((), ())), preferred_element_type=F32)


def weight_sums(act, wide_ref, act_ref):
    act_ref[0:128] = jnp.zeros((128, 128), F32)
    act_ref[128:1152] = act.reshape(1024, 128)
    act_ref[1152:1280] = jnp.zeros((128, 128), F32)
    turned = act_ref[...].T.astype(BF16)
    stacked = jnp.concatenate([turned[:, 128 * i : 128 * i + 1024] for i in range(3)], axis=0)
    sums = [None] * 9
    for j in range(3):
        rows = wide_ref[2:18, 32 - 16 * j : 96 - 16 * j].reshape(1024, 384)
        part = jnp.dot(stacked, rows, preferred_element_type=F32)
        for i in range(3):
            sums[i * 3 + j] = part[128 * i : 128 * i + 128]
    return sums


def own_kernel(factor, back_ref, one_ref, w_ref, acc_ref, sums_ref, wide_ref, act_ref):
    wide_ref[2:18, 0:16] = jnp.zeros((16, 16, 384), BF16)
    wide_ref[2:18, 80:96] = jnp.zeros((16, 16, 384), BF16)
    wide_ref[2:18, 16:80] = triple(back_ref[...].astype(F32))
    acc_ref[...] = jnp.zeros((16, 96, 128), F32)
    rows = wide_ref[2:18, 16:80].reshape(1024, 384)
    for j in range(3):
        taps = jnp.concatenate([w_ref[i * 3 + j] for i in range(3)], axis=0)
        part = apply_taps(rows, taps).reshape(16, 64, 384)
        ys = slice(16 * j, 16 * j + 64)
        acc_ref[0:14, ys] += part[2:16, :, 0:128]
        acc_ref[:, ys] += part[:, :, 128:256]
        acc_ref[2:16, ys] += part[0:14, :, 256:384]
    sums = weight_sums(jnp.maximum(one_ref[...].astype(F32), 0.0), wide_ref, act_ref)
    for m, block in enumerate(fold(sums, factor)):
        sums_ref[64 * m : 64 * m + 64] = block


def conv_kernel(
    factor, at_ref, acc_ref, sums_ref, one_ref, chip_ref, cross_ref, w_ref, i0, i1, i2, i3,
    mine_ref, send_ref, outer_ref, rim_ref, wide_ref, in_ref, first_ref, act_ref,
):
    me = at_ref[0]
    parts = (i0, i1, i2, i3)
    n = len(parts)
    for s, part in enumerate(parts):
        in_ref[pl.ds(lax.rem(me + n - s, n) * 4, 4)] = part[...].reshape(4, 64, 128)

    def put(side, ref):
        rim_ref[side] = ref[...]

    share(at_ref[1], put, cross_ref, chip_ref)
    wide_ref[:, 0:2] = jnp.zeros((2, 2, 32, 384), BF16)
    wide_ref[:, 18:20] = jnp.zeros((2, 2, 32, 384), BF16)
    outer_ref[0:2] = jnp.zeros((2, 96, 384), BF16)
    outer_ref[18:20] = jnp.zeros((2, 96, 384), BF16)
    for side in range(2):
        wide_ref[side, 2:18] = triple(rim_ref[side, :, 0:32].astype(F32))
    first_ref[...] = acc_ref[...]
    act = jnp.maximum(one_ref[...].astype(F32), 0.0)
    sums = [None] * 9
    for side in range(2):
        j = 2 - 2 * side
        near = 16 - 16 * side
        own = 48 * side
        turned = act[:, own : own + 16].reshape(256, 128).T.astype(BF16)
        far = jnp.zeros((512, 128), F32)
        close = jnp.zeros((256, 128), F32)
        for i in range(3):
            xs = slice(4 - 2 * i, 20 - 2 * i)
            rows = wide_ref[side, xs, near : near + 16].reshape(256, 384)
            far += apply_taps(wide_ref[side, xs].reshape(512, 384), w_ref[i * 3 + j])
            close += apply_taps(rows, w_ref[i * 3 + 1])
            sums[i * 3 + j] = jnp.dot(turned, rows, preferred_element_type=F32)
        first_ref[:, 64 * side : 64 * side + 32] += far.reshape(16, 32, 128)
        first_ref[:, 80 * side : 80 * side + 16] += close.reshape(16, 16, 128)
    second = fold(sums, factor)
    pre = jnp.concatenate([rim_ref[0, :, 32:48], one_ref[...], rim_ref[1, :, 32:48]], axis=1).astype(F32)
    outer_ref[2:18] = triple(jnp.where(pre > 0, first_ref[...], 0.0))
    first = fold(weight_sums(in_ref[...].astype(F32), outer_ref, act_ref), factor)

    def emit(half, ref):
        for m in range(7):
            ref[64 * m : 64 * m + 64] = first[7 * half + m].astype(ref.dtype)
            at = 448 * half + 64 * m
            block = second[7 * half + m] + sums_ref[at : at + 64]
            ref[448 + 64 * m : 512 + 64 * m] = block.astype(ref.dtype)

    share(at_ref[1], emit, mine_ref, send_ref)


def grad_kernel(at_ref, outer_ref, w_ref, grad_ref, turn_ref):
    grad = jnp.zeros((256, 128), F32)
    for i in range(3):
        for j in range(3):
            mine = outer_ref[pl.ds(at_ref[0] * 4 + 4 - 2 * i, 4), 32 - 16 * j : 96 - 16 * j].reshape(256, 384)
            grad += apply_taps(mine, w_ref[i * 3 + j])
    turn_ref[...] = grad
    for x in range(4):
        for t in range(8):
            grad_ref[x, :, 128 * t : 128 * t + 128] = turn_ref[pl.ds(64 * x + t, 8, stride=8), :].astype(BF16)


def spread(half, ref, hbm_refs, refs, sems):
    copies = []
    count = 14 - half
    for k, (hbm, out) in enumerate(zip(hbm_refs, refs)):
        for m in range(7):
            block = ref[448 * k + 64 * m : 448 * k + 64 * m + 64].astype(F32)
            out[2 * m] = block[:, 0:64]
            out[2 * m + 1] = block[:, 64:128]
        copies.append(
            pltpu.make_async_copy(out.at[0:count], hbm.at[14 * half : 14 * half + count], sems.at[k])
        )
        copies[-1].start()
    for copy in copies:
        copy.wait()


def half_kernel(at_ref, ref, one_hbm, two_hbm, one_ref, two_ref, sems):
    @pl.when(at_ref[1] == 0)
    def _():
        spread(0, ref, (one_hbm, two_hbm), (one_ref, two_ref), sems)

    @pl.when(at_ref[1] != 0)
    def _():
        spread(1, ref, (one_hbm, two_hbm), (one_ref, two_ref), sems)


def rest_kernel(at_ref, ref, one_in, two_in, one_hbm, two_hbm, one_ref, two_ref, sems):
    @pl.when(at_ref[1] == 0)
    def _():
        spread(1, ref, (one_hbm, two_hbm), (one_ref, two_ref), sems)

    @pl.when(at_ref[1] != 0)
    def _():
        spread(0, ref, (one_hbm, two_hbm), (one_ref, two_ref), sems)


def trans_kernel(at_ref, mine_ref, other_ref, trans_ref):
    def emit(half, ref):
        for m in range(4):
            trans_ref[256 * half : 256 * half + 256, 128 * m : 128 * m + 128] = ref[256 * m : 256 * m + 256].astype(F32)

    share(at_ref[1], emit, mine_ref, other_ref)


def rotate(value, axis, step):
    n = lax.axis_size(axis)
    return lax.ppermute(value, axis, [(i, (i + step) % n) for i in range(n)])


def swap(value, axis, bit):
    n = lax.axis_size(axis)
    return lax.ppermute(value, axis, [(i, i ^ bit) for i in range(n)])


def on_chip(mine, send):
    return (mine + swap(send, "gy", 1).astype(F32)).astype(BF16)


def across(mine):
    return mine.astype(F32) + swap(mine, "gy", 2).astype(F32)


def slab_body(input_activation, pre_one, pre_two, w_one, w_two, w_trans, keep_mask, out_grad):
    factor = 1.0 / math.sqrt(
        input_activation.shape[0] * 4 * input_activation.shape[1] * 4 * (input_activation.shape[2] // 64)
    )
    at = jnp.stack([lax.axis_index("gx"), lax.rem(lax.axis_index("gy"), 2)]).astype(jnp.int32)
    shape = jax.ShapeDtypeStruct
    vmem = pltpu.VMEM
    natural = vmem((4, 8, 1024), BF16)
    first, second = call(
        pack_kernel,
        (shape((768, 128), BF16), shape((256, 128), BF16)),
        [
            vmem((8, 4, 8, 128), BF16), natural, natural, natural, vmem((3, 256, 128), F32),
            vmem((4, 256, 128), BF16), pltpu.SemaphoreType.DMA((4,)), pltpu.SemaphoreType.DMA((4,)),
        ],
        0,
        56,
        (out_grad,),
        (pre_two,),
        (pre_one,),
        (input_activation,),
        out_space=pltpu.MemorySpace.HBM,
    )
    firsts = [first] + [rotate(first, "gx", s) for s in (1, 2, 3)]
    seconds = [second] + [rotate(second, "gx", s) for s in (1, 2, 3)]
    kept, mask, d2, d1 = call(
        weight_kernel,
        (
            shape((512, 512), BF16), shape((512, 512), BF16),
            shape((9, 128, 384), BF16), shape((9, 128, 384), BF16),
        ),
        [
            vmem((512, 512), BF16), vmem((8, 8), jnp.int32),
            vmem((27, 64, 64), BF16), vmem((27, 64, 64), BF16),
            pltpu.SemaphoreType.DMA((4,)),
        ],
        10**7,
        8,
        (w_trans,),
        (keep_mask,),
        (w_two,),
        (w_one,),
    )
    back, one, chip, cross, tmine, tsend = call(
        functools.partial(transition_kernel, factor),
        (
            shape((8, 2, 64, 128), BF16),
            shape((16, 64, 128), BF16),
            shape((8, 2, 48, 128), BF16),
            shape((8, 2, 48, 128), BF16),
            shape((1024, 128), F32),
            shape((1024, 128), BF16),
        ),
        [vmem((4, 256, 128), BF16), vmem((16, 64, 128), BF16)],
        4 * 256 * 512 * 512,
        12,
        at,
        *firsts,
        kept,
        mask,
    )
    n = lax.axis_size("gy")
    pairs = [(i, i + 1) for i in range(1, n - 1, 2)]
    cross = lax.ppermute(cross, "gy", pairs + [(j, i) for i, j in pairs])
    chip = swap(chip, "gy", 1)
    tsend, *seconds = lax.optimization_barrier((tsend, *seconds))
    tmine = on_chip(tmine, tsend)
    one, tmine = lax.optimization_barrier((one, tmine))
    acc, sums = call(
        functools.partial(own_kernel, factor),
        (shape((16, 96, 128), F32), shape((896, 128), F32)),
        [vmem((20, 96, 384), BF16), vmem((1280, 128), F32)],
        2 * 128 * 3456 * 2048,
        16,
        back.reshape(16, 64, 128),
        one,
        d2,
    )
    tmine = across(tmine)
    mine, send, outer = call(
        functools.partial(conv_kernel, factor),
        (shape((896, 128), F32), shape((896, 128), BF16), shape((20, 96, 384), BF16)),
        [
            vmem((2, 16, 48, 128), BF16),
            vmem((2, 20, 32, 384), BF16),
            vmem((16, 64, 128), BF16),
            vmem((16, 96, 128), F32),
            vmem((1280, 128), F32),
        ],
        2 * 128 * 3456 * 900,
        20,
        at,
        acc,
        sums,
        one,
        chip.reshape(16, 48, 128),
        cross.reshape(16, 48, 128),
        d2,
        *seconds,
    )
    send, tmine = lax.optimization_barrier((send, tmine))
    mine = on_chip(mine, send)
    away = swap(mine, "gy", 2)
    tother = swap(tmine, "gy", 1)
    grad_w_trans = call(trans_kernel, shape((512, 512), F32), [], 10**7, 6, at, tmine, tother)
    grad_in = call(
        grad_kernel, shape((4, 8, 1024), BF16), [vmem((256, 128), F32)], 2 * 128 * 3456 * 256, 12, at, outer, d1
    )
    away, grad_w_trans, grad_in = lax.optimization_barrier((away, grad_w_trans, grad_in))
    mine = (mine.astype(F32) + away.astype(F32)).astype(BF16)
    other = swap(mine, "gy", 1)
    taps = shape((27, 64, 64), F32)
    scratch = [vmem((14, 64, 64), F32), vmem((14, 64, 64), F32), pltpu.SemaphoreType.DMA((2,))]
    hbm = pltpu.MemorySpace.HBM
    grad_w_one, grad_w_two = call(half_kernel, (taps, taps), scratch, 10**8, 6, at, mine, out_space=hbm)
    grad_w_one, grad_w_two = call(
        rest_kernel,
        (taps, taps),
        scratch,
        0,
        6,
        at,
        other,
        (grad_w_one,),
        (grad_w_two,),
        out_space=hbm,
        aliases={2: 0, 3: 1},
    )
    return (grad_in, grad_w_one, grad_w_two, grad_w_trans)


def solution(mesh):
    fits = mesh.shape["gx"] == 4 and mesh.shape["gy"] == 4

    def pick(*args):
        shapes = tuple(a.shape for a in args)
        known = (
            ((4, 8, 1024),) * 3 + ((27, 64, 64),) * 2 + ((512, 512), (8, 8), (8, 4, 8, 128))
        )
        return (slab_body if fits and shapes == known else body)(*args)

    return jax.shard_map(
        pick,
        mesh=mesh,
        in_specs=(
            P(("grp", "gx"), "gy", None),
            P(("grp", "gx"), "gy", None),
            P(("grp", "gx"), "gy", None),
            P(),
            P(),
            P(),
            P(),
            P("grp", "gy", None, "gx"),
        ),
        out_specs=(
            P(("grp", "gx"), "gy", None),
            P("grp", None, None),
            P("grp", None, None),
            P("grp", None),
        ),
        check_vma=False,
    )
```

```python
import functools
import math

import jax
import jax.numpy as jnp
from jax import lax
from jax.experimental import pallas as pl
from jax.experimental.pallas import tpu as pltpu
from jax.sharding import PartitionSpec as P

DILATION_STEP = 2
VMEM = pltpu.MemorySpace.VMEM
SMEM = pltpu.MemorySpace.SMEM
F32 = jnp.float32
BF16 = jnp.bfloat16


def padded(cells, sides, width):
    for axis, dim in sides:
        count = lax.axis_size(axis)
        ends = count - 1
        head = lax.slice_in_dim(cells, 0, width, axis=dim)
        tail = lax.slice_in_dim(cells, cells.shape[dim] - width, cells.shape[dim], axis=dim)
        cells = jnp.concatenate(
            [
                lax.ppermute(tail, axis, [(i, (i + 1) % count) for i in range(ends)]),
                cells,
                lax.ppermute(head, axis, [((i + 1) % count, i) for i in range(ends)]),
            ],
            axis=dim,
        )
    return cells


def split_layout(joined_layout, channel_count):
    return joined_layout.reshape(joined_layout.shape[0], joined_layout.shape[1], -1, channel_count)


def to_blocks(cube_volume):
    shape_all = cube_volume.shape
    parted = cube_volume.reshape(
        shape_all[0] // 2, 2, shape_all[1] // 2, 2, shape_all[2] // 2, 2, shape_all[3]
    )
    parted = parted.transpose(0, 2, 4, 1, 3, 5, 6)
    return parted.reshape(shape_all[0] // 2, shape_all[1] // 2, shape_all[2] // 2, 8 * shape_all[3])


def from_blocks(blocked, channel_count):
    shape_all = blocked.shape
    parted = blocked.reshape(shape_all[0], shape_all[1], shape_all[2], 2, 2, 2, channel_count)
    parted = parted.transpose(0, 3, 1, 4, 2, 5, 6)
    return parted.reshape(2 * shape_all[0], 2 * shape_all[1], 2 * shape_all[2], channel_count)


def padding_depth(cube_volume, margin):
    return jnp.pad(cube_volume, ((0, 0), (0, 0), (margin, margin), (0, 0)))


def weight_terms(bordered_input, upstream_gradient):
    channel_count = upstream_gradient.shape[3]
    grid_extent = upstream_gradient.shape
    padded_input = padding_depth(bordered_input, DILATION_STEP)
    flat_grad = upstream_gradient.reshape(-1, channel_count)
    partials = []
    for x_index in range(3):
        for y_index in range(3):
            sliding_window = padded_input[
                DILATION_STEP * x_index : DILATION_STEP * x_index + grid_extent[0],
                DILATION_STEP * y_index : DILATION_STEP * y_index + grid_extent[1],
            ]
            columns = jnp.concatenate(
                [
                    sliding_window[
                        :, :, DILATION_STEP * tap_index : DILATION_STEP * tap_index + grid_extent[2]
                    ].reshape(-1, channel_count)
                    for tap_index in range(3)
                ],
                axis=1,
            )
            partials.append(
                lax.dot_general(
                    columns, flat_grad, (((0,), (0,)), ((), ())), preferred_element_type=jnp.float32
                )
            )
    return jnp.stack(partials).reshape(27, channel_count, channel_count)


def data_terms(bordered_input, weights):
    channel_count = weights.shape[1]
    x_stretch = bordered_input.shape[0] - 2 * DILATION_STEP
    y_stretch = bordered_input.shape[1] - 2 * DILATION_STEP
    depth_cells = bordered_input.shape[2]
    padded_input = padding_depth(bordered_input, DILATION_STEP)
    stacked = jnp.transpose(weights, (0, 2, 1)).reshape(9, 3 * channel_count, channel_count)
    running = jnp.zeros((x_stretch * y_stretch * depth_cells, channel_count), jnp.float32)
    for x_index in range(3):
        for y_index in range(3):
            sliding_window = padded_input[
                DILATION_STEP * (2 - x_index) : DILATION_STEP * (2 - x_index) + x_stretch,
                DILATION_STEP * (2 - y_index) : DILATION_STEP * (2 - y_index) + y_stretch,
            ]
            columns = jnp.concatenate(
                [
                    sliding_window[
                        :,
                        :,
                        DILATION_STEP * (2 - tap_index) : DILATION_STEP * (2 - tap_index)
                        + depth_cells,
                    ].reshape(-1, channel_count)
                    for tap_index in range(3)
                ],
                axis=1,
            )
            running = running + jnp.dot(
                columns, stacked[x_index * 3 + y_index], preferred_element_type=jnp.float32
            )
    return running.reshape(x_stretch, y_stretch, depth_cells, channel_count)


def body(input_activation, pre_one, pre_two, w_one, w_two, w_trans, keep_mask, out_grad):
    channel_count = w_one.shape[1]
    x_stretch, y_stretch, joined_layout = input_activation.shape
    depth_cells = joined_layout // channel_count
    width_t = w_trans.shape[0]
    factor = 1.0 / math.sqrt(
        x_stretch * lax.axis_size("gx") * y_stretch * lax.axis_size("gy") * depth_cells
    )
    blocks = jnp.repeat(
        jnp.repeat(keep_mask.astype(jnp.bfloat16), channel_count, axis=0), channel_count, axis=1
    )
    w_kept = w_trans * blocks
    regrouped = lax.all_to_all(out_grad, "gx", split_axis=0, concat_axis=3, tiled=True)
    grad_rows = regrouped.reshape(-1, width_t)
    back_blocks = lax.dot_general(
        grad_rows, w_kept, (((1,), (1,)), ((), ())), preferred_element_type=jnp.float32
    ).astype(jnp.bfloat16)
    act_two = split_layout(jnp.maximum(pre_two, 0), channel_count)
    two_rows = to_blocks(act_two).reshape(-1, width_t)
    trans_term = (
        lax.dot_general(
            two_rows, grad_rows, (((0,), (0,)), ((), ())), preferred_element_type=jnp.float32
        )
        * blocks.astype(jnp.float32)
        * factor
    )
    grad_w_trans = lax.psum(trans_term, ("gx", "gy"))
    back_two = from_blocks(
        back_blocks.reshape(x_stretch // 2, y_stretch // 2, depth_cells // 2, width_t),
        channel_count,
    )
    back_two = jnp.where(
        split_layout(pre_two, channel_count) > 0, back_two, jnp.zeros_like(back_two)
    )
    first_activation = jnp.maximum(pre_one, 0)
    bordered_input = padded(
        jnp.concatenate([input_activation, first_activation], axis=2),
        (("gx", 0), ("gy", 1)),
        DILATION_STEP,
    )
    in_rim = split_layout(bordered_input[:, :, :joined_layout], channel_count)
    one_rim = split_layout(bordered_input[:, :, joined_layout:], channel_count)
    two_term = weight_terms(one_rim, back_two) * factor
    flattened_backward = back_two.reshape(x_stretch, y_stretch, joined_layout)
    narrowed_slice = split_layout(
        padded(flattened_backward, (("gx", 0), ("gy", 1)), DILATION_STEP), channel_count
    )
    first_backward = data_terms(narrowed_slice, w_two)
    first_backward = jnp.where(
        split_layout(pre_one, channel_count) > 0, first_backward, jnp.zeros_like(first_backward)
    ).astype(jnp.bfloat16)
    one_grad_rim = split_layout(
        padded(
            first_backward.reshape(x_stretch, y_stretch, joined_layout),
            (("gx", 0), ("gy", 1)),
            DILATION_STEP,
        ),
        channel_count,
    )
    grad_w_two = lax.psum(two_term, ("gx", "gy"))
    one_term = weight_terms(in_rim, first_backward) * factor
    grad_w_one = lax.psum(one_term, ("gx", "gy"))
    grad_in = (
        data_terms(one_grad_rim, w_one)
        .astype(jnp.bfloat16)
        .reshape(x_stretch, y_stretch, joined_layout)
    )
    return (grad_in, grad_w_one, grad_w_two, grad_w_trans)


def call(kernel, out_shape, scratch, flops, limit, *args, out_space=VMEM):
    spec = []
    for a in args:
        if isinstance(a, tuple):
            spec.append(pl.BlockSpec(memory_space=pltpu.MemorySpace.HBM))
        elif a.dtype == jnp.int32:
            spec.append(pl.BlockSpec(memory_space=SMEM))
        else:
            spec.append(pl.BlockSpec(memory_space=VMEM))
    arrays = [a[0] if isinstance(a, tuple) else a for a in args]
    return pl.pallas_call(
        kernel,
        out_shape=out_shape,
        in_specs=spec,
        out_specs=jax.tree.map(lambda _: pl.BlockSpec(memory_space=out_space), out_shape),
        scratch_shapes=scratch,
        cost_estimate=pl.CostEstimate(
            flops=flops,
            transcendentals=0,
            bytes_accessed=sum(a.size * a.dtype.itemsize for a in arrays) if flops else 0,
        ),
        compiler_params=pltpu.CompilerParams(vmem_limit_bytes=limit * 1024 * 1024),
    )(*arrays)


def fetch(pairs, sems):
    copies = [pltpu.make_async_copy(src, dst, sems.at[k]) for k, (src, dst) in enumerate(pairs)]
    for copy in copies:
        copy.start()
    return copies


def pack_kernel(og, two, one, act, first_ref, second_ref, og_v, two_v, one_v, act_v, turn_ref, sems):
    copies = fetch(((og, og_v), (two, two_v), (one, one_v), (act, act_v)), sems)
    copies[0].wait()
    first_ref[0:256] = og_v[...].astype(F32).reshape(256, 128).astype(BF16)
    for k, (ref, out, at) in enumerate(((two_v, first_ref, 256), (one_v, first_ref, 512), (act_v, second_ref, 0))):
        copies[k + 1].wait()
        for x in range(4):
            for t in range(8):
                turn_ref[k, pl.ds(64 * x + t, 8, stride=8), :] = ref[x, :, 128 * t : 128 * t + 128].astype(F32)
        out[at : at + 256] = turn_ref[k].astype(BF16)


def weight_kernel(wt, keep, w2, w1, kept_ref, mask_ref, d2_ref, d1_ref, wt_v, keep_v, w2_v, w1_v, sems):
    copies = fetch(((keep, keep_v), (wt, wt_v), (w2, w2_v), (w1, w1_v)), sems)
    copies[0].wait()
    width = wt_v.shape[0]
    blocks = keep_v.shape[0]
    side = width // blocks
    left = (
        lax.broadcasted_iota(jnp.int32, (width, blocks), 0) // side
        == lax.broadcasted_iota(jnp.int32, (width, blocks), 1)
    ).astype(BF16)
    right = (
        lax.broadcasted_iota(jnp.int32, (blocks, width), 1) // side
        == lax.broadcasted_iota(jnp.int32, (blocks, width), 0)
    ).astype(BF16)
    wide = jnp.dot(keep_v[...].astype(F32).astype(BF16), right, preferred_element_type=F32).astype(BF16)
    mask = jnp.dot(left, wide, preferred_element_type=F32)
    mask_ref[...] = mask.astype(BF16)
    copies[1].wait()
    kept_ref[...] = (wt_v[...].astype(F32) * mask).astype(BF16)
    none = jnp.zeros((64, 64), BF16)
    for k, (ref, out) in enumerate(((w2_v, d2_ref), (w1_v, d1_ref))):
        copies[k + 2].wait()
        for tap in range(27):
            w = ref[tap]
            at = 128 * (tap % 3)
            out[tap // 3, 0:64, at : at + 128] = jnp.concatenate([w, none], axis=1)
            out[tap // 3, 64:128, at : at + 128] = jnp.concatenate([none, w], axis=1)


def transition_kernel(
    factor, at_ref, a0, a1, a2, a3, kept_ref, mask_ref, back_ref, one_ref, chip_ref, cross_ref, mine_ref, send_ref, og_ref, two_ref
):
    me = at_ref[0]
    parts = (a0, a1, a2, a3)
    n = len(parts)
    for s, part in enumerate(parts):
        src = lax.rem(me + n - s, n)
        og_ref[src] = part[0:256]
        spot = pl.ds(src * 4, 4)
        two_ref[spot] = part[256:512].reshape(4, 64, 128)
        one_ref[spot] = part[512:768].reshape(4, 64, 128)
    og = jnp.concatenate([og_ref[j] for j in range(n)], axis=1)
    back = lax.dot_general(og, kept_ref[...], (((1,), (1,)), ((), ())), preferred_element_type=F32)
    two = two_ref[...].astype(F32).reshape(8, 2, 4, 2, 8, 128)
    cells = []
    for p in range(2):
        halves = []
        for q in range(2):
            pre = two[:, p, :, q]
            at = (p * 2 + q) * 128
            grad = back[:, at : at + 128].reshape(8, 4, 8, 128)
            halves.append(jnp.where(pre > 0, grad, 0.0))
            cells.append(jnp.maximum(pre, 0.0).reshape(256, 128).astype(BF16))
        back_ref[:, p] = jnp.stack(halves, axis=2).reshape(8, 64, 128).astype(BF16)

    def rim(high, ref):
        at = 32 if high else 0
        ref[:, :, 0:32] = back_ref[:, :, at : at + 32]
        at = 48 if high else 0
        ref[:, :, 32:48] = one_ref[:, at : at + 16].reshape(8, 2, 16, 128)

    share(at_ref[1], rim, cross_ref, chip_ref)
    flat = jnp.concatenate(cells, axis=1)
    trans = lax.dot_general(flat, og, (((0,), (0,)), ((), ())), preferred_element_type=F32)
    trans = trans * mask_ref[...].astype(F32) * factor

    def emit(half, ref):
        for m in range(4):
            ref[256 * m : 256 * m + 256] = trans[256 * half : 256 * half + 256, 128 * m : 128 * m + 128].astype(ref.dtype)

    share(at_ref[1], emit, mine_ref, send_ref)


def share(core, emit, mine_ref, send_ref):
    @pl.when(core == 0)
    def _():
        emit(0, mine_ref)
        emit(1, send_ref)

    @pl.when(core != 0)
    def _():
        emit(1, mine_ref)
        emit(0, send_ref)


def triple(v):
    x, rows, _ = v.shape
    flat = v.reshape(x * rows, 128)
    t = lax.broadcasted_iota(jnp.int32, flat.shape, 0) % 8
    later = jnp.where(t == 7, 0.0, pltpu.roll(flat, x * rows - 1, 0))
    earlier = jnp.where(t == 0, 0.0, pltpu.roll(flat, 1, 0))
    wide = jnp.concatenate([later, flat, earlier], axis=1)
    return wide.astype(BF16).reshape(x, rows, 384)


def fold(sums, factor):
    lane = lax.broadcasted_iota(jnp.int32, (64, 128), 1)
    taps = []
    for g in sums:
        for l in range(3):
            if g is None:
                taps.append(jnp.zeros((64, 128), F32))
                continue
            part = g[:, l * 128 : (l + 1) * 128]
            f = jnp.where(lane < 64, part[0:64], part[64:128])
            taps.append((f + pltpu.roll(f, 64, 1)) * factor)
    taps.append(taps[-1])
    return [jnp.where(lane < 64, taps[2 * m], taps[2 * m + 1]) for m in range(14)]


def apply_taps(rows, taps):
    return lax.dot_general(rows, taps, (((1,), (1,)), ((), ())), preferred_element_type=F32)


def weight_sums(act, wide_ref, act_ref):
    act_ref[0:128] = jnp.zeros((128, 128), F32)
    act_ref[128:1152] = act.reshape(1024, 128)
    act_ref[1152:1280] = jnp.zeros((128, 128), F32)
    turned = act_ref[...].T.astype(BF16)
    stacked = jnp.concatenate([turned[:, 128 * i : 128 * i + 1024] for i in range(3)], axis=0)
    sums = [None] * 9
    for j in range(3):
        rows = wide_ref[2:18, 32 - 16 * j : 96 - 16 * j].reshape(1024, 384)
        part = jnp.dot(stacked, rows, preferred_element_type=F32)
        for i in range(3):
            sums[i * 3 + j] = part[128 * i : 128 * i + 128]
    return sums


def own_kernel(factor, back_ref, one_ref, w_ref, acc_ref, sums_ref, wide_ref, act_ref):
    wide_ref[2:18, 0:16] = jnp.zeros((16, 16, 384), BF16)
    wide_ref[2:18, 80:96] = jnp.zeros((16, 16, 384), BF16)
    wide_ref[2:18, 16:80] = triple(back_ref[...].astype(F32))
    acc_ref[...] = jnp.zeros((16, 96, 128), F32)
    rows = wide_ref[2:18, 16:80].reshape(1024, 384)
    for j in range(3):
        taps = jnp.concatenate([w_ref[i * 3 + j] for i in range(3)], axis=0)
        part = apply_taps(rows, taps).reshape(16, 64, 384)
        ys = slice(16 * j, 16 * j + 64)
        acc_ref[0:14, ys] += part[2:16, :, 0:128]
        acc_ref[:, ys] += part[:, :, 128:256]
        acc_ref[2:16, ys] += part[0:14, :, 256:384]
    sums = weight_sums(jnp.maximum(one_ref[...].astype(F32), 0.0), wide_ref, act_ref)
    for m, block in enumerate(fold(sums, factor)):
        sums_ref[64 * m : 64 * m + 64] = block


def conv_kernel(
    factor, at_ref, acc_ref, sums_ref, one_ref, chip_ref, cross_ref, w_ref, i0, i1, i2, i3,
    mine_ref, send_ref, outer_ref, rim_ref, wide_ref, in_ref, first_ref, act_ref,
):
    me = at_ref[0]
    parts = (i0, i1, i2, i3)
    n = len(parts)
    for s, part in enumerate(parts):
        in_ref[pl.ds(lax.rem(me + n - s, n) * 4, 4)] = part[...].reshape(4, 64, 128)

    def put(side, ref):
        rim_ref[side] = ref[...]

    share(at_ref[1], put, cross_ref, chip_ref)
    wide_ref[:, 0:2] = jnp.zeros((2, 2, 32, 384), BF16)
    wide_ref[:, 18:20] = jnp.zeros((2, 2, 32, 384), BF16)
    outer_ref[0:2] = jnp.zeros((2, 96, 384), BF16)
    outer_ref[18:20] = jnp.zeros((2, 96, 384), BF16)
    for side in range(2):
        wide_ref[side, 2:18] = triple(rim_ref[side, :, 0:32].astype(F32))
    first_ref[...] = acc_ref[...]
    act = jnp.maximum(one_ref[...].astype(F32), 0.0)
    sums = [None] * 9
    for side in range(2):
        j = 2 - 2 * side
        near = 16 - 16 * side
        own = 48 * side
        turned = act[:, own : own + 16].reshape(256, 128).T.astype(BF16)
        far = jnp.zeros((512, 128), F32)
        close = jnp.zeros((256, 128), F32)
        for i in range(3):
            xs = slice(4 - 2 * i, 20 - 2 * i)
            rows = wide_ref[side, xs, near : near + 16].reshape(256, 384)
            far += apply_taps(wide_ref[side, xs].reshape(512, 384), w_ref[i * 3 + j])
            close += apply_taps(rows, w_ref[i * 3 + 1])
            sums[i * 3 + j] = jnp.dot(turned, rows, preferred_element_type=F32)
        first_ref[:, 64 * side : 64 * side + 32] += far.reshape(16, 32, 128)
        first_ref[:, 80 * side : 80 * side + 16] += close.reshape(16, 16, 128)
    second = fold(sums, factor)
    pre = jnp.concatenate([rim_ref[0, :, 32:48], one_ref[...], rim_ref[1, :, 32:48]], axis=1).astype(F32)
    outer_ref[2:18] = triple(jnp.where(pre > 0, first_ref[...], 0.0))
    first = fold(weight_sums(in_ref[...].astype(F32), outer_ref, act_ref), factor)

    def emit(half, ref):
        for m in range(7):
            ref[64 * m : 64 * m + 64] = first[7 * half + m].astype(ref.dtype)
            at = 448 * half + 64 * m
            block = second[7 * half + m] + sums_ref[at : at + 64]
            ref[448 + 64 * m : 512 + 64 * m] = block.astype(ref.dtype)

    share(at_ref[1], emit, mine_ref, send_ref)


def grad_kernel(at_ref, outer_ref, w_ref, grad_ref, turn_ref):
    grad = jnp.zeros((256, 128), F32)
    for i in range(3):
        for j in range(3):
            mine = outer_ref[pl.ds(at_ref[0] * 4 + 4 - 2 * i, 4), 32 - 16 * j : 96 - 16 * j].reshape(256, 384)
            grad += apply_taps(mine, w_ref[i * 3 + j])
    turn_ref[...] = grad
    for x in range(4):
        for t in range(8):
            grad_ref[x, :, 128 * t : 128 * t + 128] = turn_ref[pl.ds(64 * x + t, 8, stride=8), :].astype(BF16)


def unpack(ref, at, out_ref):
    for m in range(7):
        block = ref[at + 64 * m : at + 64 * m + 64].astype(F32)
        out_ref[2 * m] = block[:, 0:64]
        out_ref[2 * m + 1] = block[:, 64:128]


def half_kernel(mine_ref, one_ref, two_ref):
    unpack(mine_ref, 0, one_ref)
    unpack(mine_ref, 448, two_ref)


def spread_kernel(at_ref, mine_one, mine_two, other_ref, one_hbm, two_hbm, one_ref, two_ref, sems):
    def emit(core):
        copies = []

        def send(half, one, two):
            count = 14 - half
            for src, dst in ((one, one_hbm), (two, two_hbm)):
                copies.append(
                    pltpu.make_async_copy(
                        src.at[0:count], dst.at[14 * half : 14 * half + count], sems.at[len(copies)]
                    )
                )
                copies[-1].start()

        send(core, mine_one, mine_two)
        unpack(other_ref, 0, one_ref)
        unpack(other_ref, 448, two_ref)
        send(1 - core, one_ref, two_ref)
        for copy in copies:
            copy.wait()

    @pl.when(at_ref[1] == 0)
    def _():
        emit(0)

    @pl.when(at_ref[1] != 0)
    def _():
        emit(1)


def trans_kernel(at_ref, mine_ref, other_ref, trans_ref):
    def emit(half, ref):
        for m in range(4):
            trans_ref[256 * half : 256 * half + 256, 128 * m : 128 * m + 128] = ref[256 * m : 256 * m + 256].astype(F32)

    share(at_ref[1], emit, mine_ref, other_ref)


def rotate(value, axis, step):
    n = lax.axis_size(axis)
    return lax.ppermute(value, axis, [(i, (i + step) % n) for i in range(n)])


def swap(value, axis, bit):
    n = lax.axis_size(axis)
    return lax.ppermute(value, axis, [(i, i ^ bit) for i in range(n)])


def on_chip(mine, send):
    return (mine + swap(send, "gy", 1).astype(F32)).astype(BF16)


def across(mine):
    return mine.astype(F32) + swap(mine, "gy", 2).astype(F32)


def slab_body(input_activation, pre_one, pre_two, w_one, w_two, w_trans, keep_mask, out_grad):
    factor = 1.0 / math.sqrt(
        input_activation.shape[0] * 4 * input_activation.shape[1] * 4 * (input_activation.shape[2] // 64)
    )
    at = jnp.stack([lax.axis_index("gx"), lax.rem(lax.axis_index("gy"), 2)]).astype(jnp.int32)
    shape = jax.ShapeDtypeStruct
    vmem = pltpu.VMEM
    natural = vmem((4, 8, 1024), BF16)
    first, second = call(
        pack_kernel,
        (shape((768, 128), BF16), shape((256, 128), BF16)),
        [
            vmem((8, 4, 8, 128), BF16), natural, natural, natural, vmem((3, 256, 128), F32),
            pltpu.SemaphoreType.DMA((4,)),
        ],
        0,
        56,
        (out_grad,),
        (pre_two,),
        (pre_one,),
        (input_activation,),
    )
    firsts = [first] + [rotate(first, "gx", s) for s in (1, 2, 3)]
    seconds = [second] + [rotate(second, "gx", s) for s in (1, 2, 3)]
    kept, mask, d2, d1 = call(
        weight_kernel,
        (
            shape((512, 512), BF16), shape((512, 512), BF16),
            shape((9, 128, 384), BF16), shape((9, 128, 384), BF16),
        ),
        [
            vmem((512, 512), BF16), vmem((8, 8), jnp.int32),
            vmem((27, 64, 64), BF16), vmem((27, 64, 64), BF16),
            pltpu.SemaphoreType.DMA((4,)),
        ],
        10**7,
        8,
        (w_trans,),
        (keep_mask,),
        (w_two,),
        (w_one,),
    )
    back, one, chip, cross, tmine, tsend = call(
        functools.partial(transition_kernel, factor),
        (
            shape((8, 2, 64, 128), BF16),
            shape((16, 64, 128), BF16),
            shape((8, 2, 48, 128), BF16),
            shape((8, 2, 48, 128), BF16),
            shape((1024, 128), F32),
            shape((1024, 128), BF16),
        ),
        [vmem((4, 256, 128), BF16), vmem((16, 64, 128), BF16)],
        4 * 256 * 512 * 512,
        12,
        at,
        *firsts,
        kept,
        mask,
    )
    n = lax.axis_size("gy")
    pairs = [(i, i + 1) for i in range(1, n - 1, 2)]
    cross = lax.ppermute(cross, "gy", pairs + [(j, i) for i, j in pairs])
    chip = swap(chip, "gy", 1)
    tsend, *seconds = lax.optimization_barrier((tsend, *seconds))
    tmine = on_chip(tmine, tsend)
    one, tmine = lax.optimization_barrier((one, tmine))
    acc, sums = call(
        functools.partial(own_kernel, factor),
        (shape((16, 96, 128), F32), shape((896, 128), F32)),
        [vmem((20, 96, 384), BF16), vmem((1280, 128), F32)],
        2 * 128 * 3456 * 2048,
        16,
        back.reshape(16, 64, 128),
        one,
        d2,
    )
    tmine = across(tmine)
    mine, send, outer = call(
        functools.partial(conv_kernel, factor),
        (shape((896, 128), F32), shape((896, 128), BF16), shape((20, 96, 384), BF16)),
        [
            vmem((2, 16, 48, 128), BF16),
            vmem((2, 20, 32, 384), BF16),
            vmem((16, 64, 128), BF16),
            vmem((16, 96, 128), F32),
            vmem((1280, 128), F32),
        ],
        2 * 128 * 3456 * 900,
        20,
        at,
        acc,
        sums,
        one,
        chip.reshape(16, 48, 128),
        cross.reshape(16, 48, 128),
        d2,
        *seconds,
    )
    send, tmine = lax.optimization_barrier((send, tmine))
    mine = on_chip(mine, send)
    away = swap(mine, "gy", 2)
    tother = swap(tmine, "gy", 1)
    grad_w_trans = call(trans_kernel, shape((512, 512), F32), [], 10**7, 6, at, tmine, tother)
    grad_in = call(
        grad_kernel, shape((4, 8, 1024), BF16), [vmem((256, 128), F32)], 2 * 128 * 3456 * 256, 12, at, outer, d1
    )
    away, grad_w_trans, grad_in = lax.optimization_barrier((away, grad_w_trans, grad_in))
    mine = (mine.astype(F32) + away.astype(F32)).astype(BF16)
    other = swap(mine, "gy", 1)
    taps = shape((27, 64, 64), F32)
    half = shape((14, 64, 64), F32)
    mine_one, mine_two = call(half_kernel, (half, half), [], 10**8, 6, mine)
    grad_w_one, grad_w_two = call(
        spread_kernel,
        (taps, taps),
        [vmem(half.shape, F32), vmem(half.shape, F32), pltpu.SemaphoreType.DMA((4,))],
        0,
        8,
        at,
        mine_one,
        mine_two,
        other,
        out_space=pltpu.MemorySpace.HBM,
    )
    return (grad_in, grad_w_one, grad_w_two, grad_w_trans)


def solution(mesh):
    fits = mesh.shape["gx"] == 4 and mesh.shape["gy"] == 4

    def pick(*args):
        shapes = tuple(a.shape for a in args)
        known = (
            ((4, 8, 1024),) * 3 + ((27, 64, 64),) * 2 + ((512, 512), (8, 8), (8, 4, 8, 128))
        )
        return (slab_body if fits and shapes == known else body)(*args)

    return jax.shard_map(
        pick,
        mesh=mesh,
        in_specs=(
            P(("grp", "gx"), "gy", None),
            P(("grp", "gx"), "gy", None),
            P(("grp", "gx"), "gy", None),
            P(),
            P(),
            P(),
            P(),
            P("grp", "gy", None, "gx"),
        ),
        out_specs=(
            P(("grp", "gx"), "gy", None),
            P("grp", None, None),
            P("grp", None, None),
            P("grp", None),
        ),
        check_vma=False,
    )
```
